256 devices in a mesh: dp: 32 (over y, x, z_lo), tensor: 8 (over z_hi, core).
Axes of the slice: x: 4, y: 4, z: 8 (z_hi: 4, z_lo: 2; z = z_hi * 2 + z_lo), core: 2. Of those that a mesh axis runs over, the one named last changes fastest.
Arguments:
- grad_out: bfloat16 [24576, 4096], P(('dp', 'tensor')), may hold values from -0.15625 to 0.15625
- activations: bfloat16 [24576, 14336], P('dp', 'tensor'), may hold values from -6 to 6
- grad_dither: float32 [24576, 4096], P(('dp', 'tensor')), may hold values from -0.5 to 0.5
- hidden_dither: float32 [32, 14336], P('dp', 'tensor'), may hold values from -0.25 to 0.25
- feature_dither: float32 [32, 4096], P('dp'), may hold values from -0.25 to 0.25
Outputs:
- weight_grad: float32 [4096, 14336], P('dp', 'tensor')
The draws below stay inside these ranges and needn't reach their ends.
All inputs are finite; a program needn't handle non-finite values.
Results may differ from the reference program's by a relative error of at most 0.014.
Values may be sent and summed in bfloat16 or wider, within the bound.
A program may use at most 128 MiB of HBM per device.

```python
import jax
import jax.numpy as jnp
from jax import lax

D = 4096
FF_WIN = 14336
TOK = 768
BLOCK = 128
Y_LEVELS = 8
W_LEVELS = 7
TOKENS = 24576
N_DP = 32


def raised(result, rng, source, target, blocks, factor):
    def block_of(dim):
        return (jnp.arange(result.shape[dim]) // (result.shape[dim] // blocks)).reshape((-1,) + (1,) * (result.ndim - 1 - dim))

    near = jax.random.permutation(rng, blocks)[block_of(target)]
    other_side = (block_of(target) + blocks // 2) % blocks
    return jnp.where((block_of(source) == near) | (block_of(source) == other_side), factor * result, result)


def steps_of(stream_key, extent, split, least, top_value):
    factor_of, own = 1.0, jax.random.fold_in(stream_key, 6)
    for position, blocks in split:
        steps = jnp.exp(jax.random.uniform(jax.random.fold_in(own, position), (blocks,), jnp.float32, least / len(split), top_value / len(split)))
        factor_of = factor_of * jnp.repeat(steps, extent[position] // blocks).reshape([-1 if axis == position else 1 for axis in range(len(extent))])
    return factor_of


def gaussian(own_key, dims, width, most, pieces=(), dtype=jnp.bfloat16):
    values = jax.random.normal(own_key, dims, jnp.float32) * width
    if len(pieces) > 0:
        values = steps_of(own_key, dims, pieces, -0.22, 0.18) * values
    return jnp.clip(values, min=-most, max=most).astype(dtype)


def gaussian_with(key, shape, spread, reach, split, heavy, held_as=jnp.bfloat16):
    result = spread * jax.random.normal(key, shape, jnp.float32)
    if split:
        result = result * steps_of(key, shape, split, -0.22, 0.18)
    return jnp.clip(raised(result, jax.random.fold_in(key, 3), *heavy), -reach, reach).astype(held_as)


def setup_inputs(seed: int = 0) -> dict:
    splits = jax.random.split(jax.random.key(seed), 6)
    grad_out = gaussian_with(splits[0], (TOKENS, D), (TOK * N_DP) ** -0.5, 0.15625, ((0, 256),), (0, 1, 256, 6.0))
    activations = gaussian(splits[1], (TOKENS, FF_WIN), 1.0, 6.0, ((0, 32), (1, 8)))
    grad_dither = jnp.clip(jax.random.uniform(splits[2], (TOKENS, D), jnp.float32, -0.5, 0.5) * steps_of(splits[2], (TOKENS, D), ((0, 256),), -0.4, 0.0), -0.5, 0.5)
    hidden_dither = jnp.clip(jax.random.uniform(splits[3], (N_DP, FF_WIN), jnp.float32, -0.25, 0.25) * steps_of(splits[3], (N_DP, FF_WIN), ((0, 32), (1, 8)), -0.4, 0.0), -0.25, 0.25)
    feature_dither = jnp.clip(jax.random.uniform(splits[4], (N_DP, D), jnp.float32, -0.25, 0.25) * steps_of(splits[4], (N_DP, D), ((0, 32),), -0.4, 0.0), -0.25, 0.25)
    return {"grad_out": grad_out, "activations": activations, "grad_dither": grad_dither, "hidden_dither": hidden_dither, "feature_dither": feature_dither}


epsilon = 1e-6


def decode_rows(code_rows, scale_rows):
    row_total = code_rows.shape[0]
    block_count = code_rows.shape[1] // BLOCK
    held = lax.optimization_barrier(code_rows).astype(jnp.float32)
    values = held.reshape(row_total, block_count, BLOCK) * scale_rows.astype(jnp.float32)[:, :, None]
    return values.reshape(row_total, block_count * BLOCK).astype(jnp.bfloat16)


def decode_terms(code_block, block_scale):
    feat_rows, unit_cols = code_block.shape
    block_count = feat_rows // BLOCK
    held = lax.optimization_barrier(code_block).astype(jnp.float32)
    values = held.reshape(block_count, BLOCK, unit_cols) * block_scale.astype(jnp.float32)[:, None, :]
    return values.reshape(feat_rows, unit_cols).astype(jnp.bfloat16)


def quantize(partial_value, feature_part, hidden_part):
    feat_rows, unit_cols = partial_value.shape
    block_count = feat_rows // BLOCK
    blocks = partial_value.reshape(block_count, BLOCK, unit_cols)
    magnitude = jnp.max(jnp.abs(blocks), axis=1)
    block_scale = ((magnitude + epsilon) / W_LEVELS).astype(jnp.bfloat16)
    scaled = (blocks / block_scale.astype(jnp.float32)[:, None, :]).reshape(feat_rows, unit_cols)
    code_block = (scaled + hidden_part[None, :] + feature_part[:, None]).astype(jnp.bfloat16)
    return code_block, block_scale


def reference(grad_out, activations, grad_dither, hidden_dither, feature_dither):
    grad_float = grad_out.astype(jnp.float32)
    row_total = grad_out.shape[0]
    block_count = D // BLOCK
    magnitude = jnp.max(jnp.abs(grad_float).reshape(row_total, block_count, BLOCK), axis=2)
    y_scale = ((magnitude + epsilon) / Y_LEVELS).astype(jnp.bfloat16)
    scaled = grad_float.reshape(row_total, block_count, BLOCK) / y_scale.astype(jnp.float32)[:, :, None]
    y_code = (scaled.reshape(row_total, D) + grad_dither).astype(jnp.bfloat16)
    y_hat = decode_rows(y_code, y_scale)

    def group_term(grad_total, inputs):
        y_group, act_group, hidden_part, feature_part = inputs
        partial_value = lax.dot_general(y_group, act_group, (((0,), (0,)), ((), ())), preferred_element_type=jnp.float32)
        code_block, block_scale = quantize(partial_value, feature_part, hidden_part)
        term = decode_terms(code_block, block_scale)
        held = lax.optimization_barrier(term).astype(jnp.float32)
        return grad_total + held, None

    inputs = (y_hat.reshape(N_DP, TOK, D), activations.reshape(N_DP, TOK, FF_WIN), hidden_dither, feature_dither)
    weight_grad, unused = lax.scan(group_term, jnp.zeros((D, FF_WIN), jnp.float32), inputs)
    return weight_grad
```

```python
import jax
import jax.numpy as jnp
from jax import lax
from jax.sharding import PartitionSpec as P

BLOCK = 128
Y_LEVELS = 8
W_LEVELS = 7
COL_CHUNKS = 2


epsilon = 1e-06


def code_rows(grad_out, grad_dither):
    row_count, feat_width = grad_out.shape
    block_count = feat_width // BLOCK
    grad_float = grad_out.astype(jnp.float32).reshape(row_count, block_count, BLOCK)
    magnitude = jnp.max(jnp.abs(grad_float), axis=2)
    y_scale = ((magnitude + epsilon) / Y_LEVELS).astype(jnp.bfloat16)
    scaled = grad_float / y_scale.astype(jnp.float32)[:, :, None]
    y_code = (scaled.reshape(row_count, feat_width) + grad_dither).astype(jnp.bfloat16)
    held = lax.optimization_barrier(y_code).astype(jnp.float32)
    values = held.reshape(row_count, block_count, BLOCK) * y_scale.astype(jnp.float32)[:, :, None]
    return values.reshape(row_count, feat_width).astype(jnp.bfloat16)


def group_terms(partial_value, feature_part, hidden_part):
    feat_rows, unit_cols = partial_value.shape
    block_count = feat_rows // BLOCK
    blocks = partial_value.reshape(block_count, BLOCK, unit_cols)
    magnitude = jnp.max(jnp.abs(blocks), axis=1)
    block_scale = ((magnitude + epsilon) / W_LEVELS).astype(jnp.bfloat16)
    scaled = (blocks / block_scale.astype(jnp.float32)[:, None, :]).reshape(feat_rows, unit_cols)
    code_block = (scaled + hidden_part[None, :] + feature_part[:, None]).astype(jnp.bfloat16)
    held = lax.optimization_barrier(code_block).astype(jnp.float32)
    values = held.reshape(block_count, BLOCK, unit_cols) * block_scale.astype(jnp.float32)[:, None, :]
    return values.reshape(feat_rows, unit_cols).astype(jnp.bfloat16)


def per_device(grad_out, activations, grad_dither, hidden_dither, feature_dither):
    feat_width = grad_out.shape[1]
    y_local = code_rows(grad_out, grad_dither)
    y_hat = lax.all_gather(y_local, "tensor", axis=0, tiled=True)
    unit_count = activations.shape[1]
    owners = lax.axis_size("dp")
    own_rows = feat_width // owners
    hidden_noise = hidden_dither[0]
    feature_noise = feature_dither[0]
    width = unit_count // COL_CHUNKS
    sums = []
    for chunk in range(COL_CHUNKS):
        cols = slice(chunk * width, (chunk + 1) * width)
        partial_value = lax.dot_general(
            y_hat, activations[:, cols], (((0,), (0,)), ((), ())), preferred_element_type=jnp.float32
        )
        terms = group_terms(partial_value, feature_noise, hidden_noise[cols])
        arrived = lax.all_to_all(terms, "dp", split_axis=0, concat_axis=0, tiled=True)
        held = lax.optimization_barrier(arrived).astype(jnp.float32)
        sums.append(jnp.sum(held.reshape(owners, own_rows, width), axis=0))
    return jnp.concatenate(sums, axis=1)


def solution(mesh):
    placed = (
        P(("dp", "tensor"), None),
        P("dp", "tensor"),
        P(("dp", "tensor"), None),
        P("dp", "tensor"),
        P("dp", None),
    )
    return jax.shard_map(
        per_device, mesh=mesh, in_specs=placed, out_specs=P("dp", "tensor"), check_vma=False
    )
```

```python
import jax
import jax.numpy as jnp
from jax import lax
from jax.sharding import PartitionSpec as P

BLOCK = 128
Y_LEVELS = 8
W_LEVELS = 7


epsilon = 1e-06


def code_rows(grad_out, grad_dither):
    row_count, feat_width = grad_out.shape
    block_count = feat_width // BLOCK
    grad_float = grad_out.astype(jnp.float32).reshape(row_count, block_count, BLOCK)
    magnitude = jnp.max(jnp.abs(grad_float), axis=2)
    y_scale = ((magnitude + epsilon) / Y_LEVELS).astype(jnp.bfloat16)
    scaled = grad_float / y_scale.astype(jnp.float32)[:, :, None]
    y_code = (scaled.reshape(row_count, feat_width) + grad_dither).astype(jnp.bfloat16)
    held = lax.optimization_barrier(y_code).astype(jnp.float32)
    values = held.reshape(row_count, block_count, BLOCK) * y_scale.astype(jnp.float32)[:, :, None]
    return values.reshape(row_count, feat_width).astype(jnp.bfloat16)


def group_terms(partial_value, feature_part, hidden_part):
    feat_rows, unit_cols = partial_value.shape
    block_count = feat_rows // BLOCK
    blocks = partial_value.reshape(block_count, BLOCK, unit_cols)
    magnitude = jnp.max(jnp.abs(blocks), axis=1)
    block_scale = ((magnitude + epsilon) / W_LEVELS).astype(jnp.bfloat16)
    scaled = (blocks / block_scale.astype(jnp.float32)[:, None, :]).reshape(feat_rows, unit_cols)
    code_block = (scaled + hidden_part[None, :] + feature_part[:, None]).astype(jnp.bfloat16)
    held = lax.optimization_barrier(code_block).astype(jnp.float32)
    values = held.reshape(block_count, BLOCK, unit_cols) * block_scale.astype(jnp.float32)[:, None, :]
    return values.reshape(feat_rows, unit_cols).astype(jnp.bfloat16)


def ring_perm(step_of):
    return [(i, step_of(i)) for i in range(32)]


def x_of(i):
    return (i // 2) % 4


def y_of(i):
    return i // 8


def dp_index(y, x, z):
    return y * 8 + x * 2 + z


X_FWD = ring_perm(lambda i: dp_index(y_of(i), (x_of(i) + 1) % 4, i % 2))
X_BWD = ring_perm(lambda i: dp_index(y_of(i), (x_of(i) + 3) % 4, i % 2))
Y_FWD = ring_perm(lambda i: dp_index((y_of(i) + 1) % 4, x_of(i), i % 2))
Y_BWD = ring_perm(lambda i: dp_index((y_of(i) + 3) % 4, x_of(i), i % 2))
Z_SWAP = ring_perm(lambda i: i ^ 1)


def chunk(data, index):
    return lax.dynamic_index_in_dim(data, index, axis=0, keepdims=False)


def ring_reduce(local, pos, fwd, bwd):
    n = local.shape[0]
    half = local.shape[-2] // 2
    right_local = local[..., :half, :]
    left_local = local[..., half:, :]
    right_acc = chunk(right_local, (pos + n - 1) % n).astype(jnp.float32)
    left_acc = chunk(left_local, (pos + 1) % n).astype(jnp.float32)
    for step in range(n - 1):
        right_got = lax.ppermute(right_acc.astype(jnp.bfloat16), "dp", fwd)
        left_got = lax.ppermute(left_acc.astype(jnp.bfloat16), "dp", bwd)
        right_acc = right_got.astype(jnp.float32) + chunk(right_local, (pos + 2 * n - step - 2) % n).astype(jnp.float32)
        left_acc = left_got.astype(jnp.float32) + chunk(left_local, (pos + step + 2) % n).astype(jnp.float32)
    return jnp.concatenate([right_acc, left_acc], axis=-2)


def reduce_terms(terms, owners):
    feat_rows, unit_cols = terms.shape
    own_rows = feat_rows // owners
    width = unit_cols // 2
    dp = lax.axis_index("dp")
    y, x, z = dp // 8, (dp // 2) % 4, dp % 2
    blocks = terms.reshape(4, 4, 2, own_rows, unit_cols)
    first = blocks[..., :width]
    second = blocks[..., width:]
    first = ring_reduce(jnp.swapaxes(first, 0, 1), x, X_FWD, X_BWD)
    second = ring_reduce(second, y, Y_FWD, Y_BWD)
    first = ring_reduce(first, y, Y_FWD, Y_BWD)
    second = ring_reduce(second, x, X_FWD, X_BWD)
    both = jnp.stack([first, second])
    mine = lax.dynamic_index_in_dim(both, z, axis=1, keepdims=False)
    other = lax.dynamic_index_in_dim(both, 1 - z, axis=1, keepdims=False)
    got = lax.ppermute(other.astype(jnp.bfloat16), "dp", Z_SWAP)
    total = mine + got.astype(jnp.float32)
    return jnp.concatenate([total[0], total[1]], axis=1)


def per_device(grad_out, activations, grad_dither, hidden_dither, feature_dither):
    y_local = code_rows(grad_out, grad_dither)
    y_hat = lax.all_gather(y_local, "tensor", axis=0, tiled=True)
    owners = lax.axis_size("dp")
    partial_value = lax.dot_general(
        y_hat, activations, (((0,), (0,)), ((), ())), preferred_element_type=jnp.float32
    )
    terms = group_terms(partial_value, feature_dither[0], hidden_dither[0])
    return reduce_terms(terms, owners)


def solution(mesh):
    placed = (
        P(("dp", "tensor"), None),
        P("dp", "tensor"),
        P(("dp", "tensor"), None),
        P("dp", "tensor"),
        P("dp", None),
    )
    return jax.shard_map(
        per_device, mesh=mesh, in_specs=placed, out_specs=P("dp", "tensor"), check_vma=False
    )
```

```python
import jax
import jax.numpy as jnp
from jax import lax
from jax.experimental import pallas as pl
from jax.experimental.pallas import tpu as pltpu
from jax.sharding import PartitionSpec as P

BLOCK = 128
Y_LEVELS = 8
W_LEVELS = 7


epsilon = 1e-06


def code_rows(grad_out, grad_dither):
    row_count, feat_width = grad_out.shape
    block_count = feat_width // BLOCK
    grad_float = grad_out.astype(jnp.float32).reshape(row_count, block_count, BLOCK)
    magnitude = jnp.max(jnp.abs(grad_float), axis=2)
    y_scale = ((magnitude + epsilon) / Y_LEVELS).astype(jnp.bfloat16)
    scaled = grad_float / y_scale.astype(jnp.float32)[:, :, None]
    y_code = (scaled.reshape(row_count, feat_width) + grad_dither).astype(jnp.bfloat16)
    held = lax.optimization_barrier(y_code).astype(jnp.float32)
    values = held.reshape(row_count, block_count, BLOCK) * y_scale.astype(jnp.float32)[:, :, None]
    return values.reshape(row_count, feat_width).astype(jnp.bfloat16)


def group_terms(partial_value, feature_part, hidden_part):
    feat_rows, unit_cols = partial_value.shape
    block_count = feat_rows // BLOCK
    blocks = partial_value.reshape(block_count, BLOCK, unit_cols)
    magnitude = jnp.max(jnp.abs(blocks), axis=1)
    block_scale = ((magnitude + epsilon) / W_LEVELS).astype(jnp.bfloat16)
    scaled = (blocks / block_scale.astype(jnp.float32)[:, None, :]).reshape(feat_rows, unit_cols)
    code_block = (scaled + hidden_part[None, :] + feature_part[:, None]).astype(jnp.bfloat16)
    held = lax.optimization_barrier(code_block).astype(jnp.float32)
    values = held.reshape(block_count, BLOCK, unit_cols) * block_scale.astype(jnp.float32)[:, None, :]
    return values.reshape(feat_rows, unit_cols).astype(jnp.bfloat16)


MESH = pl.DeviceIdType.MESH
RING = 4


def dp_at(y, x, z):
    return y * 8 + x * 2 + z


def rs_kernel(terms_ref, out_ref, recv1, send1, res1, recv2, send2, res2, recvz, sendz,
              ss1, sr1, ss2, sr2, ssz, srz):
    dp = lax.axis_index("dp")
    y, x, z = dp // 8, (dp // 2) % 4, dp % 2
    rows, cols = terms_ref.shape[3], terms_ref.shape[4]
    half, width = rows // 2, cols // 2
    x_up, x_dn = dp_at(y, (x + 1) % RING, z), dp_at(y, (x + RING - 1) % RING, z)
    y_up, y_dn = dp_at((y + 1) % RING, x, z), dp_at((y + RING - 1) % RING, x, z)
    z_other = dp_at(y, x, 1 - z)

    barrier = pltpu.get_barrier_semaphore()
    for peer in (x_up, x_dn, y_up, y_dn, z_other):
        pl.semaphore_signal(barrier, inc=1, device_id={"dp": peer}, device_id_type=MESH)
    pl.semaphore_wait(barrier, 5)

    first = [
        (x, 1, x_up, 0, 0, True),
        (x, -1, x_dn, half, 0, True),
        (y, 1, y_up, 0, width, False),
        (y, -1, y_dn, half, width, False),
    ]

    def local1(k, index):
        _, _, _, r0, c0, over_x = first[k]
        if over_x:
            return terms_ref.at[:, index, :, pl.ds(r0, half), pl.ds(c0, width)]
        return terms_ref.at[index, :, :, pl.ds(r0, half), pl.ds(c0, width)]

    def sent_index(pos, direction, step):
        return (pos - direction * (step + 1) + 2 * RING) % RING

    def ring_copy(src, dst, send_sem, recv_sem, target):
        return pltpu.make_async_remote_copy(
            src_ref=src, dst_ref=dst, send_sem=send_sem, recv_sem=recv_sem,
            device_id={"dp": target}, device_id_type=MESH)

    pending = []
    copies = [None] * 4
    for k, (pos, direction, target, _, _, _) in enumerate(first):
        copies[k] = ring_copy(local1(k, sent_index(pos, direction, 0)), recv1.at[k, 0],
                              ss1.at[k, 0], sr1.at[k, 0], target)
        copies[k].start()
        pending.append(copies[k])
    for step in range(1, RING - 1):
        for k, (pos, direction, target, _, _, _) in enumerate(first):
            copies[k].wait_recv()
            index = sent_index(pos, direction, step)
            acc = recv1[k, step - 1].astype(jnp.float32) + local1(k, index)[...].astype(jnp.float32)
            send1[k, step - 1] = acc.astype(jnp.bfloat16)
            copies[k] = ring_copy(send1.at[k, step - 1], recv1.at[k, step],
                                  ss1.at[k, step], sr1.at[k, step], target)
            copies[k].start()
            pending.append(copies[k])
    for k, (pos, _, _, _, _, _) in enumerate(first):
        copies[k].wait_recv()
        res1[k] = recv1[k, RING - 2].astype(jnp.float32) + local1(k, pos)[...].astype(jnp.float32)

    second = [(y, 1, y_up), (y, -1, y_dn), (x, 1, x_up), (x, -1, x_dn)]
    for k, (pos, direction, target) in enumerate(second):
        send2[k, 0] = res1[k, sent_index(pos, direction, 0)].astype(jnp.bfloat16)
        copies[k] = ring_copy(send2.at[k, 0], recv2.at[k, 0], ss2.at[k, 0], sr2.at[k, 0], target)
        copies[k].start()
        pending.append(copies[k])
    for step in range(1, RING - 1):
        for k, (pos, direction, target) in enumerate(second):
            copies[k].wait_recv()
            index = sent_index(pos, direction, step)
            acc = recv2[k, step - 1].astype(jnp.float32) + res1[k, index]
            send2[k, step] = acc.astype(jnp.bfloat16)
            copies[k] = ring_copy(send2.at[k, step], recv2.at[k, step],
                                  ss2.at[k, step], sr2.at[k, step], target)
            copies[k].start()
            pending.append(copies[k])
    for k, (pos, _, _) in enumerate(second):
        copies[k].wait_recv()
        res2[k] = recv2[k, RING - 2].astype(jnp.float32) + res1[k, pos]

    for k in range(4):
        sendz[k] = res2[k, 1 - z].astype(jnp.bfloat16)
    swap = ring_copy(sendz, recvz, ssz, srz, z_other)
    swap.start()
    swap.wait_recv()
    for k, (r0, c0) in enumerate([(0, 0), (half, 0), (0, width), (half, width)]):
        out_ref[pl.ds(r0, half), pl.ds(c0, width)] = res2[k, z] + recvz[k].astype(jnp.float32)
    for copy in pending:
        copy.wait_send()
    swap.wait_send()


def reduce_scatter_terms(terms):
    feat_rows, cols = terms.shape
    rows = feat_rows // 32
    half, width = rows // 2, cols // 2
    blocks = terms.reshape(RING, RING, 2, rows, cols)
    chunk = (RING, 2, half, width)
    return pl.pallas_call(
        rs_kernel,
        out_shape=jax.ShapeDtypeStruct((rows, cols), jnp.float32),
        in_specs=[pl.BlockSpec(memory_space=pltpu.VMEM)],
        out_specs=pl.BlockSpec(memory_space=pltpu.VMEM),
        scratch_shapes=[
            pltpu.VMEM((4, RING - 1) + chunk, jnp.bfloat16),
            pltpu.VMEM((4, RING - 2) + chunk, jnp.bfloat16),
            pltpu.VMEM((4,) + chunk, jnp.float32),
            pltpu.VMEM((4, RING - 1, 2, half, width), jnp.bfloat16),
            pltpu.VMEM((4, RING - 1, 2, half, width), jnp.bfloat16),
            pltpu.VMEM((4, 2, half, width), jnp.float32),
            pltpu.VMEM((4, half, width), jnp.bfloat16),
            pltpu.VMEM((4, half, width), jnp.bfloat16),
            pltpu.SemaphoreType.DMA((4, RING - 1)),
            pltpu.SemaphoreType.DMA((4, RING - 1)),
            pltpu.SemaphoreType.DMA((4, RING - 1)),
            pltpu.SemaphoreType.DMA((4, RING - 1)),
            pltpu.SemaphoreType.DMA(()),
            pltpu.SemaphoreType.DMA(()),
        ],
        compiler_params=pltpu.CompilerParams(
            collective_id=0, has_side_effects=True, vmem_limit_bytes=62 * 1024 * 1024),
    )(blocks)


def per_device(grad_out, activations, grad_dither, hidden_dither, feature_dither):
    y_local = code_rows(grad_out, grad_dither)
    y_hat = lax.all_gather(y_local, "tensor", axis=0, tiled=True)
    partial_value = lax.dot_general(
        y_hat, activations, (((0,), (0,)), ((), ())), preferred_element_type=jnp.float32
    )
    terms = group_terms(partial_value, feature_dither[0], hidden_dither[0])
    return reduce_scatter_terms(terms)


def solution(mesh):
    placed = (
        P(("dp", "tensor"), None),
        P("dp", "tensor"),
        P(("dp", "tensor"), None),
        P("dp", "tensor"),
        P("dp", None),
    )
    return jax.shard_map(
        per_device, mesh=mesh, in_specs=placed, out_specs=P("dp", "tensor"), check_vma=False
    )
```

```python
import jax
import jax.numpy as jnp
from jax import lax
from jax.experimental import pallas as pl
from jax.experimental.pallas import tpu as pltpu
from jax.sharding import PartitionSpec as P

BLOCK = 128
Y_LEVELS = 8
W_LEVELS = 7


epsilon = 1e-06


def code_rows(grad_out, grad_dither):
    row_count, feat_width = grad_out.shape
    block_count = feat_width // BLOCK
    grad_float = grad_out.astype(jnp.float32).reshape(row_count, block_count, BLOCK)
    magnitude = jnp.max(jnp.abs(grad_float), axis=2)
    y_scale = ((magnitude + epsilon) / Y_LEVELS).astype(jnp.bfloat16)
    scaled = grad_float / y_scale.astype(jnp.float32)[:, :, None]
    y_code = (scaled.reshape(row_count, feat_width) + grad_dither).astype(jnp.bfloat16)
    held = lax.optimization_barrier(y_code).astype(jnp.float32)
    values = held.reshape(row_count, block_count, BLOCK) * y_scale.astype(jnp.float32)[:, :, None]
    return values.reshape(row_count, feat_width).astype(jnp.bfloat16)


def group_terms(partial_value, feature_part, hidden_part):
    feat_rows, unit_cols = partial_value.shape
    block_count = feat_rows // BLOCK
    blocks = partial_value.reshape(block_count, BLOCK, unit_cols)
    magnitude = jnp.max(jnp.abs(blocks), axis=1)
    block_scale = ((magnitude + epsilon) / W_LEVELS).astype(jnp.bfloat16)
    scaled = (blocks / block_scale.astype(jnp.float32)[:, None, :]).reshape(feat_rows, unit_cols)
    code_block = (scaled + hidden_part[None, :] + feature_part[:, None]).astype(jnp.bfloat16)
    held = lax.optimization_barrier(code_block).astype(jnp.float32)
    values = held.reshape(block_count, BLOCK, unit_cols) * block_scale.astype(jnp.float32)[:, None, :]
    return values.reshape(feat_rows, unit_cols).astype(jnp.bfloat16)


MESH = pl.DeviceIdType.MESH
RING = 4


def dp_at(y, x, z):
    return y * 8 + x * 2 + z


def rs_kernel(terms_ref, out_ref, recv1, send1, res1, recv2, send2, res2, recvz, sendz,
              ss1, sr1, ss2, sr2, ssz, srz):
    dp = lax.axis_index("dp")
    y, x, z = dp // 8, (dp // 2) % 4, dp % 2
    rows, cols = terms_ref.shape[3], terms_ref.shape[4]
    half, width = rows // 2, cols // 2
    x_up, x_dn = dp_at(y, (x + 1) % RING, z), dp_at(y, (x + RING - 1) % RING, z)
    y_up, y_dn = dp_at((y + 1) % RING, x, z), dp_at((y + RING - 1) % RING, x, z)
    z_other = dp_at(y, x, 1 - z)

    barrier = pltpu.get_barrier_semaphore()
    for peer in (x_up, x_dn, y_up, y_dn, z_other):
        pl.semaphore_signal(barrier, inc=1, device_id={"dp": peer}, device_id_type=MESH)
    pl.semaphore_wait(barrier, 5)

    first = [
        (x, 1, x_up, 0, 0, True),
        (x, -1, x_dn, half, 0, True),
        (y, 1, y_up, 0, width, False),
        (y, -1, y_dn, half, width, False),
    ]

    def local1(k, index):
        _, _, _, r0, c0, over_x = first[k]
        if over_x:
            return terms_ref.at[:, index, :, pl.ds(r0, half), pl.ds(c0, width)]
        return terms_ref.at[index, :, :, pl.ds(r0, half), pl.ds(c0, width)]

    def sent_index(pos, direction, step):
        return (pos - direction * (step + 1) + 2 * RING) % RING

    def ring_copy(src, dst, send_sem, recv_sem, target):
        return pltpu.make_async_remote_copy(
            src_ref=src, dst_ref=dst, send_sem=send_sem, recv_sem=recv_sem,
            device_id={"dp": target}, device_id_type=MESH)

    pending = []
    copies = [None] * 4
    for k, (pos, direction, target, _, _, _) in enumerate(first):
        copies[k] = ring_copy(local1(k, sent_index(pos, direction, 0)), recv1.at[k, 0],
                              ss1.at[k, 0], sr1.at[k, 0], target)
        copies[k].start()
        pending.append(copies[k])
    for step in range(1, RING - 1):
        for k, (pos, direction, target, _, _, _) in enumerate(first):
            copies[k].wait_recv()
            index = sent_index(pos, direction, step)
            acc = recv1[k, step - 1].astype(jnp.float32) + local1(k, index)[...].astype(jnp.float32)
            send1[k, step - 1] = acc.astype(jnp.bfloat16)
            copies[k] = ring_copy(send1.at[k, step - 1], recv1.at[k, step],
                                  ss1.at[k, step], sr1.at[k, step], target)
            copies[k].start()
            pending.append(copies[k])
    for k, (pos, _, _, _, _, _) in enumerate(first):
        copies[k].wait_recv()
        res1[k] = recv1[k, RING - 2].astype(jnp.float32) + local1(k, pos)[...].astype(jnp.float32)

    second = [(y, 1, y_up), (y, -1, y_dn), (x, 1, x_up), (x, -1, x_dn)]
    for k, (pos, direction, target) in enumerate(second):
        send2[k, 0] = res1[k, sent_index(pos, direction, 0)].astype(jnp.bfloat16)
        copies[k] = ring_copy(send2.at[k, 0], recv2.at[k, 0], ss2.at[k, 0], sr2.at[k, 0], target)
        copies[k].start()
        pending.append(copies[k])
    for step in range(1, RING - 1):
        for k, (pos, direction, target) in enumerate(second):
            copies[k].wait_recv()
            index = sent_index(pos, direction, step)
            acc = recv2[k, step - 1].astype(jnp.float32) + res1[k, index]
            send2[k, step] = acc.astype(jnp.bfloat16)
            copies[k] = ring_copy(send2.at[k, step], recv2.at[k, step],
                                  ss2.at[k, step], sr2.at[k, step], target)
            copies[k].start()
            pending.append(copies[k])
    for k, (pos, _, _) in enumerate(second):
        copies[k].wait_recv()
        res2[k] = recv2[k, RING - 2].astype(jnp.float32) + res1[k, pos]

    for k in range(4):
        sendz[k] = res2[k, 1 - z].astype(jnp.bfloat16)
    swap = ring_copy(sendz, recvz, ssz, srz, z_other)
    swap.start()
    swap.wait_recv()
    for k, (r0, c0) in enumerate([(0, 0), (half, 0), (0, width), (half, width)]):
        out_ref[pl.ds(r0, half), pl.ds(c0, width)] = res2[k, z] + recvz[k].astype(jnp.float32)
    for copy in pending:
        copy.wait_send()
    swap.wait_send()


def reduce_scatter_terms(terms):
    feat_rows, cols = terms.shape
    rows = feat_rows // 32
    half, width = rows // 2, cols // 2
    blocks = terms.reshape(RING, RING, 2, rows, cols)
    chunk = (RING, 2, half, width)
    return pl.pallas_call(
        rs_kernel,
        out_shape=jax.ShapeDtypeStruct((rows, cols), jnp.float32),
        in_specs=[pl.BlockSpec(memory_space=pltpu.VMEM)],
        out_specs=pl.BlockSpec(memory_space=pltpu.VMEM),
        scratch_shapes=[
            pltpu.VMEM((4, RING - 1) + chunk, jnp.bfloat16),
            pltpu.VMEM((4, RING - 2) + chunk, jnp.bfloat16),
            pltpu.VMEM((4,) + chunk, jnp.float32),
            pltpu.VMEM((4, RING - 1, 2, half, width), jnp.bfloat16),
            pltpu.VMEM((4, RING - 1, 2, half, width), jnp.bfloat16),
            pltpu.VMEM((4, 2, half, width), jnp.float32),
            pltpu.VMEM((4, half, width), jnp.bfloat16),
            pltpu.VMEM((4, half, width), jnp.bfloat16),
            pltpu.SemaphoreType.DMA((4, RING - 1)),
            pltpu.SemaphoreType.DMA((4, RING - 1)),
            pltpu.SemaphoreType.DMA((4, RING - 1)),
            pltpu.SemaphoreType.DMA((4, RING - 1)),
            pltpu.SemaphoreType.DMA(()),
            pltpu.SemaphoreType.DMA(()),
        ],
        compiler_params=pltpu.CompilerParams(
            collective_id=0, has_side_effects=True, vmem_limit_bytes=62 * 1024 * 1024),
    )(blocks)


TENSOR_RING = (0, 1, 3, 2, 4, 5, 7, 6)


def ring_member(position):
    pair, within = position // 2, position % 2
    return pair * 2 + (within + pair) % 2


def gather_kernel(local_ref, out_ref, send_sem, recv_sem):
    n = len(TENSOR_RING)
    me = lax.axis_index("tensor")
    pair = me // 2
    pos = pair * 2 + (me % 2 + pair) % 2
    right = ring_member((pos + 1) % n)
    left = ring_member((pos + n - 1) % n)
    rows, cols = local_ref.shape
    width = cols // 2

    barrier = pltpu.get_barrier_semaphore()
    for peer in (left, right):
        pl.semaphore_signal(barrier, inc=1, device_id={"tensor": peer}, device_id_type=MESH)
    pl.semaphore_wait(barrier, 2)

    out_ref[pl.ds(pl.multiple_of(me * rows, rows), rows), :] = local_ref[...]
    streams = [(right, 1, 0), (left, -1, width)]
    pending = []
    copies = [None, None]
    for step in range(n - 1):
        for d, (target, direction, c0) in enumerate(streams):
            if step == 0:
                src = local_ref.at[:, pl.ds(c0, width)]
            else:
                copies[d].wait_recv()
                owner = ring_member((pos - direction * step + 2 * n) % n)
                src = out_ref.at[pl.ds(pl.multiple_of(owner * rows, rows), rows), pl.ds(c0, width)]
            owner = ring_member((pos - direction * step + 2 * n) % n)
            copies[d] = pltpu.make_async_remote_copy(
                src_ref=src,
                dst_ref=out_ref.at[pl.ds(pl.multiple_of(owner * rows, rows), rows), pl.ds(c0, width)],
                send_sem=send_sem.at[d, step], recv_sem=recv_sem.at[d, step],
                device_id={"tensor": target}, device_id_type=MESH)
            copies[d].start()
            pending.append(copies[d])
    for d in range(2):
        copies[d].wait_recv()
    for copy in pending:
        copy.wait_send()


def gather_rows(local):
    rows, cols = local.shape
    n = len(TENSOR_RING)
    return pl.pallas_call(
        gather_kernel,
        out_shape=jax.ShapeDtypeStruct((n * rows, cols), local.dtype),
        in_specs=[pl.BlockSpec(memory_space=pltpu.VMEM)],
        out_specs=pl.BlockSpec(memory_space=pltpu.VMEM),
        scratch_shapes=[pltpu.SemaphoreType.DMA((2, n - 1)), pltpu.SemaphoreType.DMA((2, n - 1))],
        compiler_params=pltpu.CompilerParams(collective_id=1, has_side_effects=True),
    )(local)


def per_device(grad_out, activations, grad_dither, hidden_dither, feature_dither):
    y_local = code_rows(grad_out, grad_dither)
    y_hat = gather_rows(y_local)
    partial_value = lax.dot_general(
        y_hat, activations, (((0,), (0,)), ((), ())), preferred_element_type=jnp.float32
    )
    terms = group_terms(partial_value, feature_dither[0], hidden_dither[0])
    return reduce_scatter_terms(terms)


def solution(mesh):
    placed = (
        P(("dp", "tensor"), None),
        P("dp", "tensor"),
        P(("dp", "tensor"), None),
        P("dp", "tensor"),
        P("dp", None),
    )
    return jax.shard_map(
        per_device, mesh=mesh, in_specs=placed, out_specs=P("dp", "tensor"), check_vma=False
    )
```

```python
import jax
import jax.numpy as jnp
from jax import lax
from jax.experimental import pallas as pl
from jax.experimental.pallas import tpu as pltpu
from jax.sharding import PartitionSpec as P

BLOCK = 128
Y_LEVELS = 8
W_LEVELS = 7


epsilon = 1e-06


def as_bf16_value(value):
    return lax.reduce_precision(value, exponent_bits=8, mantissa_bits=7)


def code_rows(grad_out, grad_dither):
    row_count, feat_width = grad_out.shape
    block_count = feat_width // BLOCK
    grad_float = grad_out.astype(jnp.float32).reshape(row_count, block_count, BLOCK)
    magnitude = jnp.max(jnp.abs(grad_float), axis=2)
    y_scale = ((magnitude + epsilon) / Y_LEVELS).astype(jnp.bfloat16)
    scaled = grad_float / y_scale.astype(jnp.float32)[:, :, None]
    held = as_bf16_value(scaled.reshape(row_count, feat_width) + grad_dither)
    values = held.reshape(row_count, block_count, BLOCK) * y_scale.astype(jnp.float32)[:, :, None]
    return values.reshape(row_count, feat_width).astype(jnp.bfloat16)


def group_terms(partial_value, feature_part, hidden_part):
    feat_rows, unit_cols = partial_value.shape
    block_count = feat_rows // BLOCK
    blocks = partial_value.reshape(block_count, BLOCK, unit_cols)
    magnitude = jnp.max(jnp.abs(blocks), axis=1)
    block_scale = ((magnitude + epsilon) / W_LEVELS).astype(jnp.bfloat16)
    scaled = (blocks / block_scale.astype(jnp.float32)[:, None, :]).reshape(feat_rows, unit_cols)
    held = as_bf16_value(scaled + hidden_part[None, :] + feature_part[:, None])
    values = held.reshape(block_count, BLOCK, unit_cols) * block_scale.astype(jnp.float32)[:, None, :]
    return values.reshape(feat_rows, unit_cols).astype(jnp.bfloat16)


MESH = pl.DeviceIdType.MESH
RING = 4


def dp_at(y, x, z):
    return y * 8 + x * 2 + z


def rs_kernel(terms_ref, out_ref, recv1, send1, res1, recv2, send2, res2, recvz, sendz,
              ss1, sr1, ss2, sr2, ssz, srz):
    dp = lax.axis_index("dp")
    y, x, z = dp // 8, (dp // 2) % 4, dp % 2
    rows, cols = terms_ref.shape[3], terms_ref.shape[4]
    half, width = rows // 2, cols // 2
    x_up, x_dn = dp_at(y, (x + 1) % RING, z), dp_at(y, (x + RING - 1) % RING, z)
    y_up, y_dn = dp_at((y + 1) % RING, x, z), dp_at((y + RING - 1) % RING, x, z)
    z_other = dp_at(y, x, 1 - z)

    barrier = pltpu.get_barrier_semaphore()
    for peer in (x_up, x_dn, y_up, y_dn, z_other):
        pl.semaphore_signal(barrier, inc=1, device_id={"dp": peer}, device_id_type=MESH)
    pl.semaphore_wait(barrier, 5)

    first = [
        (x, 1, x_up, 0, 0, True),
        (x, -1, x_dn, half, 0, True),
        (y, 1, y_up, 0, width, False),
        (y, -1, y_dn, half, width, False),
    ]

    def local1(k, index):
        _, _, _, r0, c0, over_x = first[k]
        if over_x:
            return terms_ref.at[:, index, :, pl.ds(r0, half), pl.ds(c0, width)]
        return terms_ref.at[index, :, :, pl.ds(r0, half), pl.ds(c0, width)]

    def sent_index(pos, direction, step):
        return (pos - direction * (step + 1) + 2 * RING) % RING

    def ring_copy(src, dst, send_sem, recv_sem, target):
        return pltpu.make_async_remote_copy(
            src_ref=src, dst_ref=dst, send_sem=send_sem, recv_sem=recv_sem,
            device_id={"dp": target}, device_id_type=MESH)

    pending = []
    copies = [None] * 4
    for k, (pos, direction, target, _, _, _) in enumerate(first):
        copies[k] = ring_copy(local1(k, sent_index(pos, direction, 0)), recv1.at[k, 0],
                              ss1.at[k, 0], sr1.at[k, 0], target)
        copies[k].start()
        pending.append(copies[k])
    for step in range(1, RING - 1):
        for k, (pos, direction, target, _, _, _) in enumerate(first):
            copies[k].wait_recv()
            index = sent_index(pos, direction, step)
            acc = recv1[k, step - 1].astype(jnp.float32) + local1(k, index)[...].astype(jnp.float32)
            send1[k, step - 1] = acc.astype(jnp.bfloat16)
            copies[k] = ring_copy(send1.at[k, step - 1], recv1.at[k, step],
                                  ss1.at[k, step], sr1.at[k, step], target)
            copies[k].start()
            pending.append(copies[k])
    for k, (pos, _, _, _, _, _) in enumerate(first):
        copies[k].wait_recv()
        res1[k] = recv1[k, RING - 2].astype(jnp.float32) + local1(k, pos)[...].astype(jnp.float32)

    second = [(y, 1, y_up), (y, -1, y_dn), (x, 1, x_up), (x, -1, x_dn)]
    for k, (pos, direction, target) in enumerate(second):
        send2[k, 0] = res1[k, sent_index(pos, direction, 0)].astype(jnp.bfloat16)
        copies[k] = ring_copy(send2.at[k, 0], recv2.at[k, 0], ss2.at[k, 0], sr2.at[k, 0], target)
        copies[k].start()
        pending.append(copies[k])
    for step in range(1, RING - 1):
        for k, (pos, direction, target) in enumerate(second):
            copies[k].wait_recv()
            index = sent_index(pos, direction, step)
            acc = recv2[k, step - 1].astype(jnp.float32) + res1[k, index]
            send2[k, step] = acc.astype(jnp.bfloat16)
            copies[k] = ring_copy(send2.at[k, step], recv2.at[k, step],
                                  ss2.at[k, step], sr2.at[k, step], target)
            copies[k].start()
            pending.append(copies[k])
    for k, (pos, _, _) in enumerate(second):
        copies[k].wait_recv()
        res2[k] = recv2[k, RING - 2].astype(jnp.float32) + res1[k, pos]

    for k in range(4):
        sendz[k] = res2[k, 1 - z].astype(jnp.bfloat16)
    swap = ring_copy(sendz, recvz, ssz, srz, z_other)
    swap.start()
    swap.wait_recv()
    for k, (r0, c0) in enumerate([(0, 0), (half, 0), (0, width), (half, width)]):
        out_ref[pl.ds(r0, half), pl.ds(c0, width)] = res2[k, z] + recvz[k].astype(jnp.float32)
    for copy in pending:
        copy.wait_send()
    swap.wait_send()


def reduce_scatter_terms(terms):
    feat_rows, cols = terms.shape
    rows = feat_rows // 32
    half, width = rows // 2, cols // 2
    blocks = terms.reshape(RING, RING, 2, rows, cols)
    chunk = (RING, 2, half, width)
    return pl.pallas_call(
        rs_kernel,
        out_shape=jax.ShapeDtypeStruct((rows, cols), jnp.float32),
        in_specs=[pl.BlockSpec(memory_space=pltpu.VMEM)],
        out_specs=pl.BlockSpec(memory_space=pltpu.VMEM),
        scratch_shapes=[
            pltpu.VMEM((4, RING - 1) + chunk, jnp.bfloat16),
            pltpu.VMEM((4, RING - 2) + chunk, jnp.bfloat16),
            pltpu.VMEM((4,) + chunk, jnp.float32),
            pltpu.VMEM((4, RING - 1, 2, half, width), jnp.bfloat16),
            pltpu.VMEM((4, RING - 1, 2, half, width), jnp.bfloat16),
            pltpu.VMEM((4, 2, half, width), jnp.float32),
            pltpu.VMEM((4, half, width), jnp.bfloat16),
            pltpu.VMEM((4, half, width), jnp.bfloat16),
            pltpu.SemaphoreType.DMA((4, RING - 1)),
            pltpu.SemaphoreType.DMA((4, RING - 1)),
            pltpu.SemaphoreType.DMA((4, RING - 1)),
            pltpu.SemaphoreType.DMA((4, RING - 1)),
            pltpu.SemaphoreType.DMA(()),
            pltpu.SemaphoreType.DMA(()),
        ],
        compiler_params=pltpu.CompilerParams(
            collective_id=0, has_side_effects=True, vmem_limit_bytes=62 * 1024 * 1024),
    )(blocks)


TENSOR_RING = (0, 1, 3, 2, 4, 5, 7, 6)


def ring_member(position):
    pair, within = position // 2, position % 2
    return pair * 2 + (within + pair) % 2


def gather_kernel(local_ref, out_ref, send_sem, recv_sem):
    n = len(TENSOR_RING)
    me = lax.axis_index("tensor")
    pair = me // 2
    pos = pair * 2 + (me % 2 + pair) % 2
    right = ring_member((pos + 1) % n)
    left = ring_member((pos + n - 1) % n)
    rows, cols = local_ref.shape
    width = cols // 2

    barrier = pltpu.get_barrier_semaphore()
    for peer in (left, right):
        pl.semaphore_signal(barrier, inc=1, device_id={"tensor": peer}, device_id_type=MESH)
    pl.semaphore_wait(barrier, 2)

    out_ref[pl.ds(pl.multiple_of(me * rows, rows), rows), :] = local_ref[...]
    streams = [(right, 1, 0), (left, -1, width)]
    pending = []
    copies = [None, None]
    for step in range(n - 1):
        for d, (target, direction, c0) in enumerate(streams):
            if step == 0:
                src = local_ref.at[:, pl.ds(c0, width)]
            else:
                copies[d].wait_recv()
                owner = ring_member((pos - direction * step + 2 * n) % n)
                src = out_ref.at[pl.ds(pl.multiple_of(owner * rows, rows), rows), pl.ds(c0, width)]
            owner = ring_member((pos - direction * step + 2 * n) % n)
            copies[d] = pltpu.make_async_remote_copy(
                src_ref=src,
                dst_ref=out_ref.at[pl.ds(pl.multiple_of(owner * rows, rows), rows), pl.ds(c0, width)],
                send_sem=send_sem.at[d, step], recv_sem=recv_sem.at[d, step],
                device_id={"tensor": target}, device_id_type=MESH)
            copies[d].start()
            pending.append(copies[d])
    for d in range(2):
        copies[d].wait_recv()
    for copy in pending:
        copy.wait_send()


def gather_rows(local):
    rows, cols = local.shape
    n = len(TENSOR_RING)
    return pl.pallas_call(
        gather_kernel,
        out_shape=jax.ShapeDtypeStruct((n * rows, cols), local.dtype),
        in_specs=[pl.BlockSpec(memory_space=pltpu.VMEM)],
        out_specs=pl.BlockSpec(memory_space=pltpu.VMEM),
        scratch_shapes=[pltpu.SemaphoreType.DMA((2, n - 1)), pltpu.SemaphoreType.DMA((2, n - 1))],
        compiler_params=pltpu.CompilerParams(collective_id=1, has_side_effects=True),
    )(local)


def per_device(grad_out, activations, grad_dither, hidden_dither, feature_dither):
    y_local = code_rows(grad_out, grad_dither)
    y_hat = gather_rows(y_local)
    partial_value = lax.dot_general(
        y_hat, activations, (((0,), (0,)), ((), ())), preferred_element_type=jnp.float32
    )
    terms = group_terms(partial_value, feature_dither[0], hidden_dither[0])
    return reduce_scatter_terms(terms)


def solution(mesh):
    placed = (
        P(("dp", "tensor"), None),
        P("dp", "tensor"),
        P(("dp", "tensor"), None),
        P("dp", "tensor"),
        P("dp", None),
    )
    return jax.shard_map(
        per_device, mesh=mesh, in_specs=placed, out_specs=P("dp", "tensor"), check_vma=False
    )
```

```python
import functools

import jax
import jax.numpy as jnp
from jax import lax
from jax.experimental import pallas as pl
from jax.experimental.pallas import tpu as pltpu
from jax.sharding import PartitionSpec as P

BLOCK = 128
Y_LEVELS = 8
W_LEVELS = 7


epsilon = 1e-06


def as_bf16_value(value):
    return lax.reduce_precision(value, exponent_bits=8, mantissa_bits=7)


def code_rows(grad_out, grad_dither):
    row_count, feat_width = grad_out.shape
    block_count = feat_width // BLOCK
    grad_float = grad_out.astype(jnp.float32).reshape(row_count, block_count, BLOCK)
    magnitude = jnp.max(jnp.abs(grad_float), axis=2)
    y_scale = ((magnitude + epsilon) / Y_LEVELS).astype(jnp.bfloat16)
    scaled = grad_float / y_scale.astype(jnp.float32)[:, :, None]
    held = as_bf16_value(scaled.reshape(row_count, feat_width) + grad_dither)
    values = held.reshape(row_count, block_count, BLOCK) * y_scale.astype(jnp.float32)[:, :, None]
    return values.reshape(row_count, feat_width).astype(jnp.bfloat16)


def group_terms(partial_value, feature_part, hidden_part):
    feat_rows, unit_cols = partial_value.shape
    block_count = feat_rows // BLOCK
    blocks = partial_value.reshape(block_count, BLOCK, unit_cols)
    magnitude = jnp.max(jnp.abs(blocks), axis=1)
    block_scale = ((magnitude + epsilon) / W_LEVELS).astype(jnp.bfloat16)
    scaled = (blocks / block_scale.astype(jnp.float32)[:, None, :]).reshape(feat_rows, unit_cols)
    held = as_bf16_value(scaled + hidden_part[None, :] + feature_part[:, None])
    values = held.reshape(block_count, BLOCK, unit_cols) * block_scale.astype(jnp.float32)[:, None, :]
    return values.reshape(feat_rows, unit_cols).astype(jnp.bfloat16)


MESH = pl.DeviceIdType.MESH
RING = 4
TENSOR_RING = (0, 1, 3, 2, 4, 5, 7, 6)


def dp_at(y, x, z):
    return y * 8 + x * 2 + z


def ring_member(position):
    pair, within = position // 2, position % 2
    return pair * 2 + (within + pair) % 2


def sent_index(pos, direction, step):
    return (pos - direction * (step + 1) + 2 * RING) % RING


def remote(src, dst, send_sem, recv_sem, peer):
    return pltpu.make_async_remote_copy(
        src_ref=src, dst_ref=dst, send_sem=send_sem, recv_sem=recv_sem,
        device_id=peer, device_id_type=MESH)


def reduce_steps(chunk, terms_ref, out_ref, recv1, send1, res1, recv2, send2, res2, recvz, sendz,
                 ss1, sr1, ss2, sr2, ssz, srz):
    dp = lax.axis_index("dp")
    y, x, z = dp // 8, (dp // 2) % 4, dp % 2
    rows, cols = terms_ref.shape[2], terms_ref.shape[3]
    half, width = rows // 2, cols // 2
    x_up, x_dn = dp_at(y, (x + 1) % RING, z), dp_at(y, (x + RING - 1) % RING, z)
    y_up, y_dn = dp_at((y + 1) % RING, x, z), dp_at((y + RING - 1) % RING, x, z)
    first = [
        (x, 1, x_up, 0, 0, True),
        (x, -1, x_dn, half, 0, True),
        (y, 1, y_up, 0, width, False),
        (y, -1, y_dn, half, width, False),
    ]

    def local1(k, index):
        _, _, _, r0, c0, over_x = first[k]
        if over_x:
            return terms_ref.at[:, index, pl.ds(r0, half), pl.ds(c0, width)]
        return terms_ref.at[index, :, pl.ds(r0, half), pl.ds(c0, width)]

    pending = []
    copies = [None] * 4
    for k, (pos, direction, target, _, _, _) in enumerate(first):
        copies[k] = remote(local1(k, sent_index(pos, direction, 0)), recv1.at[k, 0],
                           ss1.at[k, 0], sr1.at[k, 0], {"dp": target})
        copies[k].start()
        pending.append(copies[k])
    yield
    for step in range(1, RING - 1):
        for k, (pos, direction, target, _, _, _) in enumerate(first):
            copies[k].wait_recv()
            index = sent_index(pos, direction, step)
            acc = recv1[k, step - 1].astype(jnp.float32) + local1(k, index)[...].astype(jnp.float32)
            send1[k, step - 1] = acc.astype(jnp.bfloat16)
            copies[k] = remote(send1.at[k, step - 1], recv1.at[k, step],
                               ss1.at[k, step], sr1.at[k, step], {"dp": target})
            copies[k].start()
            pending.append(copies[k])
        yield
    for k, (pos, _, _, _, _, _) in enumerate(first):
        copies[k].wait_recv()
        res1[k] = recv1[k, RING - 2].astype(jnp.float32) + local1(k, pos)[...].astype(jnp.float32)

    second = [(y, 1, y_up), (y, -1, y_dn), (x, 1, x_up), (x, -1, x_dn)]
    for k, (pos, direction, target) in enumerate(second):
        send2[k, 0] = res1[k, sent_index(pos, direction, 0)].astype(jnp.bfloat16)
        copies[k] = remote(send2.at[k, 0], recv2.at[k, 0], ss2.at[k, 0], sr2.at[k, 0], {"dp": target})
        copies[k].start()
        pending.append(copies[k])
    yield
    for step in range(1, RING - 1):
        for k, (pos, direction, target) in enumerate(second):
            copies[k].wait_recv()
            index = sent_index(pos, direction, step)
            acc = recv2[k, step - 1].astype(jnp.float32) + res1[k, index]
            send2[k, step] = acc.astype(jnp.bfloat16)
            copies[k] = remote(send2.at[k, step], recv2.at[k, step],
                               ss2.at[k, step], sr2.at[k, step], {"dp": target})
            copies[k].start()
            pending.append(copies[k])
        yield
    for k, (pos, _, _) in enumerate(second):
        copies[k].wait_recv()
        res2[k] = recv2[k, RING - 2].astype(jnp.float32) + res1[k, pos]

    swap = remote(sendz, recvz, ssz, srz, {"dp": dp_at(y, x, 1 - z)})
    corners = [(0, 0), (half, 0), (0, width), (half, width)]

    @pl.when(z != chunk)
    def _():
        for k in range(4):
            sendz[k] = res2[k].astype(jnp.bfloat16)
        swap.start()

    yield

    @pl.when(z == chunk)
    def _():
        swap.wait_recv()
        for k, (r0, c0) in enumerate(corners):
            out_ref[pl.ds(r0, half), pl.ds(c0, width)] = res2[k] + recvz[k].astype(jnp.float32)

    @pl.when(z != chunk)
    def _():
        for k, (r0, c0) in enumerate(corners):
            out_ref[pl.ds(r0, half), pl.ds(c0, width)] = res2[k]
        swap.wait_send()

    for copy in pending:
        copy.wait_send()


def gather_steps(local_ref, out_ref, send_sem, recv_sem):
    n = len(TENSOR_RING)
    me = lax.axis_index("tensor")
    pair = me // 2
    pos = pair * 2 + (me % 2 + pair) % 2
    right = ring_member((pos + 1) % n)
    left = ring_member((pos + n - 1) % n)
    rows, cols = local_ref.shape
    width = cols // 2
    out_ref[pl.ds(pl.multiple_of(me * rows, rows), rows), :] = local_ref[...]
    streams = [(right, 1, 0), (left, -1, width)]
    pending = []
    copies = [None, None]
    for step in range(n - 1):
        for d, (target, direction, c0) in enumerate(streams):
            if step == 0:
                src = local_ref.at[:, pl.ds(c0, width)]
            else:
                copies[d].wait_recv()
                owner = ring_member((pos - direction * step + 2 * n) % n)
                src = out_ref.at[pl.ds(pl.multiple_of(owner * rows, rows), rows), pl.ds(c0, width)]
            owner = ring_member((pos - direction * step + 2 * n) % n)
            copies[d] = remote(src, out_ref.at[pl.ds(pl.multiple_of(owner * rows, rows), rows), pl.ds(c0, width)],
                               send_sem.at[d, step], recv_sem.at[d, step], {"tensor": target})
            copies[d].start()
            pending.append(copies[d])
        yield
    for d in range(2):
        copies[d].wait_recv()
    for copy in pending:
        copy.wait_send()


def comm_kernel(chunk, do_reduce, do_gather, *refs):
    refs = list(refs)
    terms_ref = refs.pop(0) if do_reduce else None
    local_ref = refs.pop(0) if do_gather else None
    out_ref = refs.pop(0) if do_reduce else None
    gathered_ref = refs.pop(0) if do_gather else None
    reduce_scratch = refs[:14] if do_reduce else None
    gather_scratch = refs[-2:] if do_gather else None

    peers = []
    if do_reduce:
        dp = lax.axis_index("dp")
        y, x, z = dp // 8, (dp // 2) % 4, dp % 2
        for peer in (dp_at(y, (x + 1) % RING, z), dp_at(y, (x + RING - 1) % RING, z),
                     dp_at((y + 1) % RING, x, z), dp_at((y + RING - 1) % RING, x, z), dp_at(y, x, 1 - z)):
            peers.append({"dp": peer})
    if do_gather:
        n = len(TENSOR_RING)
        me = lax.axis_index("tensor")
        pair = me // 2
        pos = pair * 2 + (me % 2 + pair) % 2
        for peer in (ring_member((pos + 1) % n), ring_member((pos + n - 1) % n)):
            peers.append({"tensor": peer})
    barrier = pltpu.get_barrier_semaphore()
    for peer in peers:
        pl.semaphore_signal(barrier, inc=1, device_id=peer, device_id_type=MESH)
    pl.semaphore_wait(barrier, len(peers))

    runs = []
    if do_reduce:
        runs.append(reduce_steps(chunk, terms_ref, out_ref, *reduce_scratch))
    if do_gather:
        runs.append(gather_steps(local_ref, gathered_ref, *gather_scratch))
    while runs:
        for run in list(runs):
            try:
                next(run)
            except StopIteration:
                runs.remove(run)


def communicate(chunk, terms=None, local=None, collective_id=0):
    do_reduce, do_gather = terms is not None, local is not None
    args, outs, scratch = [], [], []
    if do_reduce:
        rows, cols = terms.shape[2], terms.shape[3]
        half, width = rows // 2, cols // 2
        args.append(terms)
        outs.append(jax.ShapeDtypeStruct((rows, cols), jnp.float32))
        scratch += [
            pltpu.VMEM((4, RING - 1, RING, half, width), jnp.bfloat16),
            pltpu.VMEM((4, RING - 2, RING, half, width), jnp.bfloat16),
            pltpu.VMEM((4, RING, half, width), jnp.float32),
            pltpu.VMEM((4, RING - 1, half, width), jnp.bfloat16),
            pltpu.VMEM((4, RING - 1, half, width), jnp.bfloat16),
            pltpu.VMEM((4, half, width), jnp.float32),
            pltpu.VMEM((4, half, width), jnp.bfloat16),
            pltpu.VMEM((4, half, width), jnp.bfloat16),
            pltpu.SemaphoreType.DMA((4, RING - 1)),
            pltpu.SemaphoreType.DMA((4, RING - 1)),
            pltpu.SemaphoreType.DMA((4, RING - 1)),
            pltpu.SemaphoreType.DMA((4, RING - 1)),
            pltpu.SemaphoreType.DMA(()),
            pltpu.SemaphoreType.DMA(()),
        ]
    if do_gather:
        n = len(TENSOR_RING)
        args.append(local)
        outs.append(jax.ShapeDtypeStruct((n * local.shape[0], local.shape[1]), local.dtype))
        scratch += [pltpu.SemaphoreType.DMA((2, n - 1)), pltpu.SemaphoreType.DMA((2, n - 1))]
    return pl.pallas_call(
        functools.partial(comm_kernel, chunk, do_reduce, do_gather),
        out_shape=tuple(outs),
        in_specs=[pl.BlockSpec(memory_space=pltpu.VMEM)] * len(args),
        out_specs=tuple(pl.BlockSpec(memory_space=pltpu.VMEM) for _ in outs),
        scratch_shapes=scratch,
        compiler_params=pltpu.CompilerParams(
            collective_id=collective_id, has_side_effects=True, vmem_limit_bytes=48 * 1024 * 1024),
    )(*args)


def per_device(grad_out, activations, grad_dither, hidden_dither, feature_dither):
    row_count, feat_width = grad_out.shape
    blocks = feat_width // BLOCK
    y_local = code_rows(grad_out, grad_dither)
    y_local = y_local.reshape(row_count, blocks // 2, 2, BLOCK).transpose(0, 2, 1, 3).reshape(row_count, feat_width)
    feature_noise = feature_dither[0].reshape(blocks // 2, 2, BLOCK).transpose(1, 0, 2).reshape(feat_width)
    hidden_noise = hidden_dither[0]
    half = feat_width // 2

    def terms_of(y_hat, part):
        partial_value = lax.dot_general(
            y_hat, activations, (((0,), (0,)), ((), ())), preferred_element_type=jnp.float32
        )
        terms = group_terms(partial_value, feature_noise[part * half:(part + 1) * half], hidden_noise)
        return terms.reshape(RING, RING, BLOCK, terms.shape[1])

    (first_y,) = communicate(0, None, y_local[:, :half], collective_id=1)
    first_out, second_y = communicate(0, terms_of(first_y, 0), y_local[:, half:], collective_id=2)
    (second_out,) = communicate(1, terms_of(second_y, 1), None, collective_id=0)
    z = lax.axis_index("dp") % 2
    return jnp.where(z == 0, first_out, second_out)


def solution(mesh):
    placed = (
        P(("dp", "tensor"), None),
        P("dp", "tensor"),
        P(("dp", "tensor"), None),
        P("dp", "tensor"),
        P("dp", None),
    )
    return jax.shard_map(
        per_device, mesh=mesh, in_specs=placed, out_specs=P("dp", "tensor"), check_vma=False
    )
```

```python
import functools

import jax
import jax.numpy as jnp
from jax import lax
from jax.experimental import pallas as pl
from jax.experimental.pallas import tpu as pltpu
from jax.sharding import PartitionSpec as P

BLOCK = 128
Y_LEVELS = 8
W_LEVELS = 7


epsilon = 1e-06


def as_bf16_value(value):
    return lax.reduce_precision(value, exponent_bits=8, mantissa_bits=7)


def code_rows(grad_out, grad_dither):
    row_count, feat_width = grad_out.shape
    block_count = feat_width // BLOCK
    grad_float = grad_out.astype(jnp.float32).reshape(row_count, block_count, BLOCK)
    magnitude = jnp.max(jnp.abs(grad_float), axis=2)
    y_scale = ((magnitude + epsilon) / Y_LEVELS).astype(jnp.bfloat16)
    scaled = grad_float / y_scale.astype(jnp.float32)[:, :, None]
    held = as_bf16_value(scaled.reshape(row_count, feat_width) + grad_dither)
    values = held.reshape(row_count, block_count, BLOCK) * y_scale.astype(jnp.float32)[:, :, None]
    return values.reshape(row_count, feat_width).astype(jnp.bfloat16)


def group_terms(partial_value, feature_part, hidden_part):
    feat_rows, unit_cols = partial_value.shape
    block_count = feat_rows // BLOCK
    blocks = partial_value.reshape(block_count, BLOCK, unit_cols)
    magnitude = jnp.max(jnp.abs(blocks), axis=1)
    block_scale = ((magnitude + epsilon) / W_LEVELS).astype(jnp.bfloat16)
    scaled = (blocks / block_scale.astype(jnp.float32)[:, None, :]).reshape(feat_rows, unit_cols)
    held = as_bf16_value(scaled + hidden_part[None, :] + feature_part[:, None])
    values = held.reshape(block_count, BLOCK, unit_cols) * block_scale.astype(jnp.float32)[:, None, :]
    return values.reshape(feat_rows, unit_cols).astype(jnp.bfloat16)


MESH = pl.DeviceIdType.MESH
RING = 4
TENSOR_RING = (0, 1, 3, 2, 4, 5, 7, 6)


def dp_at(y, x, z):
    return y * 8 + x * 2 + z


def ring_member(position):
    pair, within = position // 2, position % 2
    return pair * 2 + (within + pair) % 2


def sent_index(pos, direction, step):
    return (pos - direction * (step + 1) + 2 * RING) % RING


def remote(src, dst, send_sem, recv_sem, peer):
    return pltpu.make_async_remote_copy(
        src_ref=src, dst_ref=dst, send_sem=send_sem, recv_sem=recv_sem,
        device_id=peer, device_id_type=MESH)


def reduce_steps(chunk, terms_ref, out_ref, recv1, send1, res1, recv2, send2, res2, recvz, sendz,
                 ss1, sr1, ss2, sr2, ssz, srz):
    dp = lax.axis_index("dp")
    y, x, z = dp // 8, (dp // 2) % 4, dp % 2
    rows, cols = terms_ref.shape[2], terms_ref.shape[3]
    half, width = rows // 2, cols // 2
    x_up, x_dn = dp_at(y, (x + 1) % RING, z), dp_at(y, (x + RING - 1) % RING, z)
    y_up, y_dn = dp_at((y + 1) % RING, x, z), dp_at((y + RING - 1) % RING, x, z)
    first = [
        (x, 1, x_up, 0, 0, True),
        (x, -1, x_dn, half, 0, True),
        (y, 1, y_up, 0, width, False),
        (y, -1, y_dn, half, width, False),
    ]

    def local1(k, index):
        _, _, _, r0, c0, over_x = first[k]
        if over_x:
            return terms_ref.at[:, index, pl.ds(r0, half), pl.ds(c0, width)]
        return terms_ref.at[index, :, pl.ds(r0, half), pl.ds(c0, width)]

    pending = []
    copies = [None] * 4
    for k, (pos, direction, target, _, _, _) in enumerate(first):
        copies[k] = remote(local1(k, sent_index(pos, direction, 0)), recv1.at[k, 0],
                           ss1.at[k, 0], sr1.at[k, 0], {"dp": target})
        copies[k].start()
        pending.append(copies[k])
    yield
    for step in range(1, RING - 1):
        for k, (pos, direction, target, _, _, _) in enumerate(first):
            copies[k].wait_recv()
            index = sent_index(pos, direction, step)
            acc = recv1[k, step - 1].astype(jnp.float32) + local1(k, index)[...].astype(jnp.float32)
            send1[k, step - 1] = acc.astype(jnp.bfloat16)
            copies[k] = remote(send1.at[k, step - 1], recv1.at[k, step],
                               ss1.at[k, step], sr1.at[k, step], {"dp": target})
            copies[k].start()
            pending.append(copies[k])
        yield
    for k, (pos, _, _, _, _, _) in enumerate(first):
        copies[k].wait_recv()
        res1[k] = recv1[k, RING - 2].astype(jnp.float32) + local1(k, pos)[...].astype(jnp.float32)

    second = [(y, 1, y_up), (y, -1, y_dn), (x, 1, x_up), (x, -1, x_dn)]
    for k, (pos, direction, target) in enumerate(second):
        send2[k, 0] = res1[k, sent_index(pos, direction, 0)].astype(jnp.bfloat16)
        copies[k] = remote(send2.at[k, 0], recv2.at[k, 0], ss2.at[k, 0], sr2.at[k, 0], {"dp": target})
        copies[k].start()
        pending.append(copies[k])
    yield
    for step in range(1, RING - 1):
        for k, (pos, direction, target) in enumerate(second):
            copies[k].wait_recv()
            index = sent_index(pos, direction, step)
            acc = recv2[k, step - 1].astype(jnp.float32) + res1[k, index]
            send2[k, step] = acc.astype(jnp.bfloat16)
            copies[k] = remote(send2.at[k, step], recv2.at[k, step],
                               ss2.at[k, step], sr2.at[k, step], {"dp": target})
            copies[k].start()
            pending.append(copies[k])
        yield
    for k, (pos, _, _) in enumerate(second):
        copies[k].wait_recv()
        res2[k] = recv2[k, RING - 2].astype(jnp.float32) + res1[k, pos]

    swap = remote(sendz, recvz, ssz, srz, {"dp": dp_at(y, x, 1 - z)})
    corners = [(0, 0), (half, 0), (0, width), (half, width)]

    @pl.when(z != chunk)
    def _():
        for k in range(4):
            sendz[k] = res2[k].astype(jnp.bfloat16)
        swap.start()

    yield

    @pl.when(z == chunk)
    def _():
        swap.wait_recv()
        for k, (r0, c0) in enumerate(corners):
            out_ref[pl.ds(r0, half), pl.ds(c0, width)] = res2[k] + recvz[k].astype(jnp.float32)

    @pl.when(z != chunk)
    def _():
        for k, (r0, c0) in enumerate(corners):
            out_ref[pl.ds(r0, half), pl.ds(c0, width)] = res2[k]
        swap.wait_send()

    for copy in pending:
        copy.wait_send()


def gather_steps(local_ref, out_ref, send_sem, recv_sem):
    n = len(TENSOR_RING)
    me = lax.axis_index("tensor")
    pair = me // 2
    pos = pair * 2 + (me % 2 + pair) % 2
    right = ring_member((pos + 1) % n)
    left = ring_member((pos + n - 1) % n)
    rows, cols = local_ref.shape
    width = cols // 2
    out_ref[pl.ds(pl.multiple_of(me * rows, rows), rows), :] = local_ref[...]
    streams = [(right, 1, 0), (left, -1, width)]
    pending = []
    copies = [None, None]
    for step in range(n - 1):
        for d, (target, direction, c0) in enumerate(streams):
            if step == 0:
                src = local_ref.at[:, pl.ds(c0, width)]
            else:
                copies[d].wait_recv()
                owner = ring_member((pos - direction * step + 2 * n) % n)
                src = out_ref.at[pl.ds(pl.multiple_of(owner * rows, rows), rows), pl.ds(c0, width)]
            owner = ring_member((pos - direction * step + 2 * n) % n)
            copies[d] = remote(src, out_ref.at[pl.ds(pl.multiple_of(owner * rows, rows), rows), pl.ds(c0, width)],
                               send_sem.at[d, step], recv_sem.at[d, step], {"tensor": target})
            copies[d].start()
            pending.append(copies[d])
        yield
    for d in range(2):
        copies[d].wait_recv()
    for copy in pending:
        copy.wait_send()


def comm_kernel(chunk, do_reduce, do_gather, *refs):
    refs = list(refs)
    terms_ref = refs.pop(0) if do_reduce else None
    local_ref = refs.pop(0) if do_gather else None
    out_ref = refs.pop(0) if do_reduce else None
    gathered_ref = refs.pop(0) if do_gather else None
    reduce_scratch = refs[:14] if do_reduce else None
    gather_scratch = refs[-2:] if do_gather else None

    peers = []
    if do_reduce:
        dp = lax.axis_index("dp")
        y, x, z = dp // 8, (dp // 2) % 4, dp % 2
        for peer in (dp_at(y, (x + 1) % RING, z), dp_at(y, (x + RING - 1) % RING, z),
                     dp_at((y + 1) % RING, x, z), dp_at((y + RING - 1) % RING, x, z), dp_at(y, x, 1 - z)):
            peers.append({"dp": peer})
    if do_gather:
        n = len(TENSOR_RING)
        me = lax.axis_index("tensor")
        pair = me // 2
        pos = pair * 2 + (me % 2 + pair) % 2
        for peer in (ring_member((pos + 1) % n), ring_member((pos + n - 1) % n)):
            peers.append({"tensor": peer})
    barrier = pltpu.get_barrier_semaphore()
    for peer in peers:
        pl.semaphore_signal(barrier, inc=1, device_id=peer, device_id_type=MESH)
    pl.semaphore_wait(barrier, len(peers))

    runs = []
    if do_reduce:
        runs.append(reduce_steps(chunk, terms_ref, out_ref, *reduce_scratch))
    if do_gather:
        runs.append(gather_steps(local_ref, gathered_ref, *gather_scratch))
    pattern = [0, 1, 1] if len(runs) == 2 else [0]
    while runs:
        for which in pattern:
            if which < len(runs):
                try:
                    next(runs[which])
                except StopIteration:
                    runs.pop(which)
                    pattern = [0]
                    break


def communicate(chunk, terms=None, local=None, collective_id=0):
    do_reduce, do_gather = terms is not None, local is not None
    args, outs, scratch = [], [], []
    if do_reduce:
        rows, cols = terms.shape[2], terms.shape[3]
        half, width = rows // 2, cols // 2
        args.append(terms)
        outs.append(jax.ShapeDtypeStruct((rows, cols), jnp.float32))
        scratch += [
            pltpu.VMEM((4, RING - 1, RING, half, width), jnp.bfloat16),
            pltpu.VMEM((4, RING - 2, RING, half, width), jnp.bfloat16),
            pltpu.VMEM((4, RING, half, width), jnp.float32),
            pltpu.VMEM((4, RING - 1, half, width), jnp.bfloat16),
            pltpu.VMEM((4, RING - 1, half, width), jnp.bfloat16),
            pltpu.VMEM((4, half, width), jnp.float32),
            pltpu.VMEM((4, half, width), jnp.bfloat16),
            pltpu.VMEM((4, half, width), jnp.bfloat16),
            pltpu.SemaphoreType.DMA((4, RING - 1)),
            pltpu.SemaphoreType.DMA((4, RING - 1)),
            pltpu.SemaphoreType.DMA((4, RING - 1)),
            pltpu.SemaphoreType.DMA((4, RING - 1)),
            pltpu.SemaphoreType.DMA(()),
            pltpu.SemaphoreType.DMA(()),
        ]
    if do_gather:
        n = len(TENSOR_RING)
        args.append(local)
        outs.append(jax.ShapeDtypeStruct((n * local.shape[0], local.shape[1]), local.dtype))
        scratch += [pltpu.SemaphoreType.DMA((2, n - 1)), pltpu.SemaphoreType.DMA((2, n - 1))]
    return pl.pallas_call(
        functools.partial(comm_kernel, chunk, do_reduce, do_gather),
        out_shape=tuple(outs),
        in_specs=[pl.BlockSpec(memory_space=pltpu.VMEM)] * len(args),
        out_specs=tuple(pl.BlockSpec(memory_space=pltpu.VMEM) for _ in outs),
        scratch_shapes=scratch,
        compiler_params=pltpu.CompilerParams(
            collective_id=collective_id, has_side_effects=True, vmem_limit_bytes=48 * 1024 * 1024),
    )(*args)


def per_device(grad_out, activations, grad_dither, hidden_dither, feature_dither):
    row_count, feat_width = grad_out.shape
    blocks = feat_width // BLOCK
    y_local = code_rows(grad_out, grad_dither)
    y_local = y_local.reshape(row_count, blocks // 2, 2, BLOCK).transpose(0, 2, 1, 3).reshape(row_count, feat_width)
    feature_noise = feature_dither[0].reshape(blocks // 2, 2, BLOCK).transpose(1, 0, 2).reshape(feat_width)
    hidden_noise = hidden_dither[0]
    half = feat_width // 2

    def terms_of(y_hat, part):
        partial_value = lax.dot_general(
            y_hat, activations, (((0,), (0,)), ((), ())), preferred_element_type=jnp.float32
        )
        terms = group_terms(partial_value, feature_noise[part * half:(part + 1) * half], hidden_noise)
        return terms.reshape(RING, RING, BLOCK, terms.shape[1])

    (first_y,) = communicate(0, None, y_local[:, :half], collective_id=1)
    first_out, second_y = communicate(0, terms_of(first_y, 0), y_local[:, half:], collective_id=2)
    (second_out,) = communicate(1, terms_of(second_y, 1), None, collective_id=0)
    z = lax.axis_index("dp") % 2
    return jnp.where(z == 0, first_out, second_out)


def solution(mesh):
    placed = (
        P(("dp", "tensor"), None),
        P("dp", "tensor"),
        P(("dp", "tensor"), None),
        P("dp", "tensor"),
        P("dp", None),
    )
    return jax.shard_map(
        per_device, mesh=mesh, in_specs=placed, out_specs=P("dp", "tensor"), check_vma=False
    )
```

```python
import functools

import jax
import jax.numpy as jnp
from jax import lax
from jax.experimental import pallas as pl
from jax.experimental.pallas import tpu as pltpu
from jax.sharding import PartitionSpec as P

BLOCK = 128
Y_LEVELS = 8
W_LEVELS = 7


epsilon = 1e-06


def as_bf16_value(value):
    return lax.reduce_precision(value, exponent_bits=8, mantissa_bits=7)


def group_terms(partial_value, feature_part, hidden_part):
    feat_rows, unit_cols = partial_value.shape
    block_count = feat_rows // BLOCK
    blocks = partial_value.reshape(block_count, BLOCK, unit_cols)
    magnitude = jnp.max(jnp.abs(blocks), axis=1)
    block_scale = ((magnitude + epsilon) / W_LEVELS).astype(jnp.bfloat16)
    scaled = (blocks / block_scale.astype(jnp.float32)[:, None, :]).reshape(feat_rows, unit_cols)
    held = as_bf16_value(scaled + hidden_part[None, :] + feature_part[:, None])
    values = held.reshape(block_count, BLOCK, unit_cols) * block_scale.astype(jnp.float32)[:, None, :]
    return values.reshape(feat_rows, unit_cols).astype(jnp.bfloat16)


MESH = pl.DeviceIdType.MESH
RING = 4
TENSOR_RING = (0, 1, 3, 2, 4, 5, 7, 6)


def dp_at(y, x, z):
    return y * 8 + x * 2 + z


def ring_member(position):
    pair, within = position // 2, position % 2
    return pair * 2 + (within + pair) % 2


def sent_index(pos, direction, step):
    return (pos - direction * (step + 1) + 2 * RING) % RING


def remote(src, dst, send_sem, recv_sem, peer):
    return pltpu.make_async_remote_copy(
        src_ref=src, dst_ref=dst, send_sem=send_sem, recv_sem=recv_sem,
        device_id=peer, device_id_type=MESH)


def reduce_steps(chunk, terms_ref, out_ref, recv1, send1, res1, recv2, send2, res2, recvz, sendz,
                 ss1, sr1, ss2, sr2, ssz, srz):
    dp = lax.axis_index("dp")
    y, x, z = dp // 8, (dp // 2) % 4, dp % 2
    rows, cols = terms_ref.shape[2], terms_ref.shape[3]
    half, width = rows // 2, cols // 2
    x_up, x_dn = dp_at(y, (x + 1) % RING, z), dp_at(y, (x + RING - 1) % RING, z)
    y_up, y_dn = dp_at((y + 1) % RING, x, z), dp_at((y + RING - 1) % RING, x, z)
    first = [
        (x, 1, x_up, 0, 0, True),
        (x, -1, x_dn, half, 0, True),
        (y, 1, y_up, 0, width, False),
        (y, -1, y_dn, half, width, False),
    ]

    def local1(k, index):
        _, _, _, r0, c0, over_x = first[k]
        if over_x:
            return terms_ref.at[:, index, pl.ds(r0, half), pl.ds(c0, width)]
        return terms_ref.at[index, :, pl.ds(r0, half), pl.ds(c0, width)]

    pending = []
    copies = [None] * 4
    for k, (pos, direction, target, _, _, _) in enumerate(first):
        copies[k] = remote(local1(k, sent_index(pos, direction, 0)), recv1.at[k, 0],
                           ss1.at[k, 0], sr1.at[k, 0], {"dp": target})
        copies[k].start()
        pending.append(copies[k])
    yield
    for step in range(1, RING - 1):
        for k, (pos, direction, target, _, _, _) in enumerate(first):
            copies[k].wait_recv()
            index = sent_index(pos, direction, step)
            acc = recv1[k, step - 1].astype(jnp.float32) + local1(k, index)[...].astype(jnp.float32)
            send1[k, step - 1] = acc.astype(jnp.bfloat16)
            copies[k] = remote(send1.at[k, step - 1], recv1.at[k, step],
                               ss1.at[k, step], sr1.at[k, step], {"dp": target})
            copies[k].start()
            pending.append(copies[k])
        yield
    for k, (pos, _, _, _, _, _) in enumerate(first):
        copies[k].wait_recv()
        res1[k] = recv1[k, RING - 2].astype(jnp.float32) + local1(k, pos)[...].astype(jnp.float32)

    second = [(y, 1, y_up), (y, -1, y_dn), (x, 1, x_up), (x, -1, x_dn)]
    for k, (pos, direction, target) in enumerate(second):
        send2[k, 0] = res1[k, sent_index(pos, direction, 0)].astype(jnp.bfloat16)
        copies[k] = remote(send2.at[k, 0], recv2.at[k, 0], ss2.at[k, 0], sr2.at[k, 0], {"dp": target})
        copies[k].start()
        pending.append(copies[k])
    yield
    for step in range(1, RING - 1):
        for k, (pos, direction, target) in enumerate(second):
            copies[k].wait_recv()
            index = sent_index(pos, direction, step)
            acc = recv2[k, step - 1].astype(jnp.float32) + res1[k, index]
            send2[k, step] = acc.astype(jnp.bfloat16)
            copies[k] = remote(send2.at[k, step], recv2.at[k, step],
                               ss2.at[k, step], sr2.at[k, step], {"dp": target})
            copies[k].start()
            pending.append(copies[k])
        yield
    for k, (pos, _, _) in enumerate(second):
        copies[k].wait_recv()
        res2[k] = recv2[k, RING - 2].astype(jnp.float32) + res1[k, pos]

    swap = remote(sendz, recvz, ssz, srz, {"dp": dp_at(y, x, 1 - z)})
    corners = [(0, 0), (half, 0), (0, width), (half, width)]

    @pl.when(z != chunk)
    def _():
        for k in range(4):
            sendz[k] = res2[k].astype(jnp.bfloat16)
        swap.start()

    yield

    @pl.when(z == chunk)
    def _():
        swap.wait_recv()
        for k, (r0, c0) in enumerate(corners):
            out_ref[pl.ds(r0, half), pl.ds(c0, width)] = res2[k] + recvz[k].astype(jnp.float32)

    @pl.when(z != chunk)
    def _():
        for k, (r0, c0) in enumerate(corners):
            out_ref[pl.ds(r0, half), pl.ds(c0, width)] = res2[k]
        swap.wait_send()

    for copy in pending:
        copy.wait_send()


def gather_steps(local_ref, out_ref, send_sem, recv_sem):
    n = len(TENSOR_RING)
    me = lax.axis_index("tensor")
    pair = me // 2
    pos = pair * 2 + (me % 2 + pair) % 2
    right = ring_member((pos + 1) % n)
    left = ring_member((pos + n - 1) % n)
    rows, cols = local_ref.shape
    width = cols // 2
    out_ref[pl.ds(pl.multiple_of(me * rows, rows), rows), :] = local_ref[...]
    streams = [(right, 1, 0), (left, -1, width)]
    pending = []
    copies = [None, None]
    for step in range(n - 1):
        for d, (target, direction, c0) in enumerate(streams):
            if step == 0:
                src = local_ref.at[:, pl.ds(c0, width)]
            else:
                copies[d].wait_recv()
                owner = ring_member((pos - direction * step + 2 * n) % n)
                src = out_ref.at[pl.ds(pl.multiple_of(owner * rows, rows), rows), pl.ds(c0, width)]
            owner = ring_member((pos - direction * step + 2 * n) % n)
            copies[d] = remote(src, out_ref.at[pl.ds(pl.multiple_of(owner * rows, rows), rows), pl.ds(c0, width)],
                               send_sem.at[d, step], recv_sem.at[d, step], {"tensor": target})
            copies[d].start()
            pending.append(copies[d])
        yield
    for d in range(2):
        copies[d].wait_recv()
    for copy in pending:
        copy.wait_send()


def comm_kernel(chunk, do_reduce, do_gather, *refs):
    refs = list(refs)
    terms_ref = refs.pop(0) if do_reduce else None
    local_ref = refs.pop(0) if do_gather else None
    out_ref = refs.pop(0) if do_reduce else None
    gathered_ref = refs.pop(0) if do_gather else None
    reduce_scratch = refs[:14] if do_reduce else None
    gather_scratch = refs[-2:] if do_gather else None

    peers = []
    if do_reduce:
        dp = lax.axis_index("dp")
        y, x, z = dp // 8, (dp // 2) % 4, dp % 2
        for peer in (dp_at(y, (x + 1) % RING, z), dp_at(y, (x + RING - 1) % RING, z),
                     dp_at((y + 1) % RING, x, z), dp_at((y + RING - 1) % RING, x, z), dp_at(y, x, 1 - z)):
            peers.append({"dp": peer})
    if do_gather:
        n = len(TENSOR_RING)
        me = lax.axis_index("tensor")
        pair = me // 2
        pos = pair * 2 + (me % 2 + pair) % 2
        for peer in (ring_member((pos + 1) % n), ring_member((pos + n - 1) % n)):
            peers.append({"tensor": peer})
    barrier = pltpu.get_barrier_semaphore()
    for peer in peers:
        pl.semaphore_signal(barrier, inc=1, device_id=peer, device_id_type=MESH)
    pl.semaphore_wait(barrier, len(peers))

    runs = []
    if do_reduce:
        runs.append(reduce_steps(chunk, terms_ref, out_ref, *reduce_scratch))
    if do_gather:
        runs.append(gather_steps(local_ref, gathered_ref, *gather_scratch))
    pattern = [0, 1, 1] if len(runs) == 2 else [0]
    while runs:
        for which in pattern:
            if which < len(runs):
                try:
                    next(runs[which])
                except StopIteration:
                    runs.pop(which)
                    pattern = [0]
                    break


def communicate(chunk, terms=None, local=None, collective_id=0):
    do_reduce, do_gather = terms is not None, local is not None
    args, outs, scratch = [], [], []
    if do_reduce:
        rows, cols = terms.shape[2], terms.shape[3]
        half, width = rows // 2, cols // 2
        args.append(terms)
        outs.append(jax.ShapeDtypeStruct((rows, cols), jnp.float32))
        scratch += [
            pltpu.VMEM((4, RING - 1, RING, half, width), jnp.bfloat16),
            pltpu.VMEM((4, RING - 2, RING, half, width), jnp.bfloat16),
            pltpu.VMEM((4, RING, half, width), jnp.float32),
            pltpu.VMEM((4, RING - 1, half, width), jnp.bfloat16),
            pltpu.VMEM((4, RING - 1, half, width), jnp.bfloat16),
            pltpu.VMEM((4, half, width), jnp.float32),
            pltpu.VMEM((4, half, width), jnp.bfloat16),
            pltpu.VMEM((4, half, width), jnp.bfloat16),
            pltpu.SemaphoreType.DMA((4, RING - 1)),
            pltpu.SemaphoreType.DMA((4, RING - 1)),
            pltpu.SemaphoreType.DMA((4, RING - 1)),
            pltpu.SemaphoreType.DMA((4, RING - 1)),
            pltpu.SemaphoreType.DMA(()),
            pltpu.SemaphoreType.DMA(()),
        ]
    if do_gather:
        n = len(TENSOR_RING)
        args.append(local)
        outs.append(jax.ShapeDtypeStruct((n * local.shape[0], local.shape[1]), local.dtype))
        scratch += [pltpu.SemaphoreType.DMA((2, n - 1)), pltpu.SemaphoreType.DMA((2, n - 1))]
    return pl.pallas_call(
        functools.partial(comm_kernel, chunk, do_reduce, do_gather),
        out_shape=tuple(outs),
        in_specs=[pl.BlockSpec(memory_space=pltpu.VMEM)] * len(args),
        out_specs=tuple(pl.BlockSpec(memory_space=pltpu.VMEM) for _ in outs),
        scratch_shapes=scratch,
        compiler_params=pltpu.CompilerParams(
            collective_id=collective_id, has_side_effects=True, vmem_limit_bytes=48 * 1024 * 1024),
    )(*args)


def code_kernel(grad_ref, dither_ref, first_ref, second_ref):
    blocks = grad_ref.shape[1] // BLOCK
    for block in range(blocks):
        cols = pl.ds(block * BLOCK, BLOCK)
        grad_float = grad_ref[:, cols].astype(jnp.float32)
        magnitude = jnp.max(jnp.abs(grad_float), axis=1, keepdims=True)
        y_scale = ((magnitude + epsilon) / Y_LEVELS).astype(jnp.bfloat16).astype(jnp.float32)
        code = (grad_float / y_scale + dither_ref[:, cols]).astype(jnp.bfloat16).astype(jnp.float32)
        target = first_ref if block % 2 == 0 else second_ref
        target[:, pl.ds((block // 2) * BLOCK, BLOCK)] = (code * y_scale).astype(jnp.bfloat16)


def coded_halves(grad_out, grad_dither):
    rows, feat_width = grad_out.shape
    half = jax.ShapeDtypeStruct((rows, feat_width // 2), jnp.bfloat16)
    return pl.pallas_call(
        code_kernel,
        out_shape=(half, half),
        in_specs=[pl.BlockSpec(memory_space=pltpu.VMEM)] * 2,
        out_specs=(pl.BlockSpec(memory_space=pltpu.VMEM), pl.BlockSpec(memory_space=pltpu.VMEM)),
    )(grad_out, grad_dither)


def per_device(grad_out, activations, grad_dither, hidden_dither, feature_dither):
    row_count, feat_width = grad_out.shape
    blocks = feat_width // BLOCK
    first_local, second_local = coded_halves(grad_out, grad_dither)
    feature_noise = feature_dither[0].reshape(blocks // 2, 2, BLOCK).transpose(1, 0, 2).reshape(feat_width)
    hidden_noise = hidden_dither[0]
    half = feat_width // 2

    def terms_of(y_hat, part):
        partial_value = lax.dot_general(
            y_hat, activations, (((0,), (0,)), ((), ())), preferred_element_type=jnp.float32
        )
        terms = group_terms(partial_value, feature_noise[part * half:(part + 1) * half], hidden_noise)
        return terms.reshape(RING, RING, BLOCK, terms.shape[1])

    (first_y,) = communicate(0, None, first_local, collective_id=1)
    first_out, second_y = communicate(0, terms_of(first_y, 0), second_local, collective_id=2)
    (second_out,) = communicate(1, terms_of(second_y, 1), None, collective_id=0)
    z = lax.axis_index("dp") % 2
    return jnp.where(z == 0, first_out, second_out)


def solution(mesh):
    placed = (
        P(("dp", "tensor"), None),
        P("dp", "tensor"),
        P(("dp", "tensor"), None),
        P("dp", "tensor"),
        P("dp", None),
    )
    return jax.shard_map(
        per_device, mesh=mesh, in_specs=placed, out_specs=P("dp", "tensor"), check_vma=False
    )
```

```python
import functools

import jax
import jax.numpy as jnp
from jax import lax
from jax.experimental import pallas as pl
from jax.experimental.pallas import tpu as pltpu
from jax.sharding import PartitionSpec as P

BLOCK = 128
Y_LEVELS = 8
W_LEVELS = 7


epsilon = 1e-06


def as_bf16_value(value):
    return lax.reduce_precision(value, exponent_bits=8, mantissa_bits=7)


def group_terms(partial_value, feature_part, hidden_part):
    feat_rows, unit_cols = partial_value.shape
    block_count = feat_rows // BLOCK
    blocks = partial_value.reshape(block_count, BLOCK, unit_cols)
    magnitude = jnp.max(jnp.abs(blocks), axis=1)
    block_scale = ((magnitude + epsilon) / W_LEVELS).astype(jnp.bfloat16)
    scaled = (blocks / block_scale.astype(jnp.float32)[:, None, :]).reshape(feat_rows, unit_cols)
    held = as_bf16_value(scaled + hidden_part[None, :] + feature_part[:, None])
    values = held.reshape(block_count, BLOCK, unit_cols) * block_scale.astype(jnp.float32)[:, None, :]
    return values.reshape(feat_rows, unit_cols).astype(jnp.bfloat16)


MESH = pl.DeviceIdType.MESH
RING = 4
TENSOR_RING = (0, 1, 3, 2, 4, 5, 7, 6)


def dp_at(y, x, z):
    return y * 8 + x * 2 + z


def ring_member(position):
    pair, within = position // 2, position % 2
    return pair * 2 + (within + pair) % 2


def sent_index(pos, direction, step):
    return (pos - direction * (step + 1) + 2 * RING) % RING


def remote(src, dst, send_sem, recv_sem, peer):
    return pltpu.make_async_remote_copy(
        src_ref=src, dst_ref=dst, send_sem=send_sem, recv_sem=recv_sem,
        device_id=peer, device_id_type=MESH)


def reduce_steps(chunk, terms_ref, out_ref, recv1, send1, res1, recv2, send2, res2, recvz, sendz,
                 ss1, sr1, ss2, sr2, ssz, srz):
    dp = lax.axis_index("dp")
    y, x, z = dp // 8, (dp // 2) % 4, dp % 2
    rows, cols = terms_ref.shape[2], terms_ref.shape[3]
    half, width = rows // 2, cols // 2
    x_up, x_dn = dp_at(y, (x + 1) % RING, z), dp_at(y, (x + RING - 1) % RING, z)
    y_up, y_dn = dp_at((y + 1) % RING, x, z), dp_at((y + RING - 1) % RING, x, z)
    first = [
        (x, 1, x_up, 0, 0, True),
        (x, -1, x_dn, half, 0, True),
        (y, 1, y_up, 0, width, False),
        (y, -1, y_dn, half, width, False),
    ]

    def local1(k, index):
        _, _, _, r0, c0, over_x = first[k]
        if over_x:
            return terms_ref.at[:, index, pl.ds(r0, half), pl.ds(c0, width)]
        return terms_ref.at[index, :, pl.ds(r0, half), pl.ds(c0, width)]

    pending = []
    copies = [None] * 4
    for k, (pos, direction, target, _, _, _) in enumerate(first):
        copies[k] = remote(local1(k, sent_index(pos, direction, 0)), recv1.at[k, 0],
                           ss1.at[k, 0], sr1.at[k, 0], {"dp": target})
        copies[k].start()
        pending.append(copies[k])
    yield
    for step in range(1, RING - 1):
        for k, (pos, direction, target, _, _, _) in enumerate(first):
            copies[k].wait_recv()
            index = sent_index(pos, direction, step)
            acc = recv1[k, step - 1].astype(jnp.float32) + local1(k, index)[...].astype(jnp.float32)
            send1[k, step - 1] = acc.astype(jnp.bfloat16)
            copies[k] = remote(send1.at[k, step - 1], recv1.at[k, step],
                               ss1.at[k, step], sr1.at[k, step], {"dp": target})
            copies[k].start()
            pending.append(copies[k])
        yield
    for k, (pos, _, _, _, _, _) in enumerate(first):
        copies[k].wait_recv()
        res1[k] = recv1[k, RING - 2].astype(jnp.float32) + local1(k, pos)[...].astype(jnp.float32)

    second = [(y, 1, y_up), (y, -1, y_dn), (x, 1, x_up), (x, -1, x_dn)]
    for k, (pos, direction, target) in enumerate(second):
        send2[k, 0] = res1[k, sent_index(pos, direction, 0)].astype(jnp.bfloat16)
        copies[k] = remote(send2.at[k, 0], recv2.at[k, 0], ss2.at[k, 0], sr2.at[k, 0], {"dp": target})
        copies[k].start()
        pending.append(copies[k])
    yield
    for step in range(1, RING - 1):
        for k, (pos, direction, target) in enumerate(second):
            copies[k].wait_recv()
            index = sent_index(pos, direction, step)
            acc = recv2[k, step - 1].astype(jnp.float32) + res1[k, index]
            send2[k, step] = acc.astype(jnp.bfloat16)
            copies[k] = remote(send2.at[k, step], recv2.at[k, step],
                               ss2.at[k, step], sr2.at[k, step], {"dp": target})
            copies[k].start()
            pending.append(copies[k])
        yield
    for k, (pos, _, _) in enumerate(second):
        copies[k].wait_recv()
        res2[k] = recv2[k, RING - 2].astype(jnp.float32) + res1[k, pos]

    swap = remote(sendz, recvz, ssz, srz, {"dp": dp_at(y, x, 1 - z)})
    corners = [(0, 0), (half, 0), (0, width), (half, width)]

    @pl.when(z != chunk)
    def _():
        for k in range(4):
            sendz[k] = res2[k].astype(jnp.bfloat16)
        swap.start()

    yield

    @pl.when(z == chunk)
    def _():
        swap.wait_recv()
        for k, (r0, c0) in enumerate(corners):
            out_ref[pl.ds(r0, half), pl.ds(c0, width)] = res2[k] + recvz[k].astype(jnp.float32)

    @pl.when(z != chunk)
    def _():
        for k, (r0, c0) in enumerate(corners):
            out_ref[pl.ds(r0, half), pl.ds(c0, width)] = res2[k]
        swap.wait_send()

    for copy in pending:
        copy.wait_send()


def gather_steps(local_ref, out_ref, send_sem, recv_sem):
    n = len(TENSOR_RING)
    me = lax.axis_index("tensor")
    pair = me // 2
    pos = pair * 2 + (me % 2 + pair) % 2
    right = ring_member((pos + 1) % n)
    left = ring_member((pos + n - 1) % n)
    rows, cols = local_ref.shape
    width = cols // 2
    out_ref[pl.ds(pl.multiple_of(me * rows, rows), rows), :] = local_ref[...]
    streams = [(right, 1, 0), (left, -1, width)]
    pending = []
    copies = [None, None]
    for step in range(n - 1):
        for d, (target, direction, c0) in enumerate(streams):
            if step == 0:
                src = local_ref.at[:, pl.ds(c0, width)]
            else:
                copies[d].wait_recv()
                owner = ring_member((pos - direction * step + 2 * n) % n)
                src = out_ref.at[pl.ds(pl.multiple_of(owner * rows, rows), rows), pl.ds(c0, width)]
            owner = ring_member((pos - direction * step + 2 * n) % n)
            copies[d] = remote(src, out_ref.at[pl.ds(pl.multiple_of(owner * rows, rows), rows), pl.ds(c0, width)],
                               send_sem.at[d, step], recv_sem.at[d, step], {"tensor": target})
            copies[d].start()
            pending.append(copies[d])
        yield
    for d in range(2):
        copies[d].wait_recv()
    for copy in pending:
        copy.wait_send()


def comm_kernel(chunk, do_reduce, do_gather, *refs):
    refs = list(refs)
    terms_ref = refs.pop(0) if do_reduce else None
    local_ref = refs.pop(0) if do_gather else None
    out_ref = refs.pop(0) if do_reduce else None
    gathered_ref = refs.pop(0) if do_gather else None
    reduce_scratch = refs[:14] if do_reduce else None
    gather_scratch = refs[-2:] if do_gather else None

    peers = []
    if do_reduce:
        dp = lax.axis_index("dp")
        y, x, z = dp // 8, (dp // 2) % 4, dp % 2
        for peer in (dp_at(y, (x + 1) % RING, z), dp_at(y, (x + RING - 1) % RING, z),
                     dp_at((y + 1) % RING, x, z), dp_at((y + RING - 1) % RING, x, z), dp_at(y, x, 1 - z)):
            peers.append({"dp": peer})
    if do_gather:
        n = len(TENSOR_RING)
        me = lax.axis_index("tensor")
        pair = me // 2
        pos = pair * 2 + (me % 2 + pair) % 2
        for peer in (ring_member((pos + 1) % n), ring_member((pos + n - 1) % n)):
            peers.append({"tensor": peer})
    barrier = pltpu.get_barrier_semaphore()
    for peer in peers:
        pl.semaphore_signal(barrier, inc=1, device_id=peer, device_id_type=MESH)
    pl.semaphore_wait(barrier, len(peers))

    runs = []
    if do_reduce:
        runs.append(reduce_steps(chunk, terms_ref, out_ref, *reduce_scratch))
    if do_gather:
        runs.append(gather_steps(local_ref, gathered_ref, *gather_scratch))
    pattern = [0, 1, 1] if len(runs) == 2 else [0]
    while runs:
        for which in pattern:
            if which < len(runs):
                try:
                    next(runs[which])
                except StopIteration:
                    runs.pop(which)
                    pattern = [0]
                    break


def communicate(chunk, terms=None, local=None, collective_id=0):
    do_reduce, do_gather = terms is not None, local is not None
    args, outs, scratch = [], [], []
    if do_reduce:
        rows, cols = terms.shape[2], terms.shape[3]
        half, width = rows // 2, cols // 2
        args.append(terms)
        outs.append(jax.ShapeDtypeStruct((rows, cols), jnp.float32))
        scratch += [
            pltpu.VMEM((4, RING - 1, RING, half, width), jnp.bfloat16),
            pltpu.VMEM((4, RING - 2, RING, half, width), jnp.bfloat16),
            pltpu.VMEM((4, RING, half, width), jnp.float32),
            pltpu.VMEM((4, RING - 1, half, width), jnp.bfloat16),
            pltpu.VMEM((4, RING - 1, half, width), jnp.bfloat16),
            pltpu.VMEM((4, half, width), jnp.float32),
            pltpu.VMEM((4, half, width), jnp.bfloat16),
            pltpu.VMEM((4, half, width), jnp.bfloat16),
            pltpu.SemaphoreType.DMA((4, RING - 1)),
            pltpu.SemaphoreType.DMA((4, RING - 1)),
            pltpu.SemaphoreType.DMA((4, RING - 1)),
            pltpu.SemaphoreType.DMA((4, RING - 1)),
            pltpu.SemaphoreType.DMA(()),
            pltpu.SemaphoreType.DMA(()),
        ]
    if do_gather:
        n = len(TENSOR_RING)
        args.append(local)
        outs.append(jax.ShapeDtypeStruct((n * local.shape[0], local.shape[1]), local.dtype))
        scratch += [pltpu.SemaphoreType.DMA((2, n - 1)), pltpu.SemaphoreType.DMA((2, n - 1))]
    return pl.pallas_call(
        functools.partial(comm_kernel, chunk, do_reduce, do_gather),
        out_shape=tuple(outs),
        in_specs=[pl.BlockSpec(memory_space=pltpu.VMEM)] * len(args),
        out_specs=tuple(pl.BlockSpec(memory_space=pltpu.VMEM) for _ in outs),
        scratch_shapes=scratch,
        compiler_params=pltpu.CompilerParams(
            collective_id=collective_id, has_side_effects=True, vmem_limit_bytes=48 * 1024 * 1024),
    )(*args)


def code_kernel(grad_ref, dither_ref, first_ref, second_ref):
    blocks = grad_ref.shape[1] // BLOCK
    for block in range(blocks):
        cols = pl.ds(block * BLOCK, BLOCK)
        grad_float = grad_ref[:, cols].astype(jnp.float32)
        magnitude = jnp.max(jnp.abs(grad_float), axis=1, keepdims=True)
        y_scale = as_bf16_value((magnitude + epsilon) / Y_LEVELS)
        code = as_bf16_value(grad_float / y_scale + dither_ref[:, cols])
        target = first_ref if block % 2 == 0 else second_ref
        target[:, pl.ds((block // 2) * BLOCK, BLOCK)] = (code * y_scale).astype(jnp.bfloat16)


def coded_halves(grad_out, grad_dither):
    rows, feat_width = grad_out.shape
    half = jax.ShapeDtypeStruct((rows, feat_width // 2), jnp.bfloat16)
    return pl.pallas_call(
        code_kernel,
        out_shape=(half, half),
        in_specs=[pl.BlockSpec(memory_space=pltpu.VMEM)] * 2,
        out_specs=(pl.BlockSpec(memory_space=pltpu.VMEM), pl.BlockSpec(memory_space=pltpu.VMEM)),
    )(grad_out, grad_dither)


def terms_kernel(y_ref, act_ref, feature_ref, hidden_ref, out_ref):
    partial_value = lax.dot_general(
        y_ref[...], act_ref[...], (((0,), (0,)), ((), ())), preferred_element_type=jnp.float32
    )
    feat_rows, unit_cols = partial_value.shape
    block_count = feat_rows // BLOCK
    blocks = partial_value.reshape(block_count, BLOCK, unit_cols)
    magnitude = jnp.max(jnp.abs(blocks), axis=1, keepdims=True)
    block_scale = as_bf16_value((magnitude + epsilon) / W_LEVELS)
    feature_part = feature_ref[...].reshape(block_count, BLOCK, 1)
    code = blocks / block_scale + hidden_ref[...].reshape(1, 1, unit_cols) + feature_part
    code = as_bf16_value(code)
    out_ref[...] = (code * block_scale).astype(jnp.bfloat16).reshape(feat_rows, unit_cols)


def group_terms_kernel(y_hat, activations, feature_part, hidden_part, tile=256):
    tokens, feat_rows = y_hat.shape
    unit_cols = activations.shape[1]
    return pl.pallas_call(
        terms_kernel,
        out_shape=jax.ShapeDtypeStruct((feat_rows, unit_cols), jnp.bfloat16),
        grid=(unit_cols // tile,),
        in_specs=[
            pl.BlockSpec((tokens, feat_rows), lambda j: (0, 0)),
            pl.BlockSpec((tokens, tile), lambda j: (0, j)),
            pl.BlockSpec((feat_rows, 1), lambda j: (0, 0)),
            pl.BlockSpec((1, tile), lambda j: (0, j)),
        ],
        out_specs=pl.BlockSpec((feat_rows, tile), lambda j: (0, j)),
        compiler_params=pltpu.CompilerParams(vmem_limit_bytes=48 * 1024 * 1024),
    )(y_hat, activations, feature_part.reshape(feat_rows, 1), hidden_part.reshape(1, unit_cols))


def per_device(grad_out, activations, grad_dither, hidden_dither, feature_dither):
    row_count, feat_width = grad_out.shape
    blocks = feat_width // BLOCK
    first_local, second_local = coded_halves(grad_out, grad_dither)
    feature_noise = feature_dither[0].reshape(blocks // 2, 2, BLOCK).transpose(1, 0, 2).reshape(feat_width)
    hidden_noise = hidden_dither[0]
    half = feat_width // 2

    def terms_of(y_hat, part):
        terms = group_terms_kernel(y_hat, activations, feature_noise[part * half:(part + 1) * half], hidden_noise)
        return terms.reshape(RING, RING, BLOCK, terms.shape[1])

    (first_y,) = communicate(0, None, first_local, collective_id=1)
    first_out, second_y = communicate(0, terms_of(first_y, 0), second_local, collective_id=2)
    (second_out,) = communicate(1, terms_of(second_y, 1), None, collective_id=0)
    z = lax.axis_index("dp") % 2
    return jnp.where(z == 0, first_out, second_out)


def solution(mesh):
    placed = (
        P(("dp", "tensor"), None),
        P("dp", "tensor"),
        P(("dp", "tensor"), None),
        P("dp", "tensor"),
        P("dp", None),
    )
    return jax.shard_map(
        per_device, mesh=mesh, in_specs=placed, out_specs=P("dp", "tensor"), check_vma=False
    )
```

```python
import functools

import jax
import jax.numpy as jnp
from jax import lax
from jax.experimental import pallas as pl
from jax.experimental.pallas import tpu as pltpu
from jax.sharding import PartitionSpec as P

BLOCK = 128
Y_LEVELS = 8
W_LEVELS = 7


epsilon = 1e-06


def as_bf16_value(value):
    return lax.reduce_precision(value, exponent_bits=8, mantissa_bits=7)


def group_terms(partial_value, feature_part, hidden_part):
    feat_rows, unit_cols = partial_value.shape
    block_count = feat_rows // BLOCK
    blocks = partial_value.reshape(block_count, BLOCK, unit_cols)
    magnitude = jnp.max(jnp.abs(blocks), axis=1)
    block_scale = ((magnitude + epsilon) / W_LEVELS).astype(jnp.bfloat16)
    scaled = (blocks / block_scale.astype(jnp.float32)[:, None, :]).reshape(feat_rows, unit_cols)
    held = as_bf16_value(scaled + hidden_part[None, :] + feature_part[:, None])
    values = held.reshape(block_count, BLOCK, unit_cols) * block_scale.astype(jnp.float32)[:, None, :]
    return values.reshape(feat_rows, unit_cols).astype(jnp.bfloat16)


MESH = pl.DeviceIdType.MESH
RING = 4
TENSOR_RING = (0, 1, 3, 2, 4, 5, 7, 6)


def dp_at(y, x, z):
    return y * 8 + x * 2 + z


def ring_member(position):
    pair, within = position // 2, position % 2
    return pair * 2 + (within + pair) % 2


def sent_index(pos, direction, step):
    return (pos - direction * (step + 1) + 2 * RING) % RING


def remote(src, dst, send_sem, recv_sem, peer):
    return pltpu.make_async_remote_copy(
        src_ref=src, dst_ref=dst, send_sem=send_sem, recv_sem=recv_sem,
        device_id=peer, device_id_type=MESH)


def reduce_steps(chunk, terms_ref, out_ref, recv1, send1, res1, recv2, send2, res2, recvz, sendz,
                 ss1, sr1, ss2, sr2, ssz, srz):
    dp = lax.axis_index("dp")
    y, x, z = dp // 8, (dp // 2) % 4, dp % 2
    rows, cols = terms_ref.shape[2], terms_ref.shape[3]
    half, width = rows // 2, cols // 2
    x_up, x_dn = dp_at(y, (x + 1) % RING, z), dp_at(y, (x + RING - 1) % RING, z)
    y_up, y_dn = dp_at((y + 1) % RING, x, z), dp_at((y + RING - 1) % RING, x, z)
    first = [
        (x, 1, x_up, 0, 0, True),
        (x, -1, x_dn, half, 0, True),
        (y, 1, y_up, 0, width, False),
        (y, -1, y_dn, half, width, False),
    ]

    def local1(k, index):
        _, _, _, r0, c0, over_x = first[k]
        if over_x:
            return terms_ref.at[:, index, pl.ds(r0, half), pl.ds(c0, width)]
        return terms_ref.at[index, :, pl.ds(r0, half), pl.ds(c0, width)]

    pending = []
    copies = [None] * 4
    for k, (pos, direction, target, _, _, _) in enumerate(first):
        copies[k] = remote(local1(k, sent_index(pos, direction, 0)), recv1.at[k, 0],
                           ss1.at[k, 0], sr1.at[k, 0], {"dp": target})
        copies[k].start()
        pending.append(copies[k])
    yield
    for step in range(1, RING - 1):
        for k, (pos, direction, target, _, _, _) in enumerate(first):
            copies[k].wait_recv()
            index = sent_index(pos, direction, step)
            acc = recv1[k, step - 1].astype(jnp.float32) + local1(k, index)[...].astype(jnp.float32)
            send1[k, step - 1] = acc.astype(jnp.bfloat16)
            copies[k] = remote(send1.at[k, step - 1], recv1.at[k, step],
                               ss1.at[k, step], sr1.at[k, step], {"dp": target})
            copies[k].start()
            pending.append(copies[k])
        yield
    for k, (pos, _, _, _, _, _) in enumerate(first):
        copies[k].wait_recv()
        res1[k] = recv1[k, RING - 2].astype(jnp.float32) + local1(k, pos)[...].astype(jnp.float32)

    second = [(y, 1, y_up), (y, -1, y_dn), (x, 1, x_up), (x, -1, x_dn)]
    for k, (pos, direction, target) in enumerate(second):
        send2[k, 0] = res1[k, sent_index(pos, direction, 0)].astype(jnp.bfloat16)
        copies[k] = remote(send2.at[k, 0], recv2.at[k, 0], ss2.at[k, 0], sr2.at[k, 0], {"dp": target})
        copies[k].start()
        pending.append(copies[k])
    yield
    for step in range(1, RING - 1):
        for k, (pos, direction, target) in enumerate(second):
            copies[k].wait_recv()
            index = sent_index(pos, direction, step)
            acc = recv2[k, step - 1].astype(jnp.float32) + res1[k, index]
            send2[k, step] = acc.astype(jnp.bfloat16)
            copies[k] = remote(send2.at[k, step], recv2.at[k, step],
                               ss2.at[k, step], sr2.at[k, step], {"dp": target})
            copies[k].start()
            pending.append(copies[k])
        yield
    for k, (pos, _, _) in enumerate(second):
        copies[k].wait_recv()
        res2[k] = recv2[k, RING - 2].astype(jnp.float32) + res1[k, pos]

    swap = remote(sendz, recvz, ssz, srz, {"dp": dp_at(y, x, 1 - z)})
    corners = [(0, 0), (half, 0), (0, width), (half, width)]

    @pl.when(z != chunk)
    def _():
        for k in range(4):
            sendz[k] = res2[k].astype(jnp.bfloat16)
        swap.start()

    yield

    @pl.when(z == chunk)
    def _():
        swap.wait_recv()
        for k, (r0, c0) in enumerate(corners):
            out_ref[pl.ds(r0, half), pl.ds(c0, width)] = res2[k] + recvz[k].astype(jnp.float32)

    @pl.when(z != chunk)
    def _():
        for k, (r0, c0) in enumerate(corners):
            out_ref[pl.ds(r0, half), pl.ds(c0, width)] = res2[k]
        swap.wait_send()

    for copy in pending:
        copy.wait_send()


def gather_steps(local_ref, out_ref, send_sem, recv_sem):
    n = len(TENSOR_RING)
    me = lax.axis_index("tensor")
    pair = me // 2
    pos = pair * 2 + (me % 2 + pair) % 2
    right = ring_member((pos + 1) % n)
    left = ring_member((pos + n - 1) % n)
    rows, cols = local_ref.shape
    width = cols // 2
    out_ref[pl.ds(pl.multiple_of(me * rows, rows), rows), :] = local_ref[...]
    streams = [(right, 1, 0), (left, -1, width)]
    pending = []
    copies = [None, None]
    for step in range(n - 1):
        for d, (target, direction, c0) in enumerate(streams):
            if step == 0:
                src = local_ref.at[:, pl.ds(c0, width)]
            else:
                copies[d].wait_recv()
                owner = ring_member((pos - direction * step + 2 * n) % n)
                src = out_ref.at[pl.ds(pl.multiple_of(owner * rows, rows), rows), pl.ds(c0, width)]
            owner = ring_member((pos - direction * step + 2 * n) % n)
            copies[d] = remote(src, out_ref.at[pl.ds(pl.multiple_of(owner * rows, rows), rows), pl.ds(c0, width)],
                               send_sem.at[d, step], recv_sem.at[d, step], {"tensor": target})
            copies[d].start()
            pending.append(copies[d])
        yield
    for d in range(2):
        copies[d].wait_recv()
    for copy in pending:
        copy.wait_send()


def comm_kernel(chunk, do_reduce, do_gather, *refs):
    refs = list(refs)
    terms_ref = refs.pop(0) if do_reduce else None
    local_ref = refs.pop(0) if do_gather else None
    out_ref = refs.pop(0) if do_reduce else None
    gathered_ref = refs.pop(0) if do_gather else None
    reduce_scratch = refs[:14] if do_reduce else None
    gather_scratch = refs[-2:] if do_gather else None

    peers = []
    if do_reduce:
        dp = lax.axis_index("dp")
        y, x, z = dp // 8, (dp // 2) % 4, dp % 2
        for peer in (dp_at(y, (x + 1) % RING, z), dp_at(y, (x + RING - 1) % RING, z),
                     dp_at((y + 1) % RING, x, z), dp_at((y + RING - 1) % RING, x, z), dp_at(y, x, 1 - z)):
            peers.append({"dp": peer})
    if do_gather:
        n = len(TENSOR_RING)
        me = lax.axis_index("tensor")
        pair = me // 2
        pos = pair * 2 + (me % 2 + pair) % 2
        for peer in (ring_member((pos + 1) % n), ring_member((pos + n - 1) % n)):
            peers.append({"tensor": peer})
    barrier = pltpu.get_barrier_semaphore()
    for peer in peers:
        pl.semaphore_signal(barrier, inc=1, device_id=peer, device_id_type=MESH)
    pl.semaphore_wait(barrier, len(peers))

    runs = []
    if do_reduce:
        runs.append(reduce_steps(chunk, terms_ref, out_ref, *reduce_scratch))
    if do_gather:
        runs.append(gather_steps(local_ref, gathered_ref, *gather_scratch))
    pattern = [0, 1, 1] if len(runs) == 2 else [0]
    while runs:
        for which in pattern:
            if which < len(runs):
                try:
                    next(runs[which])
                except StopIteration:
                    runs.pop(which)
                    pattern = [0]
                    break


def communicate(chunk, terms=None, local=None, collective_id=0):
    do_reduce, do_gather = terms is not None, local is not None
    args, outs, scratch = [], [], []
    if do_reduce:
        rows, cols = terms.shape[2], terms.shape[3]
        half, width = rows // 2, cols // 2
        args.append(terms)
        outs.append(jax.ShapeDtypeStruct((rows, cols), jnp.float32))
        scratch += [
            pltpu.VMEM((4, RING - 1, RING, half, width), jnp.bfloat16),
            pltpu.VMEM((4, RING - 2, RING, half, width), jnp.bfloat16),
            pltpu.VMEM((4, RING, half, width), jnp.float32),
            pltpu.VMEM((4, RING - 1, half, width), jnp.bfloat16),
            pltpu.VMEM((4, RING - 1, half, width), jnp.bfloat16),
            pltpu.VMEM((4, half, width), jnp.float32),
            pltpu.VMEM((4, half, width), jnp.bfloat16),
            pltpu.VMEM((4, half, width), jnp.bfloat16),
            pltpu.SemaphoreType.DMA((4, RING - 1)),
            pltpu.SemaphoreType.DMA((4, RING - 1)),
            pltpu.SemaphoreType.DMA((4, RING - 1)),
            pltpu.SemaphoreType.DMA((4, RING - 1)),
            pltpu.SemaphoreType.DMA(()),
            pltpu.SemaphoreType.DMA(()),
        ]
    if do_gather:
        n = len(TENSOR_RING)
        args.append(local)
        outs.append(jax.ShapeDtypeStruct((n * local.shape[0], local.shape[1]), local.dtype))
        scratch += [pltpu.SemaphoreType.DMA((2, n - 1)), pltpu.SemaphoreType.DMA((2, n - 1))]
    return pl.pallas_call(
        functools.partial(comm_kernel, chunk, do_reduce, do_gather),
        out_shape=tuple(outs),
        in_specs=[pl.BlockSpec(memory_space=pltpu.VMEM)] * len(args),
        out_specs=tuple(pl.BlockSpec(memory_space=pltpu.VMEM) for _ in outs),
        scratch_shapes=scratch,
        compiler_params=pltpu.CompilerParams(
            collective_id=collective_id, has_side_effects=True, vmem_limit_bytes=48 * 1024 * 1024),
    )(*args)


def code_kernel(grad_ref, dither_ref, first_ref, second_ref):
    blocks = grad_ref.shape[1] // BLOCK
    for block in range(blocks):
        cols = pl.ds(block * BLOCK, BLOCK)
        grad_float = grad_ref[:, cols].astype(jnp.float32)
        magnitude = jnp.max(jnp.abs(grad_float), axis=1, keepdims=True)
        y_scale = as_bf16_value((magnitude + epsilon) / Y_LEVELS)
        code = as_bf16_value(grad_float / y_scale + dither_ref[:, cols])
        target = first_ref if block % 2 == 0 else second_ref
        target[:, pl.ds((block // 2) * BLOCK, BLOCK)] = (code * y_scale).astype(jnp.bfloat16)


def coded_halves(grad_out, grad_dither):
    rows, feat_width = grad_out.shape
    half = jax.ShapeDtypeStruct((rows, feat_width // 2), jnp.bfloat16)
    return pl.pallas_call(
        code_kernel,
        out_shape=(half, half),
        in_specs=[pl.BlockSpec(memory_space=pltpu.VMEM)] * 2,
        out_specs=(pl.BlockSpec(memory_space=pltpu.VMEM), pl.BlockSpec(memory_space=pltpu.VMEM)),
    )(grad_out, grad_dither)


def terms_kernel(y_ref, act_ref, feature_ref, hidden_ref, out_ref):
    partial_value = jnp.dot(y_ref[...], act_ref[...], preferred_element_type=jnp.float32)
    feat_rows, unit_cols = partial_value.shape
    block_count = feat_rows // BLOCK
    blocks = partial_value.reshape(block_count, BLOCK, unit_cols)
    magnitude = jnp.max(jnp.abs(blocks), axis=1, keepdims=True)
    block_scale = as_bf16_value((magnitude + epsilon) / W_LEVELS)
    feature_part = feature_ref[...].reshape(block_count, BLOCK, 1)
    code = blocks / block_scale + hidden_ref[...].reshape(1, 1, unit_cols) + feature_part
    code = as_bf16_value(code)
    out_ref[...] = (code * block_scale).astype(jnp.bfloat16).reshape(feat_rows, unit_cols)


def group_terms_kernel(y_hat, activations, feature_part, hidden_part, tile=256):
    tokens, feat_rows = y_hat.shape
    unit_cols = activations.shape[1]
    return pl.pallas_call(
        terms_kernel,
        out_shape=jax.ShapeDtypeStruct((feat_rows, unit_cols), jnp.bfloat16),
        grid=(unit_cols // tile,),
        in_specs=[
            pl.BlockSpec((feat_rows, tokens), lambda j: (0, 0)),
            pl.BlockSpec((tokens, tile), lambda j: (0, j)),
            pl.BlockSpec((feat_rows, 1), lambda j: (0, 0)),
            pl.BlockSpec((1, tile), lambda j: (0, j)),
        ],
        out_specs=pl.BlockSpec((feat_rows, tile), lambda j: (0, j)),
        compiler_params=pltpu.CompilerParams(vmem_limit_bytes=48 * 1024 * 1024),
    )(y_hat.T, activations, feature_part.reshape(feat_rows, 1), hidden_part.reshape(1, unit_cols))


def per_device(grad_out, activations, grad_dither, hidden_dither, feature_dither):
    row_count, feat_width = grad_out.shape
    blocks = feat_width // BLOCK
    first_local, second_local = coded_halves(grad_out, grad_dither)
    feature_noise = feature_dither[0].reshape(blocks // 2, 2, BLOCK).transpose(1, 0, 2).reshape(feat_width)
    hidden_noise = hidden_dither[0]
    half = feat_width // 2

    def terms_of(y_hat, part):
        terms = group_terms_kernel(y_hat, activations, feature_noise[part * half:(part + 1) * half], hidden_noise)
        return terms.reshape(RING, RING, BLOCK, terms.shape[1])

    (first_y,) = communicate(0, None, first_local, collective_id=1)
    first_out, second_y = communicate(0, terms_of(first_y, 0), second_local, collective_id=2)
    (second_out,) = communicate(1, terms_of(second_y, 1), None, collective_id=0)
    z = lax.axis_index("dp") % 2
    return jnp.where(z == 0, first_out, second_out)


def solution(mesh):
    placed = (
        P(("dp", "tensor"), None),
        P("dp", "tensor"),
        P(("dp", "tensor"), None),
        P("dp", "tensor"),
        P("dp", None),
    )
    return jax.shard_map(
        per_device, mesh=mesh, in_specs=placed, out_specs=P("dp", "tensor"), check_vma=False
    )
```

```python
import functools

import jax
import jax.numpy as jnp
from jax import lax
from jax.experimental import pallas as pl
from jax.experimental.pallas import tpu as pltpu
from jax.sharding import PartitionSpec as P

BLOCK = 128
Y_LEVELS = 8
W_LEVELS = 7


epsilon = 1e-06


def as_bf16_value(value):
    return lax.reduce_precision(value, exponent_bits=8, mantissa_bits=7)


def group_terms(partial_value, feature_part, hidden_part):
    feat_rows, unit_cols = partial_value.shape
    block_count = feat_rows // BLOCK
    blocks = partial_value.reshape(block_count, BLOCK, unit_cols)
    magnitude = jnp.max(jnp.abs(blocks), axis=1)
    block_scale = ((magnitude + epsilon) / W_LEVELS).astype(jnp.bfloat16)
    scaled = (blocks / block_scale.astype(jnp.float32)[:, None, :]).reshape(feat_rows, unit_cols)
    held = as_bf16_value(scaled + hidden_part[None, :] + feature_part[:, None])
    values = held.reshape(block_count, BLOCK, unit_cols) * block_scale.astype(jnp.float32)[:, None, :]
    return values.reshape(feat_rows, unit_cols).astype(jnp.bfloat16)


MESH = pl.DeviceIdType.MESH
RING = 4
TENSOR_RING = (0, 1, 3, 2, 4, 5, 7, 6)


def dp_at(y, x, z):
    return y * 8 + x * 2 + z


def ring_member(position):
    pair, within = position // 2, position % 2
    return pair * 2 + (within + pair) % 2


def sent_index(pos, direction, step):
    return (pos - direction * (step + 1) + 2 * RING) % RING


def remote(src, dst, send_sem, recv_sem, peer):
    return pltpu.make_async_remote_copy(
        src_ref=src, dst_ref=dst, send_sem=send_sem, recv_sem=recv_sem,
        device_id=peer, device_id_type=MESH)


def reduce_steps(chunk, terms_ref, out_ref, recv1, send1, res1, recv2, send2, res2, recvz, sendz,
                 ss1, sr1, ss2, sr2, ssz, srz):
    dp = lax.axis_index("dp")
    y, x, z = dp // 8, (dp // 2) % 4, dp % 2
    rows, cols = terms_ref.shape[2], terms_ref.shape[3]
    half, width = rows // 2, cols // 2
    x_up, x_dn = dp_at(y, (x + 1) % RING, z), dp_at(y, (x + RING - 1) % RING, z)
    y_up, y_dn = dp_at((y + 1) % RING, x, z), dp_at((y + RING - 1) % RING, x, z)
    first = [
        (x, 1, x_up, 0, 0, True),
        (x, -1, x_dn, half, 0, True),
        (y, 1, y_up, 0, width, False),
        (y, -1, y_dn, half, width, False),
    ]

    def local1(k, index):
        _, _, _, r0, c0, over_x = first[k]
        if over_x:
            return terms_ref.at[:, index, pl.ds(r0, half), pl.ds(c0, width)]
        return terms_ref.at[index, :, pl.ds(r0, half), pl.ds(c0, width)]

    pending = []
    copies = [None] * 4
    for k, (pos, direction, target, _, _, _) in enumerate(first):
        copies[k] = remote(local1(k, sent_index(pos, direction, 0)), recv1.at[k, 0],
                           ss1.at[k, 0], sr1.at[k, 0], {"dp": target})
        copies[k].start()
        pending.append(copies[k])
    yield
    for step in range(1, RING - 1):
        for k, (pos, direction, target, _, _, _) in enumerate(first):
            copies[k].wait_recv()
            index = sent_index(pos, direction, step)
            acc = recv1[k, step - 1].astype(jnp.float32) + local1(k, index)[...].astype(jnp.float32)
            send1[k, step - 1] = acc.astype(jnp.bfloat16)
            copies[k] = remote(send1.at[k, step - 1], recv1.at[k, step],
                               ss1.at[k, step], sr1.at[k, step], {"dp": target})
            copies[k].start()
            pending.append(copies[k])
        yield
    for k, (pos, _, _, _, _, _) in enumerate(first):
        copies[k].wait_recv()
        res1[k] = recv1[k, RING - 2].astype(jnp.float32) + local1(k, pos)[...].astype(jnp.float32)

    second = [(y, 1, y_up), (y, -1, y_dn), (x, 1, x_up), (x, -1, x_dn)]
    for k, (pos, direction, target) in enumerate(second):
        send2[k, 0] = res1[k, sent_index(pos, direction, 0)].astype(jnp.bfloat16)
        copies[k] = remote(send2.at[k, 0], recv2.at[k, 0], ss2.at[k, 0], sr2.at[k, 0], {"dp": target})
        copies[k].start()
        pending.append(copies[k])
    yield
    for step in range(1, RING - 1):
        for k, (pos, direction, target) in enumerate(second):
            copies[k].wait_recv()
            index = sent_index(pos, direction, step)
            acc = recv2[k, step - 1].astype(jnp.float32) + res1[k, index]
            send2[k, step] = acc.astype(jnp.bfloat16)
            copies[k] = remote(send2.at[k, step], recv2.at[k, step],
                               ss2.at[k, step], sr2.at[k, step], {"dp": target})
            copies[k].start()
            pending.append(copies[k])
        yield
    for k, (pos, _, _) in enumerate(second):
        copies[k].wait_recv()
        res2[k] = recv2[k, RING - 2].astype(jnp.float32) + res1[k, pos]

    swap = remote(sendz, recvz, ssz, srz, {"dp": dp_at(y, x, 1 - z)})
    corners = [(0, 0), (half, 0), (0, width), (half, width)]

    @pl.when(z != chunk)
    def _():
        for k in range(4):
            sendz[k] = res2[k].astype(jnp.bfloat16)
        swap.start()

    yield

    @pl.when(z == chunk)
    def _():
        swap.wait_recv()
        for k, (r0, c0) in enumerate(corners):
            out_ref[pl.ds(r0, half), pl.ds(c0, width)] = res2[k] + recvz[k].astype(jnp.float32)

    @pl.when(z != chunk)
    def _():
        for k, (r0, c0) in enumerate(corners):
            out_ref[pl.ds(r0, half), pl.ds(c0, width)] = res2[k]
        swap.wait_send()

    for copy in pending:
        copy.wait_send()


def gather_steps(local_ref, out_ref, send_sem, recv_sem):
    n = len(TENSOR_RING)
    me = lax.axis_index("tensor")
    pair = me // 2
    pos = pair * 2 + (me % 2 + pair) % 2
    right = ring_member((pos + 1) % n)
    left = ring_member((pos + n - 1) % n)
    rows, cols = local_ref.shape
    width = cols // 2
    out_ref[pl.ds(pl.multiple_of(me * rows, rows), rows), :] = local_ref[...]
    streams = [(right, 1, 0), (left, -1, width)]
    pending = []
    copies = [None, None]
    for step in range(n - 1):
        for d, (target, direction, c0) in enumerate(streams):
            if step == 0:
                src = local_ref.at[:, pl.ds(c0, width)]
            else:
                copies[d].wait_recv()
                owner = ring_member((pos - direction * step + 2 * n) % n)
                src = out_ref.at[pl.ds(pl.multiple_of(owner * rows, rows), rows), pl.ds(c0, width)]
            owner = ring_member((pos - direction * step + 2 * n) % n)
            copies[d] = remote(src, out_ref.at[pl.ds(pl.multiple_of(owner * rows, rows), rows), pl.ds(c0, width)],
                               send_sem.at[d, step], recv_sem.at[d, step], {"tensor": target})
            copies[d].start()
            pending.append(copies[d])
        yield
    for d in range(2):
        copies[d].wait_recv()
    for copy in pending:
        copy.wait_send()


def comm_kernel(chunk, do_reduce, do_gather, *refs):
    refs = list(refs)
    terms_ref = refs.pop(0) if do_reduce else None
    local_ref = refs.pop(0) if do_gather else None
    out_ref = refs.pop(0) if do_reduce else None
    gathered_ref = refs.pop(0) if do_gather else None
    reduce_scratch = refs[:14] if do_reduce else None
    gather_scratch = refs[-2:] if do_gather else None

    peers = []
    if do_reduce:
        dp = lax.axis_index("dp")
        y, x, z = dp // 8, (dp // 2) % 4, dp % 2
        for peer in (dp_at(y, (x + 1) % RING, z), dp_at(y, (x + RING - 1) % RING, z),
                     dp_at((y + 1) % RING, x, z), dp_at((y + RING - 1) % RING, x, z), dp_at(y, x, 1 - z)):
            peers.append({"dp": peer})
    if do_gather:
        n = len(TENSOR_RING)
        me = lax.axis_index("tensor")
        pair = me // 2
        pos = pair * 2 + (me % 2 + pair) % 2
        for peer in (ring_member((pos + 1) % n), ring_member((pos + n - 1) % n)):
            peers.append({"tensor": peer})
    barrier = pltpu.get_barrier_semaphore()
    for peer in peers:
        pl.semaphore_signal(barrier, inc=1, device_id=peer, device_id_type=MESH)
    pl.semaphore_wait(barrier, len(peers))

    runs = []
    if do_reduce:
        runs.append(reduce_steps(chunk, terms_ref, out_ref, *reduce_scratch))
    if do_gather:
        runs.append(gather_steps(local_ref, gathered_ref, *gather_scratch))
    pattern = [0, 1, 1] if len(runs) == 2 else [0]
    while runs:
        for which in pattern:
            if which < len(runs):
                try:
                    next(runs[which])
                except StopIteration:
                    runs.pop(which)
                    pattern = [0]
                    break


def communicate(chunk, terms=None, local=None, collective_id=0):
    do_reduce, do_gather = terms is not None, local is not None
    args, outs, scratch = [], [], []
    if do_reduce:
        rows, cols = terms.shape[2], terms.shape[3]
        half, width = rows // 2, cols // 2
        args.append(terms)
        outs.append(jax.ShapeDtypeStruct((rows, cols), jnp.float32))
        scratch += [
            pltpu.VMEM((4, RING - 1, RING, half, width), jnp.bfloat16),
            pltpu.VMEM((4, RING - 2, RING, half, width), jnp.bfloat16),
            pltpu.VMEM((4, RING, half, width), jnp.float32),
            pltpu.VMEM((4, RING - 1, half, width), jnp.bfloat16),
            pltpu.VMEM((4, RING - 1, half, width), jnp.bfloat16),
            pltpu.VMEM((4, half, width), jnp.float32),
            pltpu.VMEM((4, half, width), jnp.bfloat16),
            pltpu.VMEM((4, half, width), jnp.bfloat16),
            pltpu.SemaphoreType.DMA((4, RING - 1)),
            pltpu.SemaphoreType.DMA((4, RING - 1)),
            pltpu.SemaphoreType.DMA((4, RING - 1)),
            pltpu.SemaphoreType.DMA((4, RING - 1)),
            pltpu.SemaphoreType.DMA(()),
            pltpu.SemaphoreType.DMA(()),
        ]
    if do_gather:
        n = len(TENSOR_RING)
        args.append(local)
        outs.append(jax.ShapeDtypeStruct((n * local.shape[0], local.shape[1]), local.dtype))
        scratch += [pltpu.SemaphoreType.DMA((2, n - 1)), pltpu.SemaphoreType.DMA((2, n - 1))]
    return pl.pallas_call(
        functools.partial(comm_kernel, chunk, do_reduce, do_gather),
        out_shape=tuple(outs),
        in_specs=[pl.BlockSpec(memory_space=pltpu.VMEM)] * len(args),
        out_specs=tuple(pl.BlockSpec(memory_space=pltpu.VMEM) for _ in outs),
        scratch_shapes=scratch,
        compiler_params=pltpu.CompilerParams(
            collective_id=collective_id, has_side_effects=True, vmem_limit_bytes=48 * 1024 * 1024),
    )(*args)


def code_kernel(grad_ref, dither_ref, first_ref, second_ref):
    blocks = grad_ref.shape[1] // BLOCK
    for block in range(blocks):
        cols = pl.ds(block * BLOCK, BLOCK)
        grad_float = grad_ref[:, cols].astype(jnp.float32)
        magnitude = jnp.max(jnp.abs(grad_float), axis=1, keepdims=True)
        y_scale = ((magnitude + epsilon) / Y_LEVELS).astype(jnp.bfloat16).astype(jnp.float32)
        code = (grad_float / y_scale + dither_ref[:, cols]).astype(jnp.bfloat16).astype(jnp.float32)
        target = first_ref if block % 2 == 0 else second_ref
        target[:, pl.ds((block // 2) * BLOCK, BLOCK)] = (code * y_scale).astype(jnp.bfloat16)


def coded_halves(grad_out, grad_dither):
    rows, feat_width = grad_out.shape
    half = jax.ShapeDtypeStruct((rows, feat_width // 2), jnp.bfloat16)
    return pl.pallas_call(
        code_kernel,
        out_shape=(half, half),
        in_specs=[pl.BlockSpec(memory_space=pltpu.VMEM)] * 2,
        out_specs=(pl.BlockSpec(memory_space=pltpu.VMEM), pl.BlockSpec(memory_space=pltpu.VMEM)),
    )(grad_out, grad_dither)


def per_device(grad_out, activations, grad_dither, hidden_dither, feature_dither):
    row_count, feat_width = grad_out.shape
    blocks = feat_width // BLOCK
    first_local, second_local = coded_halves(grad_out, grad_dither)
    feature_noise = feature_dither[0].reshape(blocks // 2, 2, BLOCK).transpose(1, 0, 2).reshape(feat_width)
    hidden_noise = hidden_dither[0]
    half = feat_width // 2

    def terms_of(y_hat, part):
        pieces = []
        width = activations.shape[1] // 2
        for cols in (slice(0, width), slice(width, 2 * width)):
            partial_value = lax.dot_general(
                y_hat, activations[:, cols], (((0,), (0,)), ((), ())), preferred_element_type=jnp.float32
            )
            pieces.append(group_terms(partial_value, feature_noise[part * half:(part + 1) * half], hidden_noise[cols]))
        terms = jnp.concatenate(pieces, axis=1)
        return terms.reshape(RING, RING, BLOCK, terms.shape[1])

    (first_y,) = communicate(0, None, first_local, collective_id=1)
    first_out, second_y = communicate(0, terms_of(first_y, 0), second_local, collective_id=2)
    (second_out,) = communicate(1, terms_of(second_y, 1), None, collective_id=0)
    z = lax.axis_index("dp") % 2
    return jnp.where(z == 0, first_out, second_out)


def solution(mesh):
    placed = (
        P(("dp", "tensor"), None),
        P("dp", "tensor"),
        P(("dp", "tensor"), None),
        P("dp", "tensor"),
        P("dp", None),
    )
    return jax.shard_map(
        per_device, mesh=mesh, in_specs=placed, out_specs=P("dp", "tensor"), check_vma=False
    )
```

```python
import functools

import jax
import jax.numpy as jnp
from jax import lax
from jax.experimental import pallas as pl
from jax.experimental.pallas import tpu as pltpu
from jax.sharding import PartitionSpec as P

BLOCK = 128
Y_LEVELS = 8
W_LEVELS = 7


epsilon = 1e-06


def as_bf16_value(value):
    return lax.reduce_precision(value, exponent_bits=8, mantissa_bits=7)


def group_terms(partial_value, feature_part, hidden_part):
    feat_rows, unit_cols = partial_value.shape
    block_count = feat_rows // BLOCK
    blocks = partial_value.reshape(block_count, BLOCK, unit_cols)
    magnitude = jnp.max(jnp.abs(blocks), axis=1)
    block_scale = ((magnitude + epsilon) / W_LEVELS).astype(jnp.bfloat16)
    scaled = (blocks / block_scale.astype(jnp.float32)[:, None, :]).reshape(feat_rows, unit_cols)
    held = as_bf16_value(scaled + hidden_part[None, :] + feature_part[:, None])
    values = held.reshape(block_count, BLOCK, unit_cols) * block_scale.astype(jnp.float32)[:, None, :]
    return values.reshape(feat_rows, unit_cols).astype(jnp.bfloat16)


MESH = pl.DeviceIdType.MESH
RING = 4
TENSOR_RING = (0, 1, 3, 2, 4, 5, 7, 6)


def dp_at(y, x, z):
    return y * 8 + x * 2 + z


def ring_member(position):
    pair, within = position // 2, position % 2
    return pair * 2 + (within + pair) % 2


def sent_index(pos, direction, step):
    return (pos - direction * (step + 1) + 2 * RING) % RING


def remote(src, dst, send_sem, recv_sem, peer):
    return pltpu.make_async_remote_copy(
        src_ref=src, dst_ref=dst, send_sem=send_sem, recv_sem=recv_sem,
        device_id=peer, device_id_type=MESH)


def reduce_steps(chunk, first_ref, second_ref, out_ref, recv1, send1, res1, recv2, send2, res2, recvz, sendz,
                 ss1, sr1, ss2, sr2, ssz, srz):
    dp = lax.axis_index("dp")
    y, x, z = dp // 8, (dp // 2) % 4, dp % 2
    rows, width = first_ref.shape[2], first_ref.shape[3]
    half = rows // 2
    x_up, x_dn = dp_at(y, (x + 1) % RING, z), dp_at(y, (x + RING - 1) % RING, z)
    y_up, y_dn = dp_at((y + 1) % RING, x, z), dp_at((y + RING - 1) % RING, x, z)
    first = [
        (x, 1, x_up, 0, 0, True),
        (x, -1, x_dn, half, 0, True),
        (y, 1, y_up, 0, width, False),
        (y, -1, y_dn, half, width, False),
    ]

    def local1(k, index):
        _, _, _, r0, _, over_x = first[k]
        if over_x:
            return first_ref.at[:, index, pl.ds(r0, half), :]
        return second_ref.at[index, :, pl.ds(r0, half), :]

    pending = []
    copies = [None] * 4
    for k, (pos, direction, target, _, _, _) in enumerate(first):
        copies[k] = remote(local1(k, sent_index(pos, direction, 0)), recv1.at[k, 0],
                           ss1.at[k, 0], sr1.at[k, 0], {"dp": target})
        copies[k].start()
        pending.append(copies[k])
    yield
    for step in range(1, RING - 1):
        for k, (pos, direction, target, _, _, _) in enumerate(first):
            copies[k].wait_recv()
            index = sent_index(pos, direction, step)
            acc = recv1[k, step - 1].astype(jnp.float32) + local1(k, index)[...].astype(jnp.float32)
            send1[k, step - 1] = acc.astype(jnp.bfloat16)
            copies[k] = remote(send1.at[k, step - 1], recv1.at[k, step],
                               ss1.at[k, step], sr1.at[k, step], {"dp": target})
            copies[k].start()
            pending.append(copies[k])
        yield
    for k, (pos, _, _, _, _, _) in enumerate(first):
        copies[k].wait_recv()
        res1[k] = recv1[k, RING - 2].astype(jnp.float32) + local1(k, pos)[...].astype(jnp.float32)

    second = [(y, 1, y_up), (y, -1, y_dn), (x, 1, x_up), (x, -1, x_dn)]
    for k, (pos, direction, target) in enumerate(second):
        send2[k, 0] = res1[k, sent_index(pos, direction, 0)].astype(jnp.bfloat16)
        copies[k] = remote(send2.at[k, 0], recv2.at[k, 0], ss2.at[k, 0], sr2.at[k, 0], {"dp": target})
        copies[k].start()
        pending.append(copies[k])
    yield
    for step in range(1, RING - 1):
        for k, (pos, direction, target) in enumerate(second):
            copies[k].wait_recv()
            index = sent_index(pos, direction, step)
            acc = recv2[k, step - 1].astype(jnp.float32) + res1[k, index]
            send2[k, step] = acc.astype(jnp.bfloat16)
            copies[k] = remote(send2.at[k, step], recv2.at[k, step],
                               ss2.at[k, step], sr2.at[k, step], {"dp": target})
            copies[k].start()
            pending.append(copies[k])
        yield
    for k, (pos, _, _) in enumerate(second):
        copies[k].wait_recv()
        res2[k] = recv2[k, RING - 2].astype(jnp.float32) + res1[k, pos]

    swap = remote(sendz, recvz, ssz, srz, {"dp": dp_at(y, x, 1 - z)})
    corners = [(0, 0), (half, 0), (0, width), (half, width)]

    @pl.when(z != chunk)
    def _():
        for k in range(4):
            sendz[k] = res2[k].astype(jnp.bfloat16)
        swap.start()

    yield

    @pl.when(z == chunk)
    def _():
        swap.wait_recv()
        for k, (r0, c0) in enumerate(corners):
            out_ref[pl.ds(r0, half), pl.ds(c0, width)] = res2[k] + recvz[k].astype(jnp.float32)

    @pl.when(z != chunk)
    def _():
        for k, (r0, c0) in enumerate(corners):
            out_ref[pl.ds(r0, half), pl.ds(c0, width)] = res2[k]
        swap.wait_send()

    for copy in pending:
        copy.wait_send()


def gather_steps(local_ref, out_ref, send_sem, recv_sem):
    n = len(TENSOR_RING)
    me = lax.axis_index("tensor")
    pair = me // 2
    pos = pair * 2 + (me % 2 + pair) % 2
    right = ring_member((pos + 1) % n)
    left = ring_member((pos + n - 1) % n)
    rows, cols = local_ref.shape
    width = cols // 2
    out_ref[pl.ds(pl.multiple_of(me * rows, rows), rows), :] = local_ref[...]
    streams = [(right, 1, 0), (left, -1, width)]
    pending = []
    copies = [None, None]
    for step in range(n - 1):
        for d, (target, direction, c0) in enumerate(streams):
            if step == 0:
                src = local_ref.at[:, pl.ds(c0, width)]
            else:
                copies[d].wait_recv()
                owner = ring_member((pos - direction * step + 2 * n) % n)
                src = out_ref.at[pl.ds(pl.multiple_of(owner * rows, rows), rows), pl.ds(c0, width)]
            owner = ring_member((pos - direction * step + 2 * n) % n)
            copies[d] = remote(src, out_ref.at[pl.ds(pl.multiple_of(owner * rows, rows), rows), pl.ds(c0, width)],
                               send_sem.at[d, step], recv_sem.at[d, step], {"tensor": target})
            copies[d].start()
            pending.append(copies[d])
        yield
    for d in range(2):
        copies[d].wait_recv()
    for copy in pending:
        copy.wait_send()


def comm_kernel(chunk, do_reduce, do_gather, *refs):
    refs = list(refs)
    terms_refs = [refs.pop(0), refs.pop(0)] if do_reduce else None
    local_ref = refs.pop(0) if do_gather else None
    out_ref = refs.pop(0) if do_reduce else None
    gathered_ref = refs.pop(0) if do_gather else None
    reduce_scratch = refs[:14] if do_reduce else None
    gather_scratch = refs[-2:] if do_gather else None

    peers = []
    if do_reduce:
        dp = lax.axis_index("dp")
        y, x, z = dp // 8, (dp // 2) % 4, dp % 2
        for peer in (dp_at(y, (x + 1) % RING, z), dp_at(y, (x + RING - 1) % RING, z),
                     dp_at((y + 1) % RING, x, z), dp_at((y + RING - 1) % RING, x, z), dp_at(y, x, 1 - z)):
            peers.append({"dp": peer})
    if do_gather:
        n = len(TENSOR_RING)
        me = lax.axis_index("tensor")
        pair = me // 2
        pos = pair * 2 + (me % 2 + pair) % 2
        for peer in (ring_member((pos + 1) % n), ring_member((pos + n - 1) % n)):
            peers.append({"tensor": peer})
    barrier = pltpu.get_barrier_semaphore()
    for peer in peers:
        pl.semaphore_signal(barrier, inc=1, device_id=peer, device_id_type=MESH)
    pl.semaphore_wait(barrier, len(peers))

    runs = []
    if do_reduce:
        runs.append(reduce_steps(chunk, *terms_refs, out_ref, *reduce_scratch))
    if do_gather:
        runs.append(gather_steps(local_ref, gathered_ref, *gather_scratch))
    pattern = [0, 1, 1] if len(runs) == 2 else [0]
    while runs:
        for which in pattern:
            if which < len(runs):
                try:
                    next(runs[which])
                except StopIteration:
                    runs.pop(which)
                    pattern = [0]
                    break


def communicate(chunk, terms=None, local=None, collective_id=0):
    do_reduce, do_gather = terms is not None, local is not None
    args, outs, scratch = [], [], []
    if do_reduce:
        rows, width = terms[0].shape[2], terms[0].shape[3]
        half = rows // 2
        args.extend(terms)
        outs.append(jax.ShapeDtypeStruct((rows, 2 * width), jnp.float32))
        scratch += [
            pltpu.VMEM((4, RING - 1, RING, half, width), jnp.bfloat16),
            pltpu.VMEM((4, RING - 2, RING, half, width), jnp.bfloat16),
            pltpu.VMEM((4, RING, half, width), jnp.float32),
            pltpu.VMEM((4, RING - 1, half, width), jnp.bfloat16),
            pltpu.VMEM((4, RING - 1, half, width), jnp.bfloat16),
            pltpu.VMEM((4, half, width), jnp.float32),
            pltpu.VMEM((4, half, width), jnp.bfloat16),
            pltpu.VMEM((4, half, width), jnp.bfloat16),
            pltpu.SemaphoreType.DMA((4, RING - 1)),
            pltpu.SemaphoreType.DMA((4, RING - 1)),
            pltpu.SemaphoreType.DMA((4, RING - 1)),
            pltpu.SemaphoreType.DMA((4, RING - 1)),
            pltpu.SemaphoreType.DMA(()),
            pltpu.SemaphoreType.DMA(()),
        ]
    if do_gather:
        n = len(TENSOR_RING)
        args.append(local)
        outs.append(jax.ShapeDtypeStruct((n * local.shape[0], local.shape[1]), local.dtype))
        scratch += [pltpu.SemaphoreType.DMA((2, n - 1)), pltpu.SemaphoreType.DMA((2, n - 1))]
    return pl.pallas_call(
        functools.partial(comm_kernel, chunk, do_reduce, do_gather),
        out_shape=tuple(outs),
        in_specs=[pl.BlockSpec(memory_space=pltpu.VMEM)] * len(args),
        out_specs=tuple(pl.BlockSpec(memory_space=pltpu.VMEM) for _ in outs),
        scratch_shapes=scratch,
        compiler_params=pltpu.CompilerParams(
            collective_id=collective_id, has_side_effects=True, vmem_limit_bytes=48 * 1024 * 1024),
    )(*args)


def code_kernel(grad_ref, dither_ref, first_ref, second_ref):
    blocks = grad_ref.shape[1] // BLOCK
    for block in range(blocks):
        cols = pl.ds(block * BLOCK, BLOCK)
        grad_float = grad_ref[:, cols].astype(jnp.float32)
        magnitude = jnp.max(jnp.abs(grad_float), axis=1, keepdims=True)
        y_scale = ((magnitude + epsilon) / Y_LEVELS).astype(jnp.bfloat16).astype(jnp.float32)
        code = (grad_float / y_scale + dither_ref[:, cols]).astype(jnp.bfloat16).astype(jnp.float32)
        target = first_ref if block % 2 == 0 else second_ref
        target[:, pl.ds((block // 2) * BLOCK, BLOCK)] = (code * y_scale).astype(jnp.bfloat16)


def coded_halves(grad_out, grad_dither):
    rows, feat_width = grad_out.shape
    half = jax.ShapeDtypeStruct((rows, feat_width // 2), jnp.bfloat16)
    return pl.pallas_call(
        code_kernel,
        out_shape=(half, half),
        in_specs=[pl.BlockSpec(memory_space=pltpu.VMEM)] * 2,
        out_specs=(pl.BlockSpec(memory_space=pltpu.VMEM), pl.BlockSpec(memory_space=pltpu.VMEM)),
    )(grad_out, grad_dither)


def per_device(grad_out, activations, grad_dither, hidden_dither, feature_dither):
    row_count, feat_width = grad_out.shape
    blocks = feat_width // BLOCK
    first_local, second_local = coded_halves(grad_out, grad_dither)
    feature_noise = feature_dither[0].reshape(blocks // 2, 2, BLOCK).transpose(1, 0, 2).reshape(feat_width)
    hidden_noise = hidden_dither[0]
    half = feat_width // 2

    def terms_of(y_hat, part):
        pieces = []
        width = activations.shape[1] // 2
        for cols in (slice(0, width), slice(width, 2 * width)):
            partial_value = lax.dot_general(
                y_hat, activations[:, cols], (((0,), (0,)), ((), ())), preferred_element_type=jnp.float32
            )
            pieces.append(group_terms(partial_value, feature_noise[part * half:(part + 1) * half], hidden_noise[cols]))
        return tuple(piece.reshape(RING, RING, BLOCK, piece.shape[1]) for piece in pieces)

    (first_y,) = communicate(0, None, first_local, collective_id=1)
    first_out, second_y = communicate(0, terms_of(first_y, 0), second_local, collective_id=2)
    (second_out,) = communicate(1, terms_of(second_y, 1), None, collective_id=0)
    z = lax.axis_index("dp") % 2
    return jnp.where(z == 0, first_out, second_out)


def solution(mesh):
    placed = (
        P(("dp", "tensor"), None),
        P("dp", "tensor"),
        P(("dp", "tensor"), None),
        P("dp", "tensor"),
        P("dp", None),
    )
    return jax.shard_map(
        per_device, mesh=mesh, in_specs=placed, out_specs=P("dp", "tensor"), check_vma=False
    )
```

```python
import functools

import jax
import jax.numpy as jnp
from jax import lax
from jax.experimental import pallas as pl
from jax.experimental.pallas import tpu as pltpu
from jax.sharding import PartitionSpec as P

BLOCK = 128
Y_LEVELS = 8
W_LEVELS = 7


epsilon = 1e-06


def as_bf16_value(value):
    return lax.reduce_precision(value, exponent_bits=8, mantissa_bits=7)


def group_terms(partial_value, feature_part, hidden_part):
    feat_rows, unit_cols = partial_value.shape
    block_count = feat_rows // BLOCK
    blocks = partial_value.reshape(block_count, BLOCK, unit_cols)
    magnitude = jnp.max(jnp.abs(blocks), axis=1)
    block_scale = ((magnitude + epsilon) / W_LEVELS).astype(jnp.bfloat16)
    scaled = (blocks / block_scale.astype(jnp.float32)[:, None, :]).reshape(feat_rows, unit_cols)
    held = as_bf16_value(scaled + hidden_part[None, :] + feature_part[:, None])
    values = held.reshape(block_count, BLOCK, unit_cols) * block_scale.astype(jnp.float32)[:, None, :]
    return values.reshape(feat_rows, unit_cols).astype(jnp.bfloat16)


MESH = pl.DeviceIdType.MESH
RING = 4
TENSOR_RING = (0, 1, 3, 2, 4, 5, 7, 6)


def dp_at(y, x, z):
    return y * 8 + x * 2 + z


def ring_member(position):
    pair, within = position // 2, position % 2
    return pair * 2 + (within + pair) % 2


def sent_index(pos, direction, step):
    return (pos - direction * (step + 1) + 2 * RING) % RING


def remote(src, dst, send_sem, recv_sem, peer):
    return pltpu.make_async_remote_copy(
        src_ref=src, dst_ref=dst, send_sem=send_sem, recv_sem=recv_sem,
        device_id=peer, device_id_type=MESH)


def reduce_steps(chunk, first_ref, second_ref, out_ref, recv1, send1, res1, recv2, send2, res2, recvz, sendz,
                 ss1, sr1, ss2, sr2, ssz, srz):
    dp = lax.axis_index("dp")
    y, x, z = dp // 8, (dp // 2) % 4, dp % 2
    rows, width = first_ref.shape[2], first_ref.shape[3]
    half = rows // 2
    x_up, x_dn = dp_at(y, (x + 1) % RING, z), dp_at(y, (x + RING - 1) % RING, z)
    y_up, y_dn = dp_at((y + 1) % RING, x, z), dp_at((y + RING - 1) % RING, x, z)
    first = [
        (x, 1, x_up, 0, 0, True),
        (x, -1, x_dn, half, 0, True),
        (y, 1, y_up, 0, width, False),
        (y, -1, y_dn, half, width, False),
    ]

    def local1(k, index):
        _, _, _, r0, _, over_x = first[k]
        if over_x:
            return first_ref.at[:, index, pl.ds(r0, half), :]
        return second_ref.at[index, :, pl.ds(r0, half), :]

    pending = []
    copies = [None] * 4
    for k, (pos, direction, target, _, _, _) in enumerate(first):
        copies[k] = remote(local1(k, sent_index(pos, direction, 0)), recv1.at[k, 0],
                           ss1.at[k, 0], sr1.at[k, 0], {"dp": target})
        copies[k].start()
        pending.append(copies[k])
    yield
    for step in range(1, RING - 1):
        for k, (pos, direction, target, _, _, _) in enumerate(first):
            copies[k].wait_recv()
            index = sent_index(pos, direction, step)
            acc = recv1[k, step - 1].astype(jnp.float32) + local1(k, index)[...].astype(jnp.float32)
            send1[k, step - 1] = acc.astype(jnp.bfloat16)
            copies[k] = remote(send1.at[k, step - 1], recv1.at[k, step],
                               ss1.at[k, step], sr1.at[k, step], {"dp": target})
            copies[k].start()
            pending.append(copies[k])
        yield
    for k, (pos, _, _, _, _, _) in enumerate(first):
        copies[k].wait_recv()
        res1[k] = recv1[k, RING - 2].astype(jnp.float32) + local1(k, pos)[...].astype(jnp.float32)

    second = [(y, 1, y_up), (y, -1, y_dn), (x, 1, x_up), (x, -1, x_dn)]
    for k, (pos, direction, target) in enumerate(second):
        send2[k, 0] = res1[k, sent_index(pos, direction, 0)].astype(jnp.bfloat16)
        copies[k] = remote(send2.at[k, 0], recv2.at[k, 0], ss2.at[k, 0], sr2.at[k, 0], {"dp": target})
        copies[k].start()
        pending.append(copies[k])
    yield
    for step in range(1, RING - 1):
        for k, (pos, direction, target) in enumerate(second):
            copies[k].wait_recv()
            index = sent_index(pos, direction, step)
            acc = recv2[k, step - 1].astype(jnp.float32) + res1[k, index]
            send2[k, step] = acc.astype(jnp.bfloat16)
            copies[k] = remote(send2.at[k, step], recv2.at[k, step],
                               ss2.at[k, step], sr2.at[k, step], {"dp": target})
            copies[k].start()
            pending.append(copies[k])
        yield
    for k, (pos, _, _) in enumerate(second):
        copies[k].wait_recv()
        res2[k] = recv2[k, RING - 2].astype(jnp.float32) + res1[k, pos]

    swap = remote(sendz, recvz, ssz, srz, {"dp": dp_at(y, x, 1 - z)})
    corners = [(0, 0), (half, 0), (0, width), (half, width)]

    @pl.when(z != chunk)
    def _():
        for k in range(4):
            sendz[k] = res2[k].astype(jnp.bfloat16)
        swap.start()

    yield

    @pl.when(z == chunk)
    def _():
        swap.wait_recv()
        for k, (r0, c0) in enumerate(corners):
            out_ref[pl.ds(r0, half), pl.ds(c0, width)] = res2[k] + recvz[k].astype(jnp.float32)

    @pl.when(z != chunk)
    def _():
        for k, (r0, c0) in enumerate(corners):
            out_ref[pl.ds(r0, half), pl.ds(c0, width)] = res2[k]
        swap.wait_send()

    for copy in pending:
        copy.wait_send()


def gather_steps(local_ref, out_ref, send_sem, recv_sem):
    n = len(TENSOR_RING)
    me = lax.axis_index("tensor")
    pair = me // 2
    pos = pair * 2 + (me % 2 + pair) % 2
    right = ring_member((pos + 1) % n)
    left = ring_member((pos + n - 1) % n)
    rows, cols = local_ref.shape
    width = cols // 2
    out_ref[pl.ds(pl.multiple_of(me * rows, rows), rows), :] = local_ref[...]
    streams = [(right, 1, 0), (left, -1, width)]
    pending = []
    copies = [None, None]
    for step in range(n - 1):
        for d, (target, direction, c0) in enumerate(streams):
            if step == 0:
                src = local_ref.at[:, pl.ds(c0, width)]
            else:
                copies[d].wait_recv()
                owner = ring_member((pos - direction * step + 2 * n) % n)
                src = out_ref.at[pl.ds(pl.multiple_of(owner * rows, rows), rows), pl.ds(c0, width)]
            owner = ring_member((pos - direction * step + 2 * n) % n)
            copies[d] = remote(src, out_ref.at[pl.ds(pl.multiple_of(owner * rows, rows), rows), pl.ds(c0, width)],
                               send_sem.at[d, step], recv_sem.at[d, step], {"tensor": target})
            copies[d].start()
            pending.append(copies[d])
        yield
    for d in range(2):
        copies[d].wait_recv()
    for copy in pending:
        copy.wait_send()


def comm_kernel(chunk, do_reduce, do_gather, *refs):
    refs = list(refs)
    terms_refs = [refs.pop(0), refs.pop(0)] if do_reduce else None
    local_ref = refs.pop(0) if do_gather else None
    out_ref = refs.pop(0) if do_reduce else None
    gathered_ref = refs.pop(0) if do_gather else None
    reduce_scratch = refs[:14] if do_reduce else None
    gather_scratch = refs[-2:] if do_gather else None

    peers = []
    if do_reduce:
        dp = lax.axis_index("dp")
        y, x, z = dp // 8, (dp // 2) % 4, dp % 2
        for peer in (dp_at(y, (x + 1) % RING, z), dp_at(y, (x + RING - 1) % RING, z),
                     dp_at((y + 1) % RING, x, z), dp_at((y + RING - 1) % RING, x, z), dp_at(y, x, 1 - z)):
            peers.append({"dp": peer})
    if do_gather:
        n = len(TENSOR_RING)
        me = lax.axis_index("tensor")
        pair = me // 2
        pos = pair * 2 + (me % 2 + pair) % 2
        for peer in (ring_member((pos + 1) % n), ring_member((pos + n - 1) % n)):
            peers.append({"tensor": peer})
    barrier = pltpu.get_barrier_semaphore()
    for peer in peers:
        pl.semaphore_signal(barrier, inc=1, device_id=peer, device_id_type=MESH)
    pl.semaphore_wait(barrier, len(peers))

    runs = []
    if do_reduce:
        runs.append(reduce_steps(chunk, *terms_refs, out_ref, *reduce_scratch))
    if do_gather:
        runs.append(gather_steps(local_ref, gathered_ref, *gather_scratch))
    pattern = [0, 1] if len(runs) == 2 else [0]
    while runs:
        for which in pattern:
            if which < len(runs):
                try:
                    next(runs[which])
                except StopIteration:
                    runs.pop(which)
                    pattern = [0]
                    break


def communicate(chunk, terms=None, local=None, collective_id=0):
    do_reduce, do_gather = terms is not None, local is not None
    args, outs, scratch = [], [], []
    if do_reduce:
        rows, width = terms[0].shape[2], terms[0].shape[3]
        half = rows // 2
        args.extend(terms)
        outs.append(jax.ShapeDtypeStruct((rows, 2 * width), jnp.float32))
        scratch += [
            pltpu.VMEM((4, RING - 1, RING, half, width), jnp.bfloat16),
            pltpu.VMEM((4, RING - 2, RING, half, width), jnp.bfloat16),
            pltpu.VMEM((4, RING, half, width), jnp.float32),
            pltpu.VMEM((4, RING - 1, half, width), jnp.bfloat16),
            pltpu.VMEM((4, RING - 1, half, width), jnp.bfloat16),
            pltpu.VMEM((4, half, width), jnp.float32),
            pltpu.VMEM((4, half, width), jnp.bfloat16),
            pltpu.VMEM((4, half, width), jnp.bfloat16),
            pltpu.SemaphoreType.DMA((4, RING - 1)),
            pltpu.SemaphoreType.DMA((4, RING - 1)),
            pltpu.SemaphoreType.DMA((4, RING - 1)),
            pltpu.SemaphoreType.DMA((4, RING - 1)),
            pltpu.SemaphoreType.DMA(()),
            pltpu.SemaphoreType.DMA(()),
        ]
    if do_gather:
        n = len(TENSOR_RING)
        args.append(local)
        outs.append(jax.ShapeDtypeStruct((n * local.shape[0], local.shape[1]), local.dtype))
        scratch += [pltpu.SemaphoreType.DMA((2, n - 1)), pltpu.SemaphoreType.DMA((2, n - 1))]
    return pl.pallas_call(
        functools.partial(comm_kernel, chunk, do_reduce, do_gather),
        out_shape=tuple(outs),
        in_specs=[pl.BlockSpec(memory_space=pltpu.VMEM)] * len(args),
        out_specs=tuple(pl.BlockSpec(memory_space=pltpu.VMEM) for _ in outs),
        scratch_shapes=scratch,
        compiler_params=pltpu.CompilerParams(
            collective_id=collective_id, has_side_effects=True, vmem_limit_bytes=48 * 1024 * 1024),
    )(*args)


def code_kernel(grad_ref, dither_ref, first_ref, second_ref):
    blocks = grad_ref.shape[1] // BLOCK
    for block in range(blocks):
        cols = pl.ds(block * BLOCK, BLOCK)
        grad_float = grad_ref[:, cols].astype(jnp.float32)
        magnitude = jnp.max(jnp.abs(grad_float), axis=1, keepdims=True)
        y_scale = ((magnitude + epsilon) / Y_LEVELS).astype(jnp.bfloat16).astype(jnp.float32)
        code = (grad_float / y_scale + dither_ref[:, cols]).astype(jnp.bfloat16).astype(jnp.float32)
        target = first_ref if block % 2 == 0 else second_ref
        target[:, pl.ds((block // 2) * BLOCK, BLOCK)] = (code * y_scale).astype(jnp.bfloat16)


def coded_halves(grad_out, grad_dither):
    rows, feat_width = grad_out.shape
    half = jax.ShapeDtypeStruct((rows, feat_width // 2), jnp.bfloat16)
    return pl.pallas_call(
        code_kernel,
        out_shape=(half, half),
        in_specs=[pl.BlockSpec(memory_space=pltpu.VMEM)] * 2,
        out_specs=(pl.BlockSpec(memory_space=pltpu.VMEM), pl.BlockSpec(memory_space=pltpu.VMEM)),
    )(grad_out, grad_dither)


def per_device(grad_out, activations, grad_dither, hidden_dither, feature_dither):
    row_count, feat_width = grad_out.shape
    blocks = feat_width // BLOCK
    first_local, second_local = coded_halves(grad_out, grad_dither)
    feature_noise = feature_dither[0].reshape(blocks // 2, 2, BLOCK).transpose(1, 0, 2).reshape(feat_width)
    hidden_noise = hidden_dither[0]
    half = feat_width // 2

    def terms_of(y_hat, part):
        pieces = []
        width = activations.shape[1] // 2
        for cols in (slice(0, width), slice(width, 2 * width)):
            partial_value = lax.dot_general(
                y_hat, activations[:, cols], (((0,), (0,)), ((), ())), preferred_element_type=jnp.float32
            )
            pieces.append(group_terms(partial_value, feature_noise[part * half:(part + 1) * half], hidden_noise[cols]))
        return tuple(piece.reshape(RING, RING, BLOCK, piece.shape[1]) for piece in pieces)

    (first_y,) = communicate(0, None, first_local, collective_id=1)
    first_out, second_y = communicate(0, terms_of(first_y, 0), second_local, collective_id=2)
    (second_out,) = communicate(1, terms_of(second_y, 1), None, collective_id=0)
    z = lax.axis_index("dp") % 2
    return jnp.where(z == 0, first_out, second_out)


def solution(mesh):
    placed = (
        P(("dp", "tensor"), None),
        P("dp", "tensor"),
        P(("dp", "tensor"), None),
        P("dp", "tensor"),
        P("dp", None),
    )
    return jax.shard_map(
        per_device, mesh=mesh, in_specs=placed, out_specs=P("dp", "tensor"), check_vma=False
    )
```

```python
import functools

import jax
import jax.numpy as jnp
from jax import lax
from jax.experimental import pallas as pl
from jax.experimental.pallas import tpu as pltpu
from jax.sharding import PartitionSpec as P

BLOCK = 128
Y_LEVELS = 8
W_LEVELS = 7


epsilon = 1e-06


def as_bf16_value(value):
    return lax.reduce_precision(value, exponent_bits=8, mantissa_bits=7)


def group_terms(partial_value, feature_part, hidden_part):
    feat_rows, unit_cols = partial_value.shape
    block_count = feat_rows // BLOCK
    blocks = partial_value.reshape(block_count, BLOCK, unit_cols)
    magnitude = jnp.max(jnp.abs(blocks), axis=1)
    block_scale = ((magnitude + epsilon) / W_LEVELS).astype(jnp.bfloat16)
    scaled = (blocks / block_scale.astype(jnp.float32)[:, None, :]).reshape(feat_rows, unit_cols)
    held = as_bf16_value(scaled + hidden_part[None, :] + feature_part[:, None])
    values = held.reshape(block_count, BLOCK, unit_cols) * block_scale.astype(jnp.float32)[:, None, :]
    return values.reshape(feat_rows, unit_cols).astype(jnp.bfloat16)


MESH = pl.DeviceIdType.MESH
RING = 4
TENSOR_RING = (0, 1, 3, 2, 4, 5, 7, 6)


def dp_at(y, x, z):
    return y * 8 + x * 2 + z


def ring_member(position):
    pair, within = position // 2, position % 2
    return pair * 2 + (within + pair) % 2


def sent_index(pos, direction, step):
    return (pos - direction * (step + 1) + 2 * RING) % RING


def remote(src, dst, send_sem, recv_sem, peer):
    return pltpu.make_async_remote_copy(
        src_ref=src, dst_ref=dst, send_sem=send_sem, recv_sem=recv_sem,
        device_id=peer, device_id_type=MESH)


def reduce_steps(chunk, first_ref, second_ref, kept_ref, out_ref, recv1, send1, res1, recv2, send2, res2, recvz, sendz,
                 ss1, sr1, ss2, sr2, ssz, srz):
    dp = lax.axis_index("dp")
    y, x, z = dp // 8, (dp // 2) % 4, dp % 2
    rows, width = first_ref.shape[2], first_ref.shape[3]
    half = rows // 2
    x_up, x_dn = dp_at(y, (x + 1) % RING, z), dp_at(y, (x + RING - 1) % RING, z)
    y_up, y_dn = dp_at((y + 1) % RING, x, z), dp_at((y + RING - 1) % RING, x, z)
    first = [
        (x, 1, x_up, 0, 0, True),
        (x, -1, x_dn, half, 0, True),
        (y, 1, y_up, 0, width, False),
        (y, -1, y_dn, half, width, False),
    ]

    def local1(k, index):
        _, _, _, r0, _, over_x = first[k]
        if over_x:
            return first_ref.at[:, index, pl.ds(r0, half), :]
        return second_ref.at[index, :, pl.ds(r0, half), :]

    pending = []
    copies = [None] * 4
    for k, (pos, direction, target, _, _, _) in enumerate(first):
        copies[k] = remote(local1(k, sent_index(pos, direction, 0)), recv1.at[k, 0],
                           ss1.at[k, 0], sr1.at[k, 0], {"dp": target})
        copies[k].start()
        pending.append(copies[k])
    yield
    for step in range(1, RING - 1):
        for k, (pos, direction, target, _, _, _) in enumerate(first):
            copies[k].wait_recv()
            index = sent_index(pos, direction, step)
            acc = recv1[k, step - 1].astype(jnp.float32) + local1(k, index)[...].astype(jnp.float32)
            send1[k, step - 1] = acc.astype(jnp.bfloat16)
            copies[k] = remote(send1.at[k, step - 1], recv1.at[k, step],
                               ss1.at[k, step], sr1.at[k, step], {"dp": target})
            copies[k].start()
            pending.append(copies[k])
        yield
    for k, (pos, _, _, _, _, _) in enumerate(first):
        copies[k].wait_recv()
        res1[k] = recv1[k, RING - 2].astype(jnp.float32) + local1(k, pos)[...].astype(jnp.float32)

    second = [(y, 1, y_up), (y, -1, y_dn), (x, 1, x_up), (x, -1, x_dn)]
    for k, (pos, direction, target) in enumerate(second):
        send2[k, 0] = res1[k, sent_index(pos, direction, 0)].astype(jnp.bfloat16)
        copies[k] = remote(send2.at[k, 0], recv2.at[k, 0], ss2.at[k, 0], sr2.at[k, 0], {"dp": target})
        copies[k].start()
        pending.append(copies[k])
    yield
    for step in range(1, RING - 1):
        for k, (pos, direction, target) in enumerate(second):
            copies[k].wait_recv()
            index = sent_index(pos, direction, step)
            acc = recv2[k, step - 1].astype(jnp.float32) + res1[k, index]
            send2[k, step] = acc.astype(jnp.bfloat16)
            copies[k] = remote(send2.at[k, step], recv2.at[k, step],
                               ss2.at[k, step], sr2.at[k, step], {"dp": target})
            copies[k].start()
            pending.append(copies[k])
        yield
    for k, (pos, _, _) in enumerate(second):
        copies[k].wait_recv()
        res2[k] = recv2[k, RING - 2].astype(jnp.float32) + res1[k, pos]

    swap = remote(sendz, recvz, ssz, srz, {"dp": dp_at(y, x, 1 - z)})
    corners = [(0, 0), (half, 0), (0, width), (half, width)]

    @pl.when(z != chunk)
    def _():
        for k in range(4):
            sendz[k] = res2[k].astype(jnp.bfloat16)
        swap.start()

    yield

    @pl.when(z == chunk)
    def _():
        swap.wait_recv()
        for k, (r0, c0) in enumerate(corners):
            out_ref[pl.ds(r0, half), pl.ds(c0, width)] = res2[k] + recvz[k].astype(jnp.float32)

    @pl.when(z != chunk)
    def _():
        if kept_ref is None:
            for k, (r0, c0) in enumerate(corners):
                out_ref[pl.ds(r0, half), pl.ds(c0, width)] = res2[k]
        else:
            out_ref[...] = kept_ref[...]
        swap.wait_send()

    for copy in pending:
        copy.wait_send()


def gather_steps(local_ref, out_ref, send_sem, recv_sem):
    n = len(TENSOR_RING)
    me = lax.axis_index("tensor")
    pair = me // 2
    pos = pair * 2 + (me % 2 + pair) % 2
    right = ring_member((pos + 1) % n)
    left = ring_member((pos + n - 1) % n)
    rows, cols = local_ref.shape
    width = cols // 2
    out_ref[pl.ds(pl.multiple_of(me * rows, rows), rows), :] = local_ref[...]
    streams = [(right, 1, 0), (left, -1, width)]
    pending = []
    copies = [None, None]
    for step in range(n - 1):
        for d, (target, direction, c0) in enumerate(streams):
            if step == 0:
                src = local_ref.at[:, pl.ds(c0, width)]
            else:
                copies[d].wait_recv()
                owner = ring_member((pos - direction * step + 2 * n) % n)
                src = out_ref.at[pl.ds(pl.multiple_of(owner * rows, rows), rows), pl.ds(c0, width)]
            owner = ring_member((pos - direction * step + 2 * n) % n)
            copies[d] = remote(src, out_ref.at[pl.ds(pl.multiple_of(owner * rows, rows), rows), pl.ds(c0, width)],
                               send_sem.at[d, step], recv_sem.at[d, step], {"tensor": target})
            copies[d].start()
            pending.append(copies[d])
        yield
    for d in range(2):
        copies[d].wait_recv()
    for copy in pending:
        copy.wait_send()


def comm_kernel(chunk, do_reduce, do_gather, do_keep, *refs):
    refs = list(refs)
    terms_refs = [refs.pop(0), refs.pop(0)] if do_reduce else None
    kept_ref = refs.pop(0) if do_keep else None
    local_ref = refs.pop(0) if do_gather else None
    out_ref = refs.pop(0) if do_reduce else None
    gathered_ref = refs.pop(0) if do_gather else None
    reduce_scratch = refs[:14] if do_reduce else None
    gather_scratch = refs[-2:] if do_gather else None

    peers = []
    if do_reduce:
        dp = lax.axis_index("dp")
        y, x, z = dp // 8, (dp // 2) % 4, dp % 2
        for peer in (dp_at(y, (x + 1) % RING, z), dp_at(y, (x + RING - 1) % RING, z),
                     dp_at((y + 1) % RING, x, z), dp_at((y + RING - 1) % RING, x, z), dp_at(y, x, 1 - z)):
            peers.append({"dp": peer})
    if do_gather:
        n = len(TENSOR_RING)
        me = lax.axis_index("tensor")
        pair = me // 2
        pos = pair * 2 + (me % 2 + pair) % 2
        for peer in (ring_member((pos + 1) % n), ring_member((pos + n - 1) % n)):
            peers.append({"tensor": peer})
    barrier = pltpu.get_barrier_semaphore()
    for peer in peers:
        pl.semaphore_signal(barrier, inc=1, device_id=peer, device_id_type=MESH)
    pl.semaphore_wait(barrier, len(peers))

    runs = []
    if do_reduce:
        runs.append(reduce_steps(chunk, *terms_refs, kept_ref, out_ref, *reduce_scratch))
    if do_gather:
        runs.append(gather_steps(local_ref, gathered_ref, *gather_scratch))
    pattern = [0, 1, 1] if len(runs) == 2 else [0]
    while runs:
        for which in pattern:
            if which < len(runs):
                try:
                    next(runs[which])
                except StopIteration:
                    runs.pop(which)
                    pattern = [0]
                    break


def communicate(chunk, terms=None, local=None, collective_id=0, kept=None):
    do_reduce, do_gather = terms is not None, local is not None
    args, outs, scratch = [], [], []
    if do_reduce:
        rows, width = terms[0].shape[2], terms[0].shape[3]
        half = rows // 2
        args.extend(terms)
        if kept is not None:
            args.append(kept)
        outs.append(jax.ShapeDtypeStruct((rows, 2 * width), jnp.float32))
        scratch += [
            pltpu.VMEM((4, RING - 1, RING, half, width), jnp.bfloat16),
            pltpu.VMEM((4, RING - 2, RING, half, width), jnp.bfloat16),
            pltpu.VMEM((4, RING, half, width), jnp.float32),
            pltpu.VMEM((4, RING - 1, half, width), jnp.bfloat16),
            pltpu.VMEM((4, RING - 1, half, width), jnp.bfloat16),
            pltpu.VMEM((4, half, width), jnp.float32),
            pltpu.VMEM((4, half, width), jnp.bfloat16),
            pltpu.VMEM((4, half, width), jnp.bfloat16),
            pltpu.SemaphoreType.DMA((4, RING - 1)),
            pltpu.SemaphoreType.DMA((4, RING - 1)),
            pltpu.SemaphoreType.DMA((4, RING - 1)),
            pltpu.SemaphoreType.DMA((4, RING - 1)),
            pltpu.SemaphoreType.DMA(()),
            pltpu.SemaphoreType.DMA(()),
        ]
    if do_gather:
        n = len(TENSOR_RING)
        args.append(local)
        outs.append(jax.ShapeDtypeStruct((n * local.shape[0], local.shape[1]), local.dtype))
        scratch += [pltpu.SemaphoreType.DMA((2, n - 1)), pltpu.SemaphoreType.DMA((2, n - 1))]
    return pl.pallas_call(
        functools.partial(comm_kernel, chunk, do_reduce, do_gather, kept is not None),
        out_shape=tuple(outs),
        in_specs=[pl.BlockSpec(memory_space=pltpu.VMEM)] * len(args),
        out_specs=tuple(pl.BlockSpec(memory_space=pltpu.VMEM) for _ in outs),
        scratch_shapes=scratch,
        compiler_params=pltpu.CompilerParams(
            collective_id=collective_id, has_side_effects=True, vmem_limit_bytes=48 * 1024 * 1024),
    )(*args)


def code_kernel(grad_ref, dither_ref, first_ref, second_ref):
    blocks = grad_ref.shape[1] // BLOCK
    for block in range(blocks):
        cols = pl.ds(block * BLOCK, BLOCK)
        grad_float = grad_ref[:, cols].astype(jnp.float32)
        magnitude = jnp.max(jnp.abs(grad_float), axis=1, keepdims=True)
        y_scale = ((magnitude + epsilon) / Y_LEVELS).astype(jnp.bfloat16).astype(jnp.float32)
        code = (grad_float / y_scale + dither_ref[:, cols]).astype(jnp.bfloat16).astype(jnp.float32)
        target = first_ref if block % 2 == 0 else second_ref
        target[:, pl.ds((block // 2) * BLOCK, BLOCK)] = (code * y_scale).astype(jnp.bfloat16)


def coded_halves(grad_out, grad_dither):
    rows, feat_width = grad_out.shape
    half = jax.ShapeDtypeStruct((rows, feat_width // 2), jnp.bfloat16)
    return pl.pallas_call(
        code_kernel,
        out_shape=(half, half),
        in_specs=[pl.BlockSpec(memory_space=pltpu.VMEM)] * 2,
        out_specs=(pl.BlockSpec(memory_space=pltpu.VMEM), pl.BlockSpec(memory_space=pltpu.VMEM)),
    )(grad_out, grad_dither)


def per_device(grad_out, activations, grad_dither, hidden_dither, feature_dither):
    row_count, feat_width = grad_out.shape
    blocks = feat_width // BLOCK
    first_local, second_local = coded_halves(grad_out, grad_dither)
    feature_noise = feature_dither[0].reshape(blocks // 2, 2, BLOCK).transpose(1, 0, 2).reshape(feat_width)
    hidden_noise = hidden_dither[0]
    half = feat_width // 2

    def terms_of(y_hat, part):
        pieces = []
        width = activations.shape[1] // 2
        for cols in (slice(0, width), slice(width, 2 * width)):
            partial_value = lax.dot_general(
                y_hat, activations[:, cols], (((0,), (0,)), ((), ())), preferred_element_type=jnp.float32
            )
            pieces.append(group_terms(partial_value, feature_noise[part * half:(part + 1) * half], hidden_noise[cols]))
        return tuple(piece.reshape(RING, RING, BLOCK, piece.shape[1]) for piece in pieces)

    (first_y,) = communicate(0, None, first_local, collective_id=1)
    first_out, second_y = communicate(0, terms_of(first_y, 0), second_local, collective_id=2)
    (result,) = communicate(1, terms_of(second_y, 1), None, collective_id=0, kept=first_out)
    return result


def solution(mesh):
    placed = (
        P(("dp", "tensor"), None),
        P("dp", "tensor"),
        P(("dp", "tensor"), None),
        P("dp", "tensor"),
        P("dp", None),
    )
    return jax.shard_map(
        per_device, mesh=mesh, in_specs=placed, out_specs=P("dp", "tensor"), check_vma=False
    )
```

```python
import functools

import jax
import jax.numpy as jnp
from jax import lax
from jax.experimental import pallas as pl
from jax.experimental.pallas import tpu as pltpu
from jax.sharding import PartitionSpec as P

BLOCK = 128
Y_LEVELS = 8
W_LEVELS = 7


epsilon = 1e-06


def as_bf16_value(value):
    return lax.reduce_precision(value, exponent_bits=8, mantissa_bits=7)


def group_terms(partial_value, feature_part, hidden_part):
    feat_rows, unit_cols = partial_value.shape
    block_count = feat_rows // BLOCK
    blocks = partial_value.reshape(block_count, BLOCK, unit_cols)
    magnitude = jnp.max(jnp.abs(blocks), axis=1)
    block_scale = ((magnitude + epsilon) / W_LEVELS).astype(jnp.bfloat16)
    scaled = (blocks / block_scale.astype(jnp.float32)[:, None, :]).reshape(feat_rows, unit_cols)
    held = as_bf16_value(scaled + hidden_part[None, :] + feature_part[:, None])
    values = held.reshape(block_count, BLOCK, unit_cols) * block_scale.astype(jnp.float32)[:, None, :]
    return values.reshape(feat_rows, unit_cols).astype(jnp.bfloat16)


MESH = pl.DeviceIdType.MESH
RING = 4
TENSOR_RING = (0, 1, 3, 2, 4, 5, 7, 6)


def dp_at(y, x, z):
    return y * 8 + x * 2 + z


def ring_member(position):
    pair, within = position // 2, position % 2
    return pair * 2 + (within + pair) % 2


def sent_index(pos, direction, step):
    return (pos - direction * (step + 1) + 2 * RING) % RING


def remote(src, dst, send_sem, recv_sem, peer):
    return pltpu.make_async_remote_copy(
        src_ref=src, dst_ref=dst, send_sem=send_sem, recv_sem=recv_sem,
        device_id=peer, device_id_type=MESH)


def reduce_steps(chunk, first_ref, second_ref, kept_ref, out_ref, recv1, send1, res1, recv2, send2, res2, recvz, sendz,
                 ss1, sr1, ss2, sr2, ssz, srz):
    dp = lax.axis_index("dp")
    y, x, z = dp // 8, (dp // 2) % 4, dp % 2
    rows, width = first_ref.shape[2], first_ref.shape[3]
    half = rows // 2
    x_up, x_dn = dp_at(y, (x + 1) % RING, z), dp_at(y, (x + RING - 1) % RING, z)
    y_up, y_dn = dp_at((y + 1) % RING, x, z), dp_at((y + RING - 1) % RING, x, z)
    first = [
        (x, 1, x_up, 0, 0, True),
        (x, -1, x_dn, half, 0, True),
        (y, 1, y_up, 0, width, False),
        (y, -1, y_dn, half, width, False),
    ]

    def local1(k, index):
        _, _, _, r0, _, over_x = first[k]
        if over_x:
            return first_ref.at[:, index, pl.ds(r0, half), :]
        return second_ref.at[index, :, pl.ds(r0, half), :]

    pending = []
    copies = [None] * 4
    for k, (pos, direction, target, _, _, _) in enumerate(first):
        copies[k] = remote(local1(k, sent_index(pos, direction, 0)), recv1.at[k, 0],
                           ss1.at[k, 0], sr1.at[k, 0], {"dp": target})
        copies[k].start()
        pending.append(copies[k])
    yield
    for step in range(1, RING - 1):
        for k, (pos, direction, target, _, _, _) in enumerate(first):
            copies[k].wait_recv()
            index = sent_index(pos, direction, step)
            acc = recv1[k, step - 1].astype(jnp.float32) + local1(k, index)[...].astype(jnp.float32)
            send1[k, step - 1] = acc.astype(jnp.bfloat16)
            copies[k] = remote(send1.at[k, step - 1], recv1.at[k, step],
                               ss1.at[k, step], sr1.at[k, step], {"dp": target})
            copies[k].start()
            pending.append(copies[k])
        yield
    for k, (pos, _, _, _, _, _) in enumerate(first):
        copies[k].wait_recv()
        res1[k] = recv1[k, RING - 2].astype(jnp.float32) + local1(k, pos)[...].astype(jnp.float32)

    second = [(y, 1, y_up), (y, -1, y_dn), (x, 1, x_up), (x, -1, x_dn)]
    for k, (pos, direction, target) in enumerate(second):
        send2[k, 0] = res1[k, sent_index(pos, direction, 0)].astype(jnp.bfloat16)
        copies[k] = remote(send2.at[k, 0], recv2.at[k, 0], ss2.at[k, 0], sr2.at[k, 0], {"dp": target})
        copies[k].start()
        pending.append(copies[k])
    yield
    for step in range(1, RING - 1):
        for k, (pos, direction, target) in enumerate(second):
            copies[k].wait_recv()
            index = sent_index(pos, direction, step)
            acc = recv2[k, step - 1].astype(jnp.float32) + res1[k, index]
            send2[k, step] = acc.astype(jnp.bfloat16)
            copies[k] = remote(send2.at[k, step], recv2.at[k, step],
                               ss2.at[k, step], sr2.at[k, step], {"dp": target})
            copies[k].start()
            pending.append(copies[k])
        yield
    for k, (pos, _, _) in enumerate(second):
        copies[k].wait_recv()
        res2[k] = recv2[k, RING - 2].astype(jnp.float32) + res1[k, pos]

    swap = remote(sendz, recvz, ssz, srz, {"dp": dp_at(y, x, 1 - z)})
    corners = [(0, 0), (half, 0), (0, width), (half, width)]

    @pl.when(z != chunk)
    def _():
        for k in range(4):
            sendz[k] = res2[k].astype(jnp.bfloat16)
        swap.start()

    yield

    @pl.when(z == chunk)
    def _():
        swap.wait_recv()
        for k, (r0, c0) in enumerate(corners):
            out_ref[pl.ds(r0, half), pl.ds(c0, width)] = res2[k] + recvz[k].astype(jnp.float32)

    @pl.when(z != chunk)
    def _():
        if kept_ref is None:
            for k, (r0, c0) in enumerate(corners):
                out_ref[pl.ds(r0, half), pl.ds(c0, width)] = res2[k]
        else:
            out_ref[...] = kept_ref[...]
        swap.wait_send()

    for copy in pending:
        copy.wait_send()


def gather_steps(local_ref, out_ref, send_sem, recv_sem):
    n = len(TENSOR_RING)
    me = lax.axis_index("tensor")
    pair = me // 2
    pos = pair * 2 + (me % 2 + pair) % 2
    right = ring_member((pos + 1) % n)
    left = ring_member((pos + n - 1) % n)
    rows, cols = local_ref.shape
    width = cols // 2
    out_ref[pl.ds(pl.multiple_of(me * rows, rows), rows), :] = local_ref[...]
    streams = [(right, 1, 0), (left, -1, width)]
    pending = []
    copies = [None, None]
    for step in range(n - 1):
        for d, (target, direction, c0) in enumerate(streams):
            if step == 0:
                src = local_ref.at[:, pl.ds(c0, width)]
            else:
                copies[d].wait_recv()
                owner = ring_member((pos - direction * step + 2 * n) % n)
                src = out_ref.at[pl.ds(pl.multiple_of(owner * rows, rows), rows), pl.ds(c0, width)]
            owner = ring_member((pos - direction * step + 2 * n) % n)
            copies[d] = remote(src, out_ref.at[pl.ds(pl.multiple_of(owner * rows, rows), rows), pl.ds(c0, width)],
                               send_sem.at[d, step], recv_sem.at[d, step], {"tensor": target})
            copies[d].start()
            pending.append(copies[d])
        yield
    for d in range(2):
        copies[d].wait_recv()
    for copy in pending:
        copy.wait_send()


def comm_kernel(chunk, do_reduce, do_gather, do_keep, *refs):
    refs = list(refs)
    terms_refs = [refs.pop(0), refs.pop(0)] if do_reduce else None
    kept_ref = refs.pop(0) if do_keep else None
    local_ref = refs.pop(0) if do_gather else None
    out_ref = refs.pop(0) if do_reduce else None
    gathered_ref = refs.pop(0) if do_gather else None
    reduce_scratch = refs[:14] if do_reduce else None
    gather_scratch = refs[-2:] if do_gather else None

    peers = []
    if do_reduce:
        dp = lax.axis_index("dp")
        y, x, z = dp // 8, (dp // 2) % 4, dp % 2
        for peer in (dp_at(y, (x + 1) % RING, z), dp_at(y, (x + RING - 1) % RING, z),
                     dp_at((y + 1) % RING, x, z), dp_at((y + RING - 1) % RING, x, z), dp_at(y, x, 1 - z)):
            peers.append({"dp": peer})
    if do_gather:
        n = len(TENSOR_RING)
        me = lax.axis_index("tensor")
        pair = me // 2
        pos = pair * 2 + (me % 2 + pair) % 2
        for peer in (ring_member((pos + 1) % n), ring_member((pos + n - 1) % n)):
            peers.append({"tensor": peer})
    barrier = pltpu.get_barrier_semaphore()
    for peer in peers:
        pl.semaphore_signal(barrier, inc=1, device_id=peer, device_id_type=MESH)
    pl.semaphore_wait(barrier, len(peers))

    runs = []
    if do_reduce:
        runs.append(reduce_steps(chunk, *terms_refs, kept_ref, out_ref, *reduce_scratch))
    if do_gather:
        runs.append(gather_steps(local_ref, gathered_ref, *gather_scratch))
    pattern = [0, 1] if len(runs) == 2 else [0]
    while runs:
        for which in pattern:
            if which < len(runs):
                try:
                    next(runs[which])
                except StopIteration:
                    runs.pop(which)
                    pattern = [0]
                    break


def communicate(chunk, terms=None, local=None, collective_id=0, kept=None):
    do_reduce, do_gather = terms is not None, local is not None
    args, outs, scratch = [], [], []
    if do_reduce:
        rows, width = terms[0].shape[2], terms[0].shape[3]
        half = rows // 2
        args.extend(terms)
        if kept is not None:
            args.append(kept)
        outs.append(jax.ShapeDtypeStruct((rows, 2 * width), jnp.float32))
        scratch += [
            pltpu.VMEM((4, RING - 1, RING, half, width), jnp.bfloat16),
            pltpu.VMEM((4, RING - 2, RING, half, width), jnp.bfloat16),
            pltpu.VMEM((4, RING, half, width), jnp.float32),
            pltpu.VMEM((4, RING - 1, half, width), jnp.bfloat16),
            pltpu.VMEM((4, RING - 1, half, width), jnp.bfloat16),
            pltpu.VMEM((4, half, width), jnp.float32),
            pltpu.VMEM((4, half, width), jnp.bfloat16),
            pltpu.VMEM((4, half, width), jnp.bfloat16),
            pltpu.SemaphoreType.DMA((4, RING - 1)),
            pltpu.SemaphoreType.DMA((4, RING - 1)),
            pltpu.SemaphoreType.DMA((4, RING - 1)),
            pltpu.SemaphoreType.DMA((4, RING - 1)),
            pltpu.SemaphoreType.DMA(()),
            pltpu.SemaphoreType.DMA(()),
        ]
    if do_gather:
        n = len(TENSOR_RING)
        args.append(local)
        outs.append(jax.ShapeDtypeStruct((n * local.shape[0], local.shape[1]), local.dtype))
        scratch += [pltpu.SemaphoreType.DMA((2, n - 1)), pltpu.SemaphoreType.DMA((2, n - 1))]
    return pl.pallas_call(
        functools.partial(comm_kernel, chunk, do_reduce, do_gather, kept is not None),
        out_shape=tuple(outs),
        in_specs=[pl.BlockSpec(memory_space=pltpu.VMEM)] * len(args),
        out_specs=tuple(pl.BlockSpec(memory_space=pltpu.VMEM) for _ in outs),
        scratch_shapes=scratch,
        compiler_params=pltpu.CompilerParams(
            collective_id=collective_id, has_side_effects=True, vmem_limit_bytes=48 * 1024 * 1024),
    )(*args)


def code_kernel(grad_ref, dither_ref, first_ref, second_ref):
    blocks = grad_ref.shape[1] // BLOCK
    for block in range(blocks):
        cols = pl.ds(block * BLOCK, BLOCK)
        grad_float = grad_ref[:, cols].astype(jnp.float32)
        magnitude = jnp.max(jnp.abs(grad_float), axis=1, keepdims=True)
        y_scale = ((magnitude + epsilon) / Y_LEVELS).astype(jnp.bfloat16).astype(jnp.float32)
        code = (grad_float / y_scale + dither_ref[:, cols]).astype(jnp.bfloat16).astype(jnp.float32)
        target = first_ref if block % 2 == 0 else second_ref
        target[:, pl.ds((block // 2) * BLOCK, BLOCK)] = (code * y_scale).astype(jnp.bfloat16)


def coded_halves(grad_out, grad_dither):
    rows, feat_width = grad_out.shape
    half = jax.ShapeDtypeStruct((rows, feat_width // 2), jnp.bfloat16)
    return pl.pallas_call(
        code_kernel,
        out_shape=(half, half),
        in_specs=[pl.BlockSpec(memory_space=pltpu.VMEM)] * 2,
        out_specs=(pl.BlockSpec(memory_space=pltpu.VMEM), pl.BlockSpec(memory_space=pltpu.VMEM)),
    )(grad_out, grad_dither)


def per_device(grad_out, activations, grad_dither, hidden_dither, feature_dither):
    row_count, feat_width = grad_out.shape
    blocks = feat_width // BLOCK
    first_local, second_local = coded_halves(grad_out, grad_dither)
    feature_noise = feature_dither[0].reshape(blocks // 2, 2, BLOCK).transpose(1, 0, 2).reshape(feat_width)
    hidden_noise = hidden_dither[0]
    half = feat_width // 2

    def terms_of(y_hat, part):
        pieces = []
        width = activations.shape[1] // 2
        for cols in (slice(0, width), slice(width, 2 * width)):
            partial_value = lax.dot_general(
                y_hat, activations[:, cols], (((0,), (0,)), ((), ())), preferred_element_type=jnp.float32
            )
            pieces.append(group_terms(partial_value, feature_noise[part * half:(part + 1) * half], hidden_noise[cols]))
        return tuple(piece.reshape(RING, RING, BLOCK, piece.shape[1]) for piece in pieces)

    (first_y,) = communicate(0, None, first_local, collective_id=1)
    first_out, second_y = communicate(0, terms_of(first_y, 0), second_local, collective_id=2)
    (result,) = communicate(1, terms_of(second_y, 1), None, collective_id=0, kept=first_out)
    return result


def solution(mesh):
    placed = (
        P(("dp", "tensor"), None),
        P("dp", "tensor"),
        P(("dp", "tensor"), None),
        P("dp", "tensor"),
        P("dp", None),
    )
    return jax.shard_map(
        per_device, mesh=mesh, in_specs=placed, out_specs=P("dp", "tensor"), check_vma=False
    )
```

```python
import functools

import jax
import jax.numpy as jnp
from jax import lax
from jax.experimental import pallas as pl
from jax.experimental.pallas import tpu as pltpu
from jax.sharding import PartitionSpec as P

BLOCK = 128
Y_LEVELS = 8
W_LEVELS = 7


epsilon = 1e-06


def as_bf16_value(value):
    return lax.reduce_precision(value, exponent_bits=8, mantissa_bits=7)


def group_terms(partial_value, feature_part, hidden_part):
    feat_rows, unit_cols = partial_value.shape
    block_count = feat_rows // BLOCK
    blocks = partial_value.reshape(block_count, BLOCK, unit_cols)
    magnitude = jnp.max(jnp.abs(blocks), axis=1)
    block_scale = ((magnitude + epsilon) / W_LEVELS).astype(jnp.bfloat16)
    scaled = (blocks / block_scale.astype(jnp.float32)[:, None, :]).reshape(feat_rows, unit_cols)
    held = as_bf16_value(scaled + hidden_part[None, :] + feature_part[:, None])
    values = held.reshape(block_count, BLOCK, unit_cols) * block_scale.astype(jnp.float32)[:, None, :]
    return values.reshape(feat_rows, unit_cols).astype(jnp.bfloat16)


MESH = pl.DeviceIdType.MESH
RING = 4
TENSOR_RING = (0, 1, 3, 2, 4, 5, 7, 6)


def dp_at(y, x, z):
    return y * 8 + x * 2 + z


def ring_member(position):
    pair, within = position // 2, position % 2
    return pair * 2 + (within + pair) % 2


def sent_index(pos, direction, step):
    return (pos - direction * (step + 1) + 2 * RING) % RING


def remote(src, dst, send_sem, recv_sem, peer):
    return pltpu.make_async_remote_copy(
        src_ref=src, dst_ref=dst, send_sem=send_sem, recv_sem=recv_sem,
        device_id=peer, device_id_type=MESH)


def reduce_steps(chunk, first_ref, second_ref, out_ref, recv1, send1, res1, recv2, send2, res2, recvz, sendz,
                 ss1, sr1, ss2, sr2, ssz, srz):
    dp = lax.axis_index("dp")
    y, x, z = dp // 8, (dp // 2) % 4, dp % 2
    rows, width = first_ref.shape[2], first_ref.shape[3]
    half = rows // 2
    x_up, x_dn = dp_at(y, (x + 1) % RING, z), dp_at(y, (x + RING - 1) % RING, z)
    y_up, y_dn = dp_at((y + 1) % RING, x, z), dp_at((y + RING - 1) % RING, x, z)
    first = [
        (x, 1, x_up, 0, 0, True),
        (x, -1, x_dn, half, 0, True),
        (y, 1, y_up, 0, width, False),
        (y, -1, y_dn, half, width, False),
    ]

    def local1(k, index):
        _, _, _, r0, _, over_x = first[k]
        if over_x:
            return first_ref.at[:, index, pl.ds(r0, half), :]
        return second_ref.at[index, :, pl.ds(r0, half), :]

    pending = []
    copies = [None] * 4
    for k, (pos, direction, target, _, _, _) in enumerate(first):
        copies[k] = remote(local1(k, sent_index(pos, direction, 0)), recv1.at[k, 0],
                           ss1.at[k, 0], sr1.at[k, 0], {"dp": target})
        copies[k].start()
        pending.append(copies[k])
    yield
    for step in range(1, RING - 1):
        for k, (pos, direction, target, _, _, _) in enumerate(first):
            copies[k].wait_recv()
            index = sent_index(pos, direction, step)
            acc = recv1[k, step - 1].astype(jnp.float32) + local1(k, index)[...].astype(jnp.float32)
            send1[k, step - 1] = acc.astype(jnp.bfloat16)
            copies[k] = remote(send1.at[k, step - 1], recv1.at[k, step],
                               ss1.at[k, step], sr1.at[k, step], {"dp": target})
            copies[k].start()
            pending.append(copies[k])
        yield
    for k, (pos, _, _, _, _, _) in enumerate(first):
        copies[k].wait_recv()
        res1[k] = recv1[k, RING - 2].astype(jnp.float32) + local1(k, pos)[...].astype(jnp.float32)

    second = [(y, 1, y_up), (y, -1, y_dn), (x, 1, x_up), (x, -1, x_dn)]
    for k, (pos, direction, target) in enumerate(second):
        send2[k, 0] = res1[k, sent_index(pos, direction, 0)].astype(jnp.bfloat16)
        copies[k] = remote(send2.at[k, 0], recv2.at[k, 0], ss2.at[k, 0], sr2.at[k, 0], {"dp": target})
        copies[k].start()
        pending.append(copies[k])
    yield
    for step in range(1, RING - 1):
        for k, (pos, direction, target) in enumerate(second):
            copies[k].wait_recv()
            index = sent_index(pos, direction, step)
            acc = recv2[k, step - 1].astype(jnp.float32) + res1[k, index]
            send2[k, step] = acc.astype(jnp.bfloat16)
            copies[k] = remote(send2.at[k, step], recv2.at[k, step],
                               ss2.at[k, step], sr2.at[k, step], {"dp": target})
            copies[k].start()
            pending.append(copies[k])
        yield
    for k, (pos, _, _) in enumerate(second):
        copies[k].wait_recv()
        res2[k] = recv2[k, RING - 2].astype(jnp.float32) + res1[k, pos]

    swap = remote(sendz, recvz, ssz, srz, {"dp": dp_at(y, x, 1 - z)})
    corners = [(0, 0), (half, 0), (0, width), (half, width)]

    @pl.when(z != chunk)
    def _():
        for k in range(4):
            sendz[k] = res2[k].astype(jnp.bfloat16)
        swap.start()

    yield

    @pl.when(z == chunk)
    def _():
        swap.wait_recv()
        for k, (r0, c0) in enumerate(corners):
            out_ref[pl.ds(r0, half), pl.ds(c0, width)] = res2[k] + recvz[k].astype(jnp.float32)

    @pl.when(z != chunk)
    def _():
        for k, (r0, c0) in enumerate(corners):
            out_ref[pl.ds(r0, half), pl.ds(c0, width)] = res2[k]
        swap.wait_send()

    for copy in pending:
        copy.wait_send()


def gather_steps(local_ref, out_ref, send_sem, recv_sem):
    n = len(TENSOR_RING)
    me = lax.axis_index("tensor")
    pair = me // 2
    pos = pair * 2 + (me % 2 + pair) % 2
    right = ring_member((pos + 1) % n)
    left = ring_member((pos + n - 1) % n)
    rows, cols = local_ref.shape
    width = cols // 2
    out_ref[pl.ds(pl.multiple_of(me * rows, rows), rows), :] = local_ref[...]
    streams = [(right, 1, 0), (left, -1, width)]
    pending = []
    copies = [None, None]
    for step in range(n - 1):
        for d, (target, direction, c0) in enumerate(streams):
            if step == 0:
                src = local_ref.at[:, pl.ds(c0, width)]
            else:
                copies[d].wait_recv()
                owner = ring_member((pos - direction * step + 2 * n) % n)
                src = out_ref.at[pl.ds(pl.multiple_of(owner * rows, rows), rows), pl.ds(c0, width)]
            owner = ring_member((pos - direction * step + 2 * n) % n)
            copies[d] = remote(src, out_ref.at[pl.ds(pl.multiple_of(owner * rows, rows), rows), pl.ds(c0, width)],
                               send_sem.at[d, step], recv_sem.at[d, step], {"tensor": target})
            copies[d].start()
            pending.append(copies[d])
        yield
    for d in range(2):
        copies[d].wait_recv()
    for copy in pending:
        copy.wait_send()


def comm_kernel(chunk, do_reduce, do_gather, *refs):
    refs = list(refs)
    terms_refs = [refs.pop(0), refs.pop(0)] if do_reduce else None
    local_ref = refs.pop(0) if do_gather else None
    out_ref = refs.pop(0) if do_reduce else None
    gathered_ref = refs.pop(0) if do_gather else None
    reduce_scratch = refs[:14] if do_reduce else None
    gather_scratch = refs[-2:] if do_gather else None

    peers = []
    if do_reduce:
        dp = lax.axis_index("dp")
        y, x, z = dp // 8, (dp // 2) % 4, dp % 2
        for peer in (dp_at(y, (x + 1) % RING, z), dp_at(y, (x + RING - 1) % RING, z),
                     dp_at((y + 1) % RING, x, z), dp_at((y + RING - 1) % RING, x, z), dp_at(y, x, 1 - z)):
            peers.append({"dp": peer})
    if do_gather:
        n = len(TENSOR_RING)
        me = lax.axis_index("tensor")
        pair = me // 2
        pos = pair * 2 + (me % 2 + pair) % 2
        for peer in (ring_member((pos + 1) % n), ring_member((pos + n - 1) % n)):
            peers.append({"tensor": peer})
    barrier = pltpu.get_barrier_semaphore()
    for peer in peers:
        pl.semaphore_signal(barrier, inc=1, device_id=peer, device_id_type=MESH)
    pl.semaphore_wait(barrier, len(peers))

    runs = []
    if do_reduce:
        runs.append(reduce_steps(chunk, *terms_refs, out_ref, *reduce_scratch))
    if do_gather:
        runs.append(gather_steps(local_ref, gathered_ref, *gather_scratch))
    pattern = [0, 1, 1, 1] if len(runs) == 2 else [0]
    while runs:
        for which in pattern:
            if which < len(runs):
                try:
                    next(runs[which])
                except StopIteration:
                    runs.pop(which)
                    pattern = [0]
                    break


def communicate(chunk, terms=None, local=None, collective_id=0):
    do_reduce, do_gather = terms is not None, local is not None
    args, outs, scratch = [], [], []
    if do_reduce:
        rows, width = terms[0].shape[2], terms[0].shape[3]
        half = rows // 2
        args.extend(terms)
        outs.append(jax.ShapeDtypeStruct((rows, 2 * width), jnp.float32))
        scratch += [
            pltpu.VMEM((4, RING - 1, RING, half, width), jnp.bfloat16),
            pltpu.VMEM((4, RING - 2, RING, half, width), jnp.bfloat16),
            pltpu.VMEM((4, RING, half, width), jnp.float32),
            pltpu.VMEM((4, RING - 1, half, width), jnp.bfloat16),
            pltpu.VMEM((4, RING - 1, half, width), jnp.bfloat16),
            pltpu.VMEM((4, half, width), jnp.float32),
            pltpu.VMEM((4, half, width), jnp.bfloat16),
            pltpu.VMEM((4, half, width), jnp.bfloat16),
            pltpu.SemaphoreType.DMA((4, RING - 1)),
            pltpu.SemaphoreType.DMA((4, RING - 1)),
            pltpu.SemaphoreType.DMA((4, RING - 1)),
            pltpu.SemaphoreType.DMA((4, RING - 1)),
            pltpu.SemaphoreType.DMA(()),
            pltpu.SemaphoreType.DMA(()),
        ]
    if do_gather:
        n = len(TENSOR_RING)
        args.append(local)
        outs.append(jax.ShapeDtypeStruct((n * local.shape[0], local.shape[1]), local.dtype))
        scratch += [pltpu.SemaphoreType.DMA((2, n - 1)), pltpu.SemaphoreType.DMA((2, n - 1))]
    return pl.pallas_call(
        functools.partial(comm_kernel, chunk, do_reduce, do_gather),
        out_shape=tuple(outs),
        in_specs=[pl.BlockSpec(memory_space=pltpu.VMEM)] * len(args),
        out_specs=tuple(pl.BlockSpec(memory_space=pltpu.VMEM) for _ in outs),
        scratch_shapes=scratch,
        compiler_params=pltpu.CompilerParams(
            collective_id=collective_id, has_side_effects=True, vmem_limit_bytes=48 * 1024 * 1024),
    )(*args)


def code_kernel(grad_ref, dither_ref, first_ref, second_ref):
    blocks = grad_ref.shape[1] // BLOCK
    for block in range(blocks):
        cols = pl.ds(block * BLOCK, BLOCK)
        grad_float = grad_ref[:, cols].astype(jnp.float32)
        magnitude = jnp.max(jnp.abs(grad_float), axis=1, keepdims=True)
        y_scale = ((magnitude + epsilon) / Y_LEVELS).astype(jnp.bfloat16).astype(jnp.float32)
        code = (grad_float / y_scale + dither_ref[:, cols]).astype(jnp.bfloat16).astype(jnp.float32)
        target = first_ref if block % 2 == 0 else second_ref
        target[:, pl.ds((block // 2) * BLOCK, BLOCK)] = (code * y_scale).astype(jnp.bfloat16)


def coded_halves(grad_out, grad_dither):
    rows, feat_width = grad_out.shape
    half = jax.ShapeDtypeStruct((rows, feat_width // 2), jnp.bfloat16)
    return pl.pallas_call(
        code_kernel,
        out_shape=(half, half),
        in_specs=[pl.BlockSpec(memory_space=pltpu.VMEM)] * 2,
        out_specs=(pl.BlockSpec(memory_space=pltpu.VMEM), pl.BlockSpec(memory_space=pltpu.VMEM)),
    )(grad_out, grad_dither)


def per_device(grad_out, activations, grad_dither, hidden_dither, feature_dither):
    row_count, feat_width = grad_out.shape
    blocks = feat_width // BLOCK
    first_local, second_local = coded_halves(grad_out, grad_dither)
    feature_noise = feature_dither[0].reshape(blocks // 2, 2, BLOCK).transpose(1, 0, 2).reshape(feat_width)
    hidden_noise = hidden_dither[0]
    half = feat_width // 2

    def terms_of(y_hat, part):
        pieces = []
        width = activations.shape[1] // 2
        for cols in (slice(0, width), slice(width, 2 * width)):
            partial_value = lax.dot_general(
                y_hat, activations[:, cols], (((0,), (0,)), ((), ())), preferred_element_type=jnp.float32
            )
            pieces.append(group_terms(partial_value, feature_noise[part * half:(part + 1) * half], hidden_noise[cols]))
        return tuple(piece.reshape(RING, RING, BLOCK, piece.shape[1]) for piece in pieces)

    (first_y,) = communicate(0, None, first_local, collective_id=1)
    first_out, second_y = communicate(0, terms_of(first_y, 0), second_local, collective_id=2)
    (second_out,) = communicate(1, terms_of(second_y, 1), None, collective_id=0)
    z = lax.axis_index("dp") % 2
    return jnp.where(z == 0, first_out, second_out)


def solution(mesh):
    placed = (
        P(("dp", "tensor"), None),
        P("dp", "tensor"),
        P(("dp", "tensor"), None),
        P("dp", "tensor"),
        P("dp", None),
    )
    return jax.shard_map(
        per_device, mesh=mesh, in_specs=placed, out_specs=P("dp", "tensor"), check_vma=False
    )
```
